128 devices in a mesh: dp: 32 (over z, x, core), seq: 4 (over y).
Axes of the slice: x: 4, y: 4, z: 4, core: 2. Of those that a mesh axis runs over, the one named last changes fastest.
Arguments:
- queries: bfloat16 [32768, 2560], P(('dp', 'seq')), may hold values from -200 to 200
- keys: bfloat16 [32768, 2560], P(('dp', 'seq')), may hold values from -200 to 200
- values: bfloat16 [32768, 2560], P(('dp', 'seq')), may hold values from -6 to 6
- gain_q: float32 [2560], replicated, may hold values from 0.5 to 1.5
- gain_k: float32 [2560], replicated, may hold values from 0.5 to 1.5
- tile_pairs: int32 [16, 8], replicated, may hold values from 0 to 15, as said below
- tile_lens: int32 [32, 16], P('dp'), may hold values from 40 to 64
- out_grad: bfloat16 [32768, 5120], P(('dp', 'seq')), may hold values from -24 to 24
- w_out: bfloat16 [5120, 2560], P('dp', 'seq'), may hold values from -0.125 to 0.125
Outputs:
- grad_q: bfloat16 [32768, 2560], P(('dp', 'seq'))
- grad_k: bfloat16 [32768, 2560], P(('dp', 'seq'))
- grad_v: bfloat16 [32768, 2560], P(('dp', 'seq'))
- grad_w: float32 [5120, 2560], P('dp', 'seq')
The draws below stay inside these ranges and needn't reach their ends.
Inputs may be any that keep to these rules, and one draw needn't show every extreme that they name: `tile_pairs`: row a lists 8 different tiles of the window, with tile a first.
All inputs are finite; a program needn't handle non-finite values.
Results may differ from the reference program's by a relative error of at most 0.02.
Values may be sent and summed in bfloat16 or wider, within the bound.
No kernel may reach another device: no remote copies, remote signals or barrier semaphores. Data moves between devices by JAX's collectives and lax.ppermute only.
A program may use at most 128 MiB of HBM per device.

```python
import math
import jax
import jax.numpy as jnp
from jax import lax

D = 5120
HEAD_DIM = 128
HEADS = 20
TILE = 64
TILES = 16
NEIGH = 8
CLIP_TOK = 1024
HD = 2560
TOKENS = 32768
N_DP = 32


def field_pair(key):
    queries = jnp.clip(jax.random.normal(jax.random.fold_in(key, 101), (TOKENS, HD), jnp.float32), -6.0, 6.0)
    keys = jnp.clip(jax.random.normal(jax.random.fold_in(key, 202), (TOKENS, HD), jnp.float32), -6.0, 6.0)
    return (queries, keys)


def draw_queries(key, part):
    return field_pair(key)[0].astype(jnp.bfloat16)


def draw_keys(key, part):
    return field_pair(key)[1].astype(jnp.bfloat16)


def draw_tile_pairs(key, part):
    row_keys = jax.random.split(jax.random.fold_in(key, 909), TILES)

    def one_row(row_key, index):
        others = jax.random.permutation(row_key, TILES - 1)[:NEIGH - 1].astype(jnp.int32)
        others = jnp.where(others >= index, others + 1, others)
        return jnp.concatenate([index[None], others]).astype(jnp.int32)
    return jax.vmap(one_row)(row_keys, jnp.arange(TILES, dtype=jnp.int32))


def touch_ends(drawn, stream_key, smallest, largest):
    shape = drawn.shape
    place = [jax.random.randint(jax.random.fold_in(stream_key, axis), (), 0, shape[axis]) for axis in range(len(shape))]
    drawn = drawn.at[tuple(place)].set(smallest)
    longest = shape.index(max(shape))
    place[longest] = (place[longest] + 1) % shape[longest]
    return drawn.at[tuple(place)].set(largest)


def strengthened(entries, key, source, target, shards_of, factor):
    def block_of(dim):
        return (jnp.arange(entries.shape[dim]) // (entries.shape[dim] // shards_of)).reshape((-1,) + (1,) * (entries.ndim - 1 - dim))

    first = jax.random.permutation(key, shards_of)[block_of(target)]
    other_side = (block_of(target) + shards_of // 2) % shards_of
    return jnp.where((block_of(source) == first) | (block_of(source) == other_side), factor * entries, entries)


def block_scale(stream_key, shape, shards, least, high):
    def one(position, shards_of):
        steps = jax.random.uniform(jax.random.fold_in(jax.random.fold_in(stream_key, 6), position), (shards_of,), jnp.float32, least / len(shards), high / len(shards))
        return jnp.repeat(jnp.exp(steps), shape[position] // shards_of).reshape((-1,) + (1,) * (len(shape) - position - 1))

    level = one(*shards[0])
    for cut in shards[1:]:
        level = level * one(*cut)
    return level


def gaussian(key, extent, scale, most, cuts=(), held_as=jnp.bfloat16):
    factor_of = block_scale(key, extent, cuts, -0.22, 0.18) if cuts else 1.0
    result = jax.random.normal(key, extent, jnp.float32) * scale * factor_of
    return jnp.minimum(jnp.maximum(result, -most), most).astype(held_as)


def gaussian_with(rng, shape, deviation, most, shards, heavy, kind=jnp.bfloat16):
    entries = deviation * jax.random.normal(rng, shape, jnp.float32)
    if shards:
        entries = entries * block_scale(rng, shape, shards, -0.22, 0.18)
    return jnp.clip(strengthened(entries, jax.random.fold_in(rng, 3), *heavy), -most, most).astype(kind)


def setup_inputs(seed: int = 0) -> dict:
    streams_of = jax.random.split(jax.random.key(seed), 10)
    queries = draw_queries(jax.random.fold_in(streams_of[9], 71), 0)
    keys = draw_keys(jax.random.fold_in(streams_of[9], 71), 0)
    values = gaussian(streams_of[2], (TOKENS, HD), 1.0, 6.0, ((0, 128),))
    gain_q = jnp.clip(1.0 + 0.1 * jax.random.normal(streams_of[3], (HD,), jnp.float32), 0.5, 1.5)
    gain_k = jnp.clip(1.0 + 0.1 * jax.random.normal(streams_of[4], (HD,), jnp.float32), 0.5, 1.5)
    tile_pairs = draw_tile_pairs(jax.random.fold_in(streams_of[9], 71), 0)
    tile_lens = touch_ends(jax.random.randint(streams_of[6], (N_DP, TILES), TILE * 5 // 8, TILE + 1), jax.random.fold_in(streams_of[6], 1), TILE * 5 // 8, TILE).astype(jnp.int32)
    out_grad = gaussian_with(streams_of[7], (TOKENS, D), 1.0, 24.0, ((0, 128),), (0, 1, 128, 5.5))
    w_out = gaussian(streams_of[8], (D, HD), HD ** -0.5, 0.125, ((0, 32), (1, 4)))
    return dict(queries=queries, keys=keys, values=values, gain_q=gain_q, gain_k=gain_k, tile_pairs=tile_pairs, tile_lens=tile_lens, out_grad=out_grad, w_out=w_out)


EPS = 1e-06

def multiply(pattern, left, right):
    return jnp.einsum(pattern, left.astype(jnp.float32), right.astype(jnp.float32), precision=lax.Precision.HIGHEST)

def normalize(field, gain):
    values_f = field.astype(jnp.float32)
    row_scale = lax.rsqrt(lax.optimization_barrier(jnp.mean(values_f * values_f, axis=-1, keepdims=True)) + EPS)
    return ((values_f * row_scale * gain.astype(jnp.float32)).astype(jnp.bfloat16), row_scale)

def norm_back(field, row_scale, gain, grad_normed):
    values_f = field.astype(jnp.float32)
    gated = gain.astype(jnp.float32) * grad_normed.astype(jnp.float32)
    inner = lax.optimization_barrier(jnp.sum(gated * values_f, axis=-1, keepdims=True))
    return (row_scale * gated - values_f * row_scale ** 3 * inner / field.shape[-1]).astype(jnp.bfloat16)

def tile_attention(query_tiles, key_tiles, value_tiles, grad_tiles, tile_pairs, live_lengths):
    tile_count, tile_rows, head_width = query_tiles.shape
    neighbours = tile_pairs.shape[1]
    factor = 1.0 / math.sqrt(head_width)
    key_near = jnp.take(key_tiles, tile_pairs, axis=0).reshape(tile_count, neighbours * tile_rows, head_width)
    value_near = jnp.take(value_tiles, tile_pairs, axis=0).reshape(tile_count, neighbours * tile_rows, head_width)
    near_lengths = jnp.take(live_lengths, tile_pairs, axis=0)
    live = (jnp.arange(tile_rows, dtype=jnp.int32)[None, None, :] < near_lengths[:, :, None]).reshape(tile_count, neighbours * tile_rows)
    scores = multiply('aqd,akd->aqk', query_tiles, key_near) * factor
    scores = jnp.where(live[:, None, :], scores, -jnp.inf)
    row_max = lax.optimization_barrier(jnp.max(scores, axis=-1, keepdims=True))
    weights = jnp.exp(scores - row_max)
    probs = weights / lax.optimization_barrier(jnp.sum(weights, axis=-1, keepdims=True))
    probs_low = probs.astype(jnp.bfloat16)
    attended = multiply('aqk,akd->aqd', probs_low, value_near).astype(jnp.bfloat16)
    grad_probs = multiply('aqd,akd->aqk', grad_tiles, value_near)
    delta = lax.optimization_barrier(jnp.sum(probs * grad_probs, axis=-1, keepdims=True))
    grad_scores = (probs * (grad_probs - delta)).astype(jnp.bfloat16)
    grad_query = (multiply('aqk,akd->aqd', grad_scores, key_near) * factor).astype(jnp.bfloat16)
    grad_key_near = multiply('aqk,aqd->akd', grad_scores, query_tiles) * factor
    grad_value_near = multiply('aqk,aqd->akd', probs_low, grad_tiles)
    owners = (tile_pairs[:, :, None] == jnp.arange(tile_count, dtype=jnp.int32)[None, None, :]).astype(jnp.float32)
    grad_key = jnp.einsum('anb,antd->btd', owners, grad_key_near.reshape(tile_count, neighbours, tile_rows, head_width), precision=lax.Precision.HIGHEST).astype(jnp.bfloat16)
    grad_value = jnp.einsum('anb,antd->btd', owners, grad_value_near.reshape(tile_count, neighbours, tile_rows, head_width), precision=lax.Precision.HIGHEST).astype(jnp.bfloat16)
    return (attended, grad_query, grad_key, grad_value)

def reference(queries, keys, values, gain_q, gain_k, tile_pairs, tile_lens, out_grad, w_out):

    def split(field):
        return field.reshape(TILES, TILE, HEADS, HEAD_DIM).transpose(2, 0, 1, 3)

    def merge(field):
        return field.transpose(1, 2, 0, 3).reshape(CLIP_TOK, HD)

    def one_clip(running, inputs):
        clip_query, clip_key, clip_value, clip_grad, clip_lengths = inputs
        query_normed, query_scale = normalize(clip_query, gain_q)
        key_normed, key_scale = normalize(clip_key, gain_k)
        grad_attended = jnp.dot(clip_grad, w_out, preferred_element_type=jnp.float32).astype(jnp.bfloat16)

        def one_head(group):
            return tile_attention(group[0], group[1], group[2], group[3], tile_pairs, clip_lengths)
        attended, grad_qn, grad_kn, grad_vh = lax.map(one_head, (split(query_normed), split(key_normed), split(clip_value), split(grad_attended)))
        attended = merge(attended)
        running = running + jnp.dot(clip_grad.T, attended, preferred_element_type=jnp.float32) / N_DP
        grad_query = norm_back(clip_query, query_scale, gain_q, merge(grad_qn))
        grad_key = norm_back(clip_key, key_scale, gain_k, merge(grad_kn))
        return (running, (grad_query, grad_key, merge(grad_vh)))
    clips = (queries.reshape(N_DP, CLIP_TOK, HD), keys.reshape(N_DP, CLIP_TOK, HD), values.reshape(N_DP, CLIP_TOK, HD), out_grad.reshape(N_DP, CLIP_TOK, D), tile_lens)
    grad_w, stacked = lax.scan(one_clip, jnp.zeros((D, HD), jnp.float32), clips)
    grad_q = stacked[0].reshape(TOKENS, HD)
    grad_k = stacked[1].reshape(TOKENS, HD)
    grad_v = stacked[2].reshape(TOKENS, HD)
    return (grad_q, grad_k, grad_v, grad_w)
```

```python
import functools
import math

import jax
import jax.numpy as jnp
from jax import lax
from jax.experimental import pallas as pl
from jax.experimental.pallas import tpu as pltpu
from jax.sharding import Mesh, PartitionSpec as P

HEAD_DIM = 128


EPS = 1e-06
LOG2E = 1.4426950408889634


def contract(left, right, left_dim, right_dim):
    return lax.dot_general(
        left, right, (((left_dim,), (right_dim,)), ((), ())), preferred_element_type=jnp.float32
    )


def row_scale_of(values_f):
    return lax.rsqrt(jnp.mean(values_f * values_f, axis=-1, keepdims=True) + EPS)


def norm_kernel(x_ref, gain_ref, out_ref):
    values_f = x_ref[...].astype(jnp.float32)
    normed = (values_f * row_scale_of(values_f) * gain_ref[...]).astype(jnp.bfloat16)
    parts, _, width = out_ref.shape
    for part in range(parts):
        out_ref[part] = normed[:, part * width : (part + 1) * width]


def split_kernel(x_ref, out_ref):
    parts, _, width = out_ref.shape
    for part in range(parts):
        out_ref[part] = x_ref[:, part * width : (part + 1) * width]


def to_parts(field, gain, parts, block=64):
    rows, width = field.shape
    row_spec = pl.BlockSpec((block, width), lambda i: (i, 0))
    gain_spec = pl.BlockSpec((1, width), lambda i: (0, 0))
    return pl.pallas_call(
        split_kernel if gain is None else norm_kernel,
        grid=(rows // block,),
        in_specs=[row_spec] if gain is None else [row_spec, gain_spec],
        out_specs=pl.BlockSpec((parts, block, width // parts), lambda i: (0, i, 0)),
        out_shape=jax.ShapeDtypeStruct((parts, rows, width // parts), jnp.bfloat16),
        name="split_rows" if gain is None else "norm_rows",
    )(*((field,) if gain is None else (field, gain.reshape(1, width))))


def norm_back_kernel(x_ref, gain_ref, grad_ref, out_ref):
    parts = grad_ref.shape[0]
    width = x_ref.shape[1]
    values_f = x_ref[...].astype(jnp.float32)
    row_scale = row_scale_of(values_f)
    grad = jnp.concatenate([grad_ref[part] for part in range(parts)], axis=1).astype(jnp.float32)
    gated = gain_ref[...] * grad
    inner = jnp.sum(gated * values_f, axis=-1, keepdims=True)
    out_ref[...] = (
        row_scale * gated - values_f * (row_scale * row_scale * row_scale * inner * (1.0 / width))
    ).astype(jnp.bfloat16)


def join_kernel(parts_ref, out_ref):
    parts, _, width = parts_ref.shape
    for part in range(parts):
        out_ref[:, part * width : (part + 1) * width] = parts_ref[part]


def norm_back(field, gain, grad_parts, block=64):
    rows, width = field.shape
    parts = grad_parts.shape[0]
    row_spec = pl.BlockSpec((block, width), lambda i: (i, 0))
    return pl.pallas_call(
        norm_back_kernel,
        grid=(rows // block,),
        in_specs=[
            row_spec,
            pl.BlockSpec((1, width), lambda i: (0, 0)),
            pl.BlockSpec((parts, block, width // parts), lambda i: (0, i, 0)),
        ],
        out_specs=row_spec,
        out_shape=jax.ShapeDtypeStruct((rows, width), jnp.bfloat16),
        name="norm_back",
    )(field, gain.reshape(1, width), grad_parts)


def join(parts_of, block=64):
    parts, rows, width = parts_of.shape
    return pl.pallas_call(
        join_kernel,
        grid=(rows // block,),
        in_specs=[pl.BlockSpec((parts, block, width), lambda i: (0, i, 0))],
        out_specs=pl.BlockSpec((block, parts * width), lambda i: (i, 0)),
        out_shape=jax.ShapeDtypeStruct((rows, parts * width), jnp.bfloat16),
        name="join_rows",
    )(parts_of)


def attention_kernel(tile_rows, pairs_ref, lens_ref, q_ref, k_ref, v_ref, g_ref,
                     att_ref, gq_ref, gk_ref, gv_ref, gk_acc, gv_acc):
    clip_rows, width = q_ref.shape
    tile_count, neighbours = pairs_ref.shape
    factor = 1.0 / math.sqrt(width)
    rows = 2 * tile_rows
    gk_acc[...] = jnp.zeros_like(gk_acc)
    gv_acc[...] = jnp.zeros_like(gv_acc)
    lane = lax.broadcasted_iota(jnp.int32, (tile_rows, rows), 1)
    slot = lax.broadcasted_iota(jnp.int32, (tile_rows, rows), 0)
    first = lane < tile_rows
    pair_first = (lax.broadcasted_iota(jnp.int32, (rows, 2 * width), 0) < tile_rows) == (
        lax.broadcasted_iota(jnp.int32, (rows, 2 * width), 1) < width)

    def spread(block):
        twice = jnp.concatenate([block, block], axis=1)
        return jnp.where(pair_first, twice, jnp.zeros_like(twice))

    def tile(ref, index):
        return ref[pl.ds(pl.multiple_of(index * tile_rows, tile_rows), tile_rows), :]

    def step(pair, carry):
        row = pl.multiple_of(pair * rows, rows)
        near = [[pairs_ref[2 * pair + half, n] for n in range(neighbours)] for half in range(2)]
        keys = jnp.concatenate(
            [jnp.concatenate([tile(k_ref, near[0][n]), tile(k_ref, near[1][n])], axis=1)
             for n in range(neighbours)], axis=0)
        vals = jnp.concatenate(
            [jnp.concatenate([tile(v_ref, near[0][n]), tile(v_ref, near[1][n])], axis=1)
             for n in range(neighbours)], axis=0)
        queries = spread(q_ref[pl.ds(row, rows), :])
        grads = spread(g_ref[pl.ds(row, rows), :])
        scores = contract(keys, queries, 1, 1)
        live = jnp.concatenate(
            [slot < jnp.where(first, lens_ref[0, near[0][n]], lens_ref[0, near[1][n]])
             for n in range(neighbours)], axis=0)
        scores = jnp.where(live, scores * (factor * LOG2E), -jnp.inf)
        top = jnp.max(scores, axis=0, keepdims=True)
        weights = jnp.exp2(scores - top)
        probs = weights * (1.0 / jnp.sum(weights, axis=0, keepdims=True))
        probs_low = probs.astype(jnp.bfloat16)
        grad_probs = contract(vals, grads, 1, 1)
        delta = jnp.sum(probs * grad_probs, axis=0, keepdims=True)
        grad_scores = (probs * (grad_probs - delta)).astype(jnp.bfloat16)
        attended = contract(probs_low, vals, 0, 0)
        grad_query = contract(grad_scores, keys, 0, 0) * factor
        for half in range(2):
            at = (slice(half * tile_rows, (half + 1) * tile_rows), slice(half * width, (half + 1) * width))
            place = pl.ds(pl.multiple_of(row + half * tile_rows, tile_rows), tile_rows)
            att_ref[place, :] = attended[at].astype(jnp.bfloat16)
            gq_ref[place, :] = grad_query[at].astype(jnp.bfloat16)
        grad_keys = contract(grad_scores, queries, 1, 0)
        grad_vals = contract(probs_low, grads, 1, 0)
        for half in range(2):
            for n in range(neighbours):
                at = (slice(n * tile_rows, (n + 1) * tile_rows), slice(half * width, (half + 1) * width))
                place = pl.ds(pl.multiple_of(near[half][n] * tile_rows, tile_rows), tile_rows)
                gk_acc[place, :] += grad_keys[at]
                gv_acc[place, :] += grad_vals[at]
        return carry

    lax.fori_loop(0, tile_count // 2, step, 0)
    gk_ref[...] = (gk_acc[...] * factor).astype(jnp.bfloat16)
    gv_ref[...] = gv_acc[...].astype(jnp.bfloat16)


def attention(queries, keys, values, grads, tile_pairs, tile_lens):
    clip_rows, local_width = queries.shape
    tile_rows = clip_rows // tile_pairs.shape[0]
    block = pl.BlockSpec((clip_rows, HEAD_DIM), lambda h: (0, h))
    smem = pl.BlockSpec(memory_space=pltpu.SMEM)
    return pl.pallas_call(
        functools.partial(attention_kernel, tile_rows),
        grid=(local_width // HEAD_DIM,),
        in_specs=[smem, smem, block, block, block, block],
        out_specs=[block] * 4,
        out_shape=[jax.ShapeDtypeStruct(queries.shape, jnp.bfloat16)] * 4,
        scratch_shapes=[pltpu.VMEM((clip_rows, HEAD_DIM), jnp.float32)] * 2,
        compiler_params=pltpu.CompilerParams(vmem_limit_bytes=32 << 20),
        name="tile_attention",
    )(tile_pairs, tile_lens, queries, keys, values, grads)


def per_device(queries, keys, values, gain_q, gain_k, tile_pairs, tile_lens, out_grad, w_out):
    seq_count = lax.axis_size("seq")
    dp_count = lax.axis_size("dp")
    tok_rows, width = queries.shape
    local_width = width // seq_count
    clip_rows = tok_rows * seq_count

    def exchange(parts):
        return lax.all_to_all(parts, "seq", split_axis=0, concat_axis=0, tiled=True)

    def to_heads(parts):
        return exchange(parts).reshape(clip_rows, local_width)

    def to_rows(field):
        return exchange(field.reshape(seq_count, tok_rows, local_width))

    query_heads = to_heads(to_parts(queries, gain_q, seq_count))
    key_heads = to_heads(to_parts(keys, gain_k, seq_count))
    value_heads = to_heads(to_parts(values, None, seq_count))
    cot_all = lax.all_gather(out_grad, "seq", axis=0, tiled=True)
    w_all = lax.all_gather(w_out, "dp", axis=0, tiled=True)
    grad_attended = jnp.dot(cot_all, w_all, preferred_element_type=jnp.float32).astype(jnp.bfloat16)
    attended, grad_qn, grad_kn, grad_vh = attention(
        query_heads, key_heads, value_heads, grad_attended, tile_pairs, tile_lens
    )
    grad_w = lax.psum_scatter(
        (
            jnp.einsum("td,te->de", cot_all, attended, preferred_element_type=jnp.float32) / dp_count
        ).astype(jnp.bfloat16),
        "dp",
        scatter_dimension=0,
        tiled=True,
    ).astype(jnp.float32)
    grad_q = norm_back(queries, gain_q, to_rows(grad_qn))
    grad_k = norm_back(keys, gain_k, to_rows(grad_kn))
    grad_v = join(to_rows(grad_vh))
    return (grad_q, grad_k, grad_v, grad_w)


def solution(mesh):
    return jax.shard_map(
        per_device,
        mesh=mesh,
        in_specs=(
            P(("dp", "seq"), None),
            P(("dp", "seq"), None),
            P(("dp", "seq"), None),
            P(),
            P(),
            P(),
            P("dp", None),
            P(("dp", "seq"), None),
            P("dp", "seq"),
        ),
        out_specs=(
            P(("dp", "seq"), None),
            P(("dp", "seq"), None),
            P(("dp", "seq"), None),
            P("dp", "seq"),
        ),
        check_vma=False,
    )
```

```python
import functools
import math

import jax
import jax.numpy as jnp
from jax import lax
from jax.experimental import pallas as pl
from jax.experimental.pallas import tpu as pltpu
from jax.sharding import Mesh, PartitionSpec as P

HEAD_DIM = 128


EPS = 1e-06
LOG2E = 1.4426950408889634
MIN_LIVE = 40
SEQ = 4
CORES = 2


def smem():
    return pl.BlockSpec(memory_space=pltpu.SMEM)


def params():
    return pltpu.CompilerParams(vmem_limit_bytes=48 << 20)


def contract(left, right, left_dim, right_dim):
    return lax.dot_general(
        left, right, (((left_dim,), (right_dim,)), ((), ())), preferred_element_type=jnp.float32
    )


def row_scale_of(values_f):
    return lax.rsqrt(jnp.mean(values_f * values_f, axis=-1, keepdims=True) + EPS)


def shard_of(place_ref, round_, width):
    return pl.ds(pl.multiple_of(jnp.bitwise_xor(place_ref[0], round_) * width, 128), width)


def norm_kernel(place_ref, x_ref, gain_ref, *refs):
    outs, normed = refs[:-1], refs[-1]
    values_f = x_ref[...].astype(jnp.float32)
    normed[...] = (values_f * row_scale_of(values_f) * gain_ref[...]).astype(jnp.bfloat16)
    for round_, out in enumerate(outs):
        out[...] = normed[:, shard_of(place_ref, round_, out.shape[1])]


def split_kernel(place_ref, x_ref, *outs):
    for round_, out in enumerate(outs):
        out[...] = x_ref[:, shard_of(place_ref, round_, out.shape[1])]


def to_rounds(place, field, gain, block=64):
    rows, width = field.shape
    row_spec = pl.BlockSpec((block, width), lambda i: (i, 0))
    gain_spec = pl.BlockSpec((1, width), lambda i: (0, 0))
    plain = gain is None
    return pl.pallas_call(
        split_kernel if plain else norm_kernel,
        grid=(rows // block,),
        in_specs=[smem(), row_spec] + ([] if plain else [gain_spec]),
        out_specs=[pl.BlockSpec((block, width // SEQ), lambda i: (i, 0))] * SEQ,
        out_shape=[jax.ShapeDtypeStruct((rows, width // SEQ), jnp.bfloat16)] * SEQ,
        scratch_shapes=[] if plain else [pltpu.VMEM((block, width), jnp.bfloat16)],
        name="split_rows" if plain else "norm_rows",
    )(place, field, *(() if plain else (gain.reshape(1, width),)))


def norm_back_kernel(place_ref, x_ref, gain_ref, *refs):
    parts, out_ref, joined = refs[:-2], refs[-2], refs[-1]
    width = x_ref.shape[1]
    for round_, part in enumerate(parts):
        joined[:, shard_of(place_ref, round_, part.shape[1])] = part[...]
    values_f = x_ref[...].astype(jnp.float32)
    row_scale = row_scale_of(values_f)
    gated = gain_ref[...] * joined[...].astype(jnp.float32)
    inner = jnp.sum(gated * values_f, axis=-1, keepdims=True)
    out_ref[...] = (
        row_scale * gated - values_f * (row_scale * row_scale * row_scale * inner * (1.0 / width))
    ).astype(jnp.bfloat16)


def join_kernel(place_ref, *refs):
    parts, out_ref = refs[:-1], refs[-1]
    for round_, part in enumerate(parts):
        out_ref[:, shard_of(place_ref, round_, part.shape[1])] = part[...]


def from_rounds(place, parts, field=None, gain=None, block=64):
    rows, part_width = parts[0].shape
    width = part_width * SEQ
    row_spec = pl.BlockSpec((block, width), lambda i: (i, 0))
    part_specs = [pl.BlockSpec((block, part_width), lambda i: (i, 0))] * SEQ
    plain = field is None
    return pl.pallas_call(
        join_kernel if plain else norm_back_kernel,
        grid=(rows // block,),
        in_specs=[smem()]
        + ([] if plain else [row_spec, pl.BlockSpec((1, width), lambda i: (0, 0))])
        + part_specs,
        out_specs=row_spec,
        out_shape=jax.ShapeDtypeStruct((rows, width), jnp.bfloat16),
        scratch_shapes=[] if plain else [pltpu.VMEM((block, width), jnp.bfloat16)],
        name="join_rows" if plain else "norm_back",
    )(place, *(() if plain else (field, gain.reshape(1, width))), *parts)


def tile_at(ref, index, rows):
    return ref[pl.ds(pl.multiple_of(index * rows, rows), rows), :]


def gather_pair(ref, near, rows):
    return jnp.concatenate(
        [
            jnp.concatenate([tile_at(ref, one, rows), tile_at(ref, two, rows)], axis=1)
            for one, two in zip(*near)
        ],
        axis=0,
    )


def spread(block, rows):
    twice = jnp.concatenate([block, block], axis=1)
    width = block.shape[1]
    own = (lax.broadcasted_iota(jnp.int32, twice.shape, 0) < rows) == (
        lax.broadcasted_iota(jnp.int32, twice.shape, 1) < width
    )
    return jnp.where(own, twice, jnp.zeros_like(twice))


def near_of(place_ref, pairs_ref, pair):
    flip = place_ref[3]
    return [
        [
            jnp.bitwise_xor(pairs_ref[jnp.bitwise_xor(2 * pair + half, flip), n], flip)
            for n in range(pairs_ref.shape[1])
        ]
        for half in range(2)
    ]


def forward_kernel(place_ref, pairs_ref, lens_ref, *refs):
    q_parts, k_parts, v_parts = refs[:SEQ], refs[SEQ : 2 * SEQ], refs[2 * SEQ : 3 * SEQ]
    att_ref, probs_ref, q_all, k_all, v_all = refs[3 * SEQ :]
    tile_count, neighbours = pairs_ref.shape
    clip_rows, width = q_all.shape
    tile_rows = clip_rows // tile_count
    rows = 2 * tile_rows
    depth = neighbours * tile_rows
    scale = LOG2E / math.sqrt(width)
    for parts, whole in ((q_parts, q_all), (k_parts, k_all), (v_parts, v_all)):
        for at, part in enumerate(parts):
            whole[at * part.shape[0] : (at + 1) * part.shape[0], :] = part[...]
    shape = (tile_rows - MIN_LIVE, rows)
    first = lax.broadcasted_iota(jnp.int32, shape, 1) < tile_rows
    slot = lax.broadcasted_iota(jnp.int32, shape, 0) + MIN_LIVE

    def length(tile):
        return lens_ref[0, jnp.bitwise_xor(tile, place_ref[3])]

    def step(pair, carry):
        row = pl.multiple_of(pair * rows, rows)
        near = near_of(place_ref, pairs_ref, pair)
        keys = gather_pair(k_all, near, tile_rows)
        vals = gather_pair(v_all, near, tile_rows)
        queries = spread(q_all[pl.ds(row, rows), :], tile_rows)
        scores = contract(keys, queries, 1, 1)
        pieces = []
        for n in range(neighbours):
            start = n * tile_rows
            pieces.append(scores[start : start + MIN_LIVE])
            live = slot < jnp.where(first, length(near[0][n]), length(near[1][n]))
            pieces.append(jnp.where(live, scores[start + MIN_LIVE : start + tile_rows], -jnp.inf))
        scores = jnp.concatenate(pieces, axis=0)
        weights = jnp.exp2((scores - jnp.max(scores, axis=0, keepdims=True)) * scale)
        probs = weights * (1.0 / jnp.sum(weights, axis=0, keepdims=True))
        probs_low = probs.astype(jnp.bfloat16)
        probs_ref[0, pl.ds(pl.multiple_of(pair * depth, depth), depth), :] = probs_low
        attended = contract(probs_low, vals, 0, 0)
        for half in range(2):
            part = attended[half * tile_rows : (half + 1) * tile_rows, half * width : (half + 1) * width]
            place = pl.ds(pl.multiple_of(row + half * tile_rows, tile_rows), tile_rows)
            att_ref[place, :] = part.astype(jnp.bfloat16)
        return carry

    lax.fori_loop(0, tile_count // 2, step, 0, unroll=2)


def forward(place, tile_pairs, lens, query_parts, key_parts, value_parts):
    rows, local_width = query_parts[0].shape
    heads = local_width // HEAD_DIM
    clip_rows = rows * SEQ
    pairs = tile_pairs.shape[0] // 2
    depth = tile_pairs.shape[1] * (clip_rows // tile_pairs.shape[0])
    part_spec = pl.BlockSpec((rows, HEAD_DIM), lambda h: (0, h))
    return pl.pallas_call(
        forward_kernel,
        grid=(heads,),
        in_specs=[smem()] * 3 + [part_spec] * (3 * SEQ),
        out_specs=[
            pl.BlockSpec((clip_rows, HEAD_DIM), lambda h: (0, h)),
            pl.BlockSpec((1, pairs * depth, HEAD_DIM), lambda h: (h, 0, 0)),
        ],
        out_shape=[
            jax.ShapeDtypeStruct((clip_rows, local_width), jnp.bfloat16),
            jax.ShapeDtypeStruct((heads, pairs * depth, HEAD_DIM), jnp.bfloat16),
        ],
        scratch_shapes=[pltpu.VMEM((clip_rows, HEAD_DIM), jnp.bfloat16)] * 3,
        compiler_params=params(),
        name="attention_forward",
    )(place, tile_pairs, lens, *query_parts, *key_parts, *value_parts)


def backward_kernel(place_ref, pairs_ref, *refs):
    q_parts, k_parts, v_parts = refs[:SEQ], refs[SEQ : 2 * SEQ], refs[2 * SEQ : 3 * SEQ]
    own_grads, other_grads = refs[3 * SEQ : 4 * SEQ], refs[4 * SEQ : 5 * SEQ]
    probs_ref = refs[5 * SEQ]
    outs = refs[5 * SEQ + 1 : 8 * SEQ + 1]
    q_all, k_all, v_all, g_all, gq_all, gk_acc, gv_acc = refs[8 * SEQ + 1 :]
    tile_count, neighbours = pairs_ref.shape
    clip_rows, width = q_all.shape
    tile_rows = clip_rows // tile_count
    rows = 2 * tile_rows
    depth = neighbours * tile_rows
    factor = 1.0 / math.sqrt(width)
    for parts, whole in ((q_parts, q_all), (k_parts, k_all), (v_parts, v_all)):
        for at, part in enumerate(parts):
            whole[at * part.shape[0] : (at + 1) * part.shape[0], :] = part[...]
    half_rows = own_grads[0].shape[0]
    core = place_ref[1]
    for at in range(SEQ):
        for grads, half in ((own_grads[at], core), (other_grads[at ^ 1], 1 - core)):
            g_all[pl.ds(pl.multiple_of((2 * at + half) * half_rows, half_rows), half_rows), :] = grads[...]
    gk_acc[...] = jnp.zeros_like(gk_acc)
    gv_acc[...] = jnp.zeros_like(gv_acc)

    def step(pair, carry):
        row = pl.multiple_of(pair * rows, rows)
        near = near_of(place_ref, pairs_ref, pair)
        keys = gather_pair(k_all, near, tile_rows)
        vals = gather_pair(v_all, near, tile_rows)
        queries = spread(q_all[pl.ds(row, rows), :], tile_rows)
        grads = spread(g_all[pl.ds(row, rows), :], tile_rows)
        probs_low = probs_ref[0, pl.ds(pl.multiple_of(pair * depth, depth), depth), :]
        probs = probs_low.astype(jnp.float32)
        grad_probs = contract(vals, grads, 1, 1)
        delta = jnp.sum(probs * grad_probs, axis=0, keepdims=True)
        grad_scores = (probs * (grad_probs - delta)).astype(jnp.bfloat16)
        grad_query = contract(grad_scores, keys, 0, 0) * factor
        for half in range(2):
            part = grad_query[half * tile_rows : (half + 1) * tile_rows, half * width : (half + 1) * width]
            place = pl.ds(pl.multiple_of(row + half * tile_rows, tile_rows), tile_rows)
            gq_all[place, :] = part.astype(jnp.bfloat16)
        grad_keys = contract(grad_scores, queries, 1, 0)
        grad_vals = contract(probs_low, grads, 1, 0)
        for half in range(2):
            for n in range(neighbours):
                at = (slice(n * tile_rows, (n + 1) * tile_rows), slice(half * width, (half + 1) * width))
                place = pl.ds(pl.multiple_of(near[half][n] * tile_rows, tile_rows), tile_rows)
                gk_acc[place, :] += grad_keys[at]
                gv_acc[place, :] += grad_vals[at]
        return carry

    lax.fori_loop(0, tile_count // 2, step, 0)
    for at in range(SEQ):
        part = slice(at * outs[0].shape[0], (at + 1) * outs[0].shape[0])
        outs[at][...] = gq_all[part, :]
        outs[SEQ + at][...] = (gk_acc[part, :] * factor).astype(jnp.bfloat16)
        outs[2 * SEQ + at][...] = gv_acc[part, :].astype(jnp.bfloat16)


def backward(place, tile_pairs, query_parts, key_parts, value_parts, own_grads, other_grads, probs):
    rows, local_width = query_parts[0].shape
    heads = local_width // HEAD_DIM
    clip_rows = rows * SEQ
    part_spec = pl.BlockSpec((rows, HEAD_DIM), lambda h: (0, h))
    grad_spec = pl.BlockSpec((own_grads[0].shape[0], HEAD_DIM), lambda h: (0, h))
    bf16_rows = pltpu.VMEM((clip_rows, HEAD_DIM), jnp.bfloat16)
    f32_rows = pltpu.VMEM((clip_rows, HEAD_DIM), jnp.float32)
    outs = pl.pallas_call(
        backward_kernel,
        grid=(heads,),
        in_specs=[smem()] * 2
        + [part_spec] * (3 * SEQ)
        + [grad_spec] * (2 * SEQ)
        + [pl.BlockSpec((1,) + probs.shape[1:], lambda h: (h, 0, 0))],
        out_specs=[part_spec] * (3 * SEQ),
        out_shape=[jax.ShapeDtypeStruct((rows, local_width), jnp.bfloat16)] * (3 * SEQ),
        scratch_shapes=[bf16_rows] * 5 + [f32_rows] * 2,
        compiler_params=params(),
        name="attention_backward",
    )(place, tile_pairs, *query_parts, *key_parts, *value_parts, *own_grads, *other_grads, probs)
    return outs[:SEQ], outs[SEQ : 2 * SEQ], outs[2 * SEQ :]


def weight_grad_kernel(place_ref, mean, att_ref, *refs):
    own, other, out_ref = refs[:SEQ], refs[SEQ : 2 * SEQ], refs[2 * SEQ]
    half_rows = own[0].shape[0]
    core = place_ref[1]
    columns, attended = [], []
    for at in range(SEQ):
        for part, half in ((own[at], core), (other[at ^ 1], 1 - core)):
            columns.append(part[...])
            start = pl.multiple_of((2 * at + half) * half_rows, half_rows)
            attended.append(att_ref[pl.ds(start, half_rows), :])
    total = contract(jnp.concatenate(columns, axis=0), jnp.concatenate(attended, axis=0), 0, 0)
    out_ref[...] = (total * mean).astype(jnp.bfloat16)


def weight_grad(place, attended, own, other, mean, block=640):
    half_rows, features = own[0].shape
    local_width = attended.shape[1]
    return pl.pallas_call(
        lambda place_ref, *refs: weight_grad_kernel(place_ref, mean, *refs),
        grid=(features // block,),
        in_specs=[smem(), pl.BlockSpec(attended.shape, lambda i: (0, 0))]
        + [pl.BlockSpec((half_rows, block), lambda i: (0, i))] * (2 * SEQ),
        out_specs=pl.BlockSpec((block, local_width), lambda i: (i, 0)),
        out_shape=jax.ShapeDtypeStruct((features, local_width), jnp.bfloat16),
        compiler_params=params(),
        name="weight_grad",
    )(place, attended, *own, *other)


def device_of(core, seq):
    return core * SEQ + seq


def outward(round_):
    pairs = []
    for core in range(CORES):
        for token in range(SEQ):
            shard = token ^ round_
            pairs.append((device_of(core, token), device_of(shard % 2, 2 * core + shard // 2)))
    return pairs


def inward(round_):
    return [(target, source) for source, target in outward(round_)]


def send(value, pairs):
    return lax.ppermute(value, ("core", "seq"), pairs)


def swap_cores(value):
    return lax.ppermute(value, "core", [(0, 1), (1, 0)])


def shift(value, axis, by):
    count = lax.axis_size(axis)
    return lax.ppermute(value, axis, [(i, (i + by) % count) for i in range(count)])


def add(*terms):
    total = terms[0].astype(jnp.float32)
    for term in terms[1:]:
        total = total + term.astype(jnp.float32)
    return total.astype(jnp.bfloat16)


def take(value, index, axis=0):
    return lax.dynamic_index_in_dim(value, index, axis, keepdims=False)


def scatter_sum(value, axis, dim=0):
    here = lax.axis_index(axis)
    count = lax.axis_size(axis)
    got = [shift(take(value, (here + by) % count, dim), axis, by) for by in (2, 1, 3)]
    return add(take(value, here, dim), *got)


def to_shard_holders(w_out, core, seq):
    got = []
    for other in range(2):
        pairs = []
        for holder in range(CORES):
            for shard in range(SEQ):
                window = holder ^ other
                pairs.append((device_of(holder, shard), device_of(shard % 2, shard // 2 + 2 * window)))
        got.append(send(w_out, pairs))
    window = seq // 2
    return jnp.where(window == 0, jnp.concatenate(got), jnp.concatenate(got[::-1]))


def to_owners(total, seq):
    half = total.shape[0] // 2
    window = seq // 2
    got = []
    for other in range(2):
        pairs = []
        for core in range(CORES):
            for at in range(SEQ):
                holder = (at // 2) ^ other
                pairs.append((device_of(core, at), device_of(holder, 2 * (at % 2) + core)))
        rows = jnp.where((window ^ other) == 0, total[:half], total[half:])
        got.append(send(rows, pairs))
    return got[0].astype(jnp.float32) + got[1].astype(jnp.float32)


def per_device(queries, keys, values, gain_q, gain_k, tile_pairs, tile_lens, out_grad, w_out):
    core = lax.axis_index("core")
    seq = lax.axis_index("seq")
    count_z = lax.axis_size("z")
    count_x = lax.axis_size("x")
    rows, features = out_grad.shape
    shard = 2 * (seq % 2) + core
    tiles_per_block = tile_pairs.shape[0] // SEQ
    place = jnp.stack([seq, core, shard, shard * tiles_per_block]).astype(jnp.int32)
    lens = jnp.where(seq // 2 == core, tile_lens, swap_cores(tile_lens))

    rounds = range(SEQ)
    key_parts = [send(part, outward(r)) for r, part in enumerate(to_rounds(place, keys, gain_k))]
    query_parts = [send(part, outward(r)) for r, part in enumerate(to_rounds(place, queries, gain_q))]
    value_parts = [send(part, outward(r)) for r, part in enumerate(to_rounds(place, values, None))]

    halves = out_grad.reshape(2, rows // 2, features)
    even = take(halves, seq % 2)
    odd = take(halves, 1 - seq % 2)
    own = [send(odd if r % 2 else even, outward(r)) for r in rounds]
    other = [swap_cores(part) for part in own]

    w_all = lax.all_gather(to_shard_holders(w_out, core, seq), ("z", "x"), axis=0, tiled=True)

    def project(part):
        return jnp.dot(part, w_all, preferred_element_type=jnp.float32).astype(jnp.bfloat16)

    attended, probs = forward(place, tile_pairs, lens, query_parts, key_parts, value_parts)
    own_grads = [project(part) for part in own]
    other_grads = [project(part) for part in other]
    grad_w = weight_grad(place, attended, own, other, 1.0 / (count_z * count_x * CORES))
    grad_qn, grad_kn, grad_vh = backward(
        place, tile_pairs, query_parts, key_parts, value_parts, own_grads, other_grads, probs
    )

    def to_rows(parts):
        return [send(part, inward(r)) for r, part in enumerate(parts)]

    grad_q = from_rounds(place, to_rows(grad_qn), queries, gain_q)
    grad_k = from_rounds(place, to_rows(grad_kn), keys, gain_k)
    grad_v = from_rounds(place, to_rows(grad_vh))

    grad_w = grad_w.reshape(count_z, count_x, 2, -1, grad_w.shape[1])
    one = scatter_sum(scatter_sum(grad_w[:, :, 0], "x", 1), "z")
    two = scatter_sum(scatter_sum(grad_w[:, :, 1], "z"), "x")
    grad_w = to_owners(jnp.concatenate([one, two]), seq)
    return (grad_q, grad_k, grad_v, grad_w)


def solution(mesh):
    dp = mesh.shape["dp"]
    side = math.isqrt(dp // CORES)
    parts = Mesh(mesh.devices.reshape(side, side, CORES, SEQ), ("z", "x", "core", "seq"))
    dp_axes = ("z", "x", "core")
    tokens = P(dp_axes + ("seq",), None)
    return jax.shard_map(
        per_device,
        mesh=parts,
        in_specs=(tokens, tokens, tokens, P(), P(), P(), P(dp_axes, None), tokens, P(dp_axes, "seq")),
        out_specs=(tokens, tokens, tokens, P(dp_axes, "seq")),
        check_vma=False,
    )
```

```python
import functools
import math

import jax
import jax.numpy as jnp
from jax import lax
from jax.experimental import pallas as pl
from jax.experimental.pallas import tpu as pltpu
from jax.sharding import Mesh, PartitionSpec as P

HEAD_DIM = 128


EPS = 1e-06
LOG2E = 1.4426950408889634
MIN_LIVE = 40
SEQ = 4
CORES = 2
GROUP = 4


def smem():
    return pl.BlockSpec(memory_space=pltpu.SMEM)


def params():
    return pltpu.CompilerParams(vmem_limit_bytes=48 << 20)


def contract(left, right, left_dim, right_dim):
    return lax.dot_general(
        left, right, (((left_dim,), (right_dim,)), ((), ())), preferred_element_type=jnp.float32
    )


def row_scale_of(values_f):
    return lax.rsqrt(jnp.mean(values_f * values_f, axis=-1, keepdims=True) + EPS)


def shard_of(place_ref, round_, width):
    return pl.ds(pl.multiple_of(jnp.bitwise_xor(place_ref[0], round_) * width, 128), width)


def rounds_kernel(place_ref, q_ref, k_ref, v_ref, gain_q_ref, gain_k_ref, *refs):
    outs, normed = refs[:-1], refs[-1]
    for at, (x_ref, gain_ref) in enumerate(((q_ref, gain_q_ref), (k_ref, gain_k_ref))):
        values_f = x_ref[...].astype(jnp.float32)
        normed[at] = (values_f * row_scale_of(values_f) * gain_ref[...]).astype(jnp.bfloat16)
    for round_, out in enumerate(outs):
        columns = shard_of(place_ref, round_, out.shape[2])
        out[0] = normed[0, :, columns]
        out[1] = normed[1, :, columns]
        out[2] = v_ref[:, columns]


def to_rounds(place, queries, keys, values, gain_q, gain_k, block=64):
    rows, width = queries.shape
    row_spec = pl.BlockSpec((block, width), lambda i: (i, 0))
    gain_spec = pl.BlockSpec((1, width), lambda i: (0, 0))
    return pl.pallas_call(
        rounds_kernel,
        grid=(rows // block,),
        in_specs=[smem()] + [row_spec] * 3 + [gain_spec] * 2,
        out_specs=[pl.BlockSpec((3, block, width // SEQ), lambda i: (0, i, 0))] * SEQ,
        out_shape=[jax.ShapeDtypeStruct((3, rows, width // SEQ), jnp.bfloat16)] * SEQ,
        scratch_shapes=[pltpu.VMEM((2, block, width), jnp.bfloat16)],
        name="norm_rows",
    )(place, queries, keys, values, gain_q.reshape(1, width), gain_k.reshape(1, width))


def finish_kernel(place_ref, q_ref, k_ref, gain_q_ref, gain_k_ref, *refs):
    parts, outs, joined = refs[:SEQ], refs[SEQ:-1], refs[-1]
    width = q_ref.shape[1]
    for round_, part in enumerate(parts):
        columns = shard_of(place_ref, round_, part.shape[2])
        joined[0, :, columns] = part[0]
        joined[1, :, columns] = part[1]
        outs[2][:, columns] = part[2]
    for at, (x_ref, gain_ref) in enumerate(((q_ref, gain_q_ref), (k_ref, gain_k_ref))):
        values_f = x_ref[...].astype(jnp.float32)
        row_scale = row_scale_of(values_f)
        gated = gain_ref[...] * joined[at].astype(jnp.float32)
        inner = jnp.sum(gated * values_f, axis=-1, keepdims=True)
        back = values_f * (row_scale * row_scale * row_scale * inner * (1.0 / width))
        outs[at][...] = (row_scale * gated - back).astype(jnp.bfloat16)


def finish(place, queries, keys, gain_q, gain_k, parts, block=64):
    rows, width = queries.shape
    row_spec = pl.BlockSpec((block, width), lambda i: (i, 0))
    gain_spec = pl.BlockSpec((1, width), lambda i: (0, 0))
    return pl.pallas_call(
        finish_kernel,
        grid=(rows // block,),
        in_specs=[smem()]
        + [row_spec] * 2
        + [gain_spec] * 2
        + [pl.BlockSpec((3, block, width // SEQ), lambda i: (0, i, 0))] * SEQ,
        out_specs=[row_spec] * 3,
        out_shape=[jax.ShapeDtypeStruct((rows, width), jnp.bfloat16)] * 3,
        scratch_shapes=[pltpu.VMEM((2, block, width), jnp.bfloat16)],
        name="norm_back",
    )(place, queries, keys, gain_q.reshape(1, width), gain_k.reshape(1, width), *parts)


def tile_at(ref, index, rows):
    return ref[pl.ds(pl.multiple_of(index * rows, rows), rows), :]


def gather_pair(ref, near, rows):
    return jnp.concatenate(
        [
            jnp.concatenate([tile_at(ref, one, rows), tile_at(ref, two, rows)], axis=1)
            for one, two in zip(*near)
        ],
        axis=0,
    )


def spread(block, rows):
    twice = jnp.concatenate([block, block], axis=1)
    width = block.shape[1]
    own = (lax.broadcasted_iota(jnp.int32, twice.shape, 0) < rows) == (
        lax.broadcasted_iota(jnp.int32, twice.shape, 1) < width
    )
    return jnp.where(own, twice, jnp.zeros_like(twice))


def near_of(place_ref, pairs_ref, pair):
    flip = place_ref[3]
    return [
        [
            jnp.bitwise_xor(pairs_ref[jnp.bitwise_xor(2 * pair + half, flip), n], flip)
            for n in range(pairs_ref.shape[1])
        ]
        for half in range(2)
    ]


def load_parts(parts, whole):
    for at, part in enumerate(parts):
        whole[at * part.shape[0] : (at + 1) * part.shape[0], :] = part[...]


def diagonal(product, half, tile_rows, width):
    return product[half * tile_rows : (half + 1) * tile_rows, half * width : (half + 1) * width]


def forward_kernel(place_ref, pairs_ref, lens_ref, *refs):
    q_parts, k_parts, v_parts = refs[:SEQ], refs[SEQ : 2 * SEQ], refs[2 * SEQ : 3 * SEQ]
    att_ref, probs_ref, q_all, k_all, v_all = refs[3 * SEQ :]
    tile_count, neighbours = pairs_ref.shape
    clip_rows, width = q_all.shape
    tile_rows = clip_rows // tile_count
    rows = 2 * tile_rows
    depth = neighbours * tile_rows
    scale = LOG2E / math.sqrt(width)
    load_parts(q_parts, q_all)
    load_parts(k_parts, k_all)
    load_parts(v_parts, v_all)
    shape = (tile_rows - MIN_LIVE, rows)
    first = lax.broadcasted_iota(jnp.int32, shape, 1) < tile_rows
    slot = lax.broadcasted_iota(jnp.int32, shape, 0) + MIN_LIVE

    def length(tile):
        return lens_ref[0, jnp.bitwise_xor(tile, place_ref[3])]

    def score(pair, near):
        keys = gather_pair(k_all, near, tile_rows)
        queries = spread(q_all[pl.ds(pl.multiple_of(pair * rows, rows), rows), :], tile_rows)
        scores = contract(keys, queries, 1, 1)
        pieces = []
        for n in range(neighbours):
            start = n * tile_rows
            pieces.append(scores[start : start + MIN_LIVE])
            live = slot < jnp.where(first, length(near[0][n]), length(near[1][n]))
            pieces.append(jnp.where(live, scores[start + MIN_LIVE : start + tile_rows], -jnp.inf))
        return jnp.concatenate(pieces, axis=0)

    def soften(scores):
        weights = jnp.exp2((scores - jnp.max(scores, axis=0, keepdims=True)) * scale)
        return (weights * (1.0 / jnp.sum(weights, axis=0, keepdims=True))).astype(jnp.bfloat16)

    def body(group, carry):
        pairs = [group * GROUP + at for at in range(GROUP)]
        nears = [near_of(place_ref, pairs_ref, pair) for pair in pairs]
        probs = [soften(score(pair, near)) for pair, near in zip(pairs, nears)]
        attended = [
            contract(prob, gather_pair(v_all, near, tile_rows), 0, 0) for prob, near in zip(probs, nears)
        ]
        for pair, prob, product in zip(pairs, probs, attended):
            probs_ref[0, pl.ds(pl.multiple_of(pair * depth, depth), depth), :] = prob
            for half in range(2):
                place = pl.ds(pl.multiple_of((2 * pair + half) * tile_rows, tile_rows), tile_rows)
                att_ref[place, :] = diagonal(product, half, tile_rows, width).astype(jnp.bfloat16)
        return carry

    lax.fori_loop(0, tile_count // 2 // GROUP, body, 0)


def pack_specs(rows):
    return [pl.BlockSpec((None, rows, HEAD_DIM), lambda h, which=which: (which, 0, h)) for which in range(3)]


def forward(place, tile_pairs, lens, packs):
    _, rows, local_width = packs[0].shape
    heads = local_width // HEAD_DIM
    clip_rows = rows * SEQ
    pairs = tile_pairs.shape[0] // 2
    depth = tile_pairs.shape[1] * (clip_rows // tile_pairs.shape[0])
    return pl.pallas_call(
        forward_kernel,
        grid=(heads,),
        in_specs=[smem()] * 3 + [spec for spec in pack_specs(rows) for _ in packs],
        out_specs=[
            pl.BlockSpec((clip_rows, HEAD_DIM), lambda h: (0, h)),
            pl.BlockSpec((1, pairs * depth, HEAD_DIM), lambda h: (h, 0, 0)),
        ],
        out_shape=[
            jax.ShapeDtypeStruct((clip_rows, local_width), jnp.bfloat16),
            jax.ShapeDtypeStruct((heads, pairs * depth, HEAD_DIM), jnp.bfloat16),
        ],
        scratch_shapes=[pltpu.VMEM((clip_rows, HEAD_DIM), jnp.bfloat16)] * 3,
        compiler_params=params(),
        name="attention_forward",
    )(place, tile_pairs, lens, *packs, *packs, *packs)


def backward_kernel(place_ref, pairs_ref, *refs):
    q_parts, k_parts, v_parts = refs[:SEQ], refs[SEQ : 2 * SEQ], refs[2 * SEQ : 3 * SEQ]
    own_grads, other_grads = refs[3 * SEQ : 4 * SEQ], refs[4 * SEQ : 5 * SEQ]
    probs_ref = refs[5 * SEQ]
    outs = refs[5 * SEQ + 1 : 6 * SEQ + 1]
    q_all, k_all, v_all, g_all, gq_all, gk_acc, gv_acc = refs[6 * SEQ + 1 :]
    tile_count, neighbours = pairs_ref.shape
    clip_rows, width = q_all.shape
    tile_rows = clip_rows // tile_count
    rows = 2 * tile_rows
    depth = neighbours * tile_rows
    factor = 1.0 / math.sqrt(width)
    load_parts(q_parts, q_all)
    load_parts(k_parts, k_all)
    load_parts(v_parts, v_all)
    half_rows = own_grads[0].shape[0]
    core = place_ref[1]
    for at in range(SEQ):
        for grads, half in ((own_grads[at], core), (other_grads[at ^ 1], 1 - core)):
            g_all[pl.ds(pl.multiple_of((2 * at + half) * half_rows, half_rows), half_rows), :] = grads[...]
    gk_acc[...] = jnp.zeros_like(gk_acc)
    gv_acc[...] = jnp.zeros_like(gv_acc)

    def rows_of(pair):
        return pl.ds(pl.multiple_of(pair * rows, rows), rows)

    def body(group, carry):
        pairs = [group * GROUP + at for at in range(GROUP)]
        nears = [near_of(place_ref, pairs_ref, pair) for pair in pairs]
        probs = [
            probs_ref[0, pl.ds(pl.multiple_of(pair * depth, depth), depth), :] for pair in pairs
        ]
        grads = [spread(g_all[rows_of(pair), :], tile_rows) for pair in pairs]
        grad_scores = []
        for prob, grad, near in zip(probs, grads, nears):
            grad_prob = contract(gather_pair(v_all, near, tile_rows), grad, 1, 1)
            wide = prob.astype(jnp.float32)
            delta = jnp.sum(wide * grad_prob, axis=0, keepdims=True)
            grad_scores.append((wide * (grad_prob - delta)).astype(jnp.bfloat16))
        grad_queries = [
            contract(grad_score, gather_pair(k_all, near, tile_rows), 0, 0) * factor
            for grad_score, near in zip(grad_scores, nears)
        ]
        grad_keys = [
            contract(grad_score, spread(q_all[rows_of(pair), :], tile_rows), 1, 0)
            for grad_score, pair in zip(grad_scores, pairs)
        ]
        grad_vals = [contract(prob, grad, 1, 0) for prob, grad in zip(probs, grads)]
        for pair, near, grad_query, grad_key, grad_val in zip(
            pairs, nears, grad_queries, grad_keys, grad_vals
        ):
            for half in range(2):
                place = pl.ds(pl.multiple_of((2 * pair + half) * tile_rows, tile_rows), tile_rows)
                gq_all[place, :] = diagonal(grad_query, half, tile_rows, width).astype(jnp.bfloat16)
                for n in range(neighbours):
                    at = (slice(n * tile_rows, (n + 1) * tile_rows), slice(half * width, (half + 1) * width))
                    place = pl.ds(pl.multiple_of(near[half][n] * tile_rows, tile_rows), tile_rows)
                    gk_acc[place, :] += grad_key[at]
                    gv_acc[place, :] += grad_val[at]
        return carry

    lax.fori_loop(0, tile_count // 2 // GROUP, body, 0)
    for at, out in enumerate(outs):
        part = slice(at * out.shape[1], (at + 1) * out.shape[1])
        out[0] = gq_all[part, :]
        out[1] = (gk_acc[part, :] * factor).astype(jnp.bfloat16)
        out[2] = gv_acc[part, :].astype(jnp.bfloat16)


def backward(place, tile_pairs, packs, own_grads, other_grads, probs):
    _, rows, local_width = packs[0].shape
    heads = local_width // HEAD_DIM
    clip_rows = rows * SEQ
    grad_spec = pl.BlockSpec((own_grads[0].shape[0], HEAD_DIM), lambda h: (0, h))
    bf16_rows = pltpu.VMEM((clip_rows, HEAD_DIM), jnp.bfloat16)
    f32_rows = pltpu.VMEM((clip_rows, HEAD_DIM), jnp.float32)
    return pl.pallas_call(
        backward_kernel,
        grid=(heads,),
        in_specs=[smem()] * 2
        + [spec for spec in pack_specs(rows) for _ in packs]
        + [grad_spec] * (2 * SEQ)
        + [pl.BlockSpec((1,) + probs.shape[1:], lambda h: (h, 0, 0))],
        out_specs=[pl.BlockSpec((3, rows, HEAD_DIM), lambda h: (0, 0, h))] * SEQ,
        out_shape=[jax.ShapeDtypeStruct((3, rows, local_width), jnp.bfloat16)] * SEQ,
        scratch_shapes=[bf16_rows] * 5 + [f32_rows] * 2,
        compiler_params=params(),
        name="attention_backward",
    )(place, tile_pairs, *packs, *packs, *packs, *own_grads, *other_grads, probs)


def weight_grad_kernel(place_ref, mean, att_ref, *refs):
    own, other, outs = refs[:SEQ], refs[SEQ : 2 * SEQ], refs[2 * SEQ :]
    half_rows = own[0].shape[0]
    core = place_ref[1]
    columns, attended = [], []
    for at in range(SEQ):
        for part, half in ((own[at], core), (other[at ^ 1], 1 - core)):
            columns.append(part[...])
            start = pl.multiple_of((2 * at + half) * half_rows, half_rows)
            attended.append(att_ref[pl.ds(start, half_rows), :])
    total = contract(jnp.concatenate(columns, axis=0), jnp.concatenate(attended, axis=0), 0, 0)
    total = (total * mean).astype(jnp.bfloat16)
    count, piece = outs[0].shape[:2]
    for at in range(count):
        for holder, out in enumerate(outs):
            start = (2 * at + holder) * piece
            out[at] = total[start : start + piece]


def weight_grad(place, attended, own, other, mean, owners, block=640):
    half_rows, features = own[0].shape
    local_width = attended.shape[1]
    piece = features // owners // CORES
    return pl.pallas_call(
        lambda place_ref, *refs: weight_grad_kernel(place_ref, mean, *refs),
        grid=(features // block,),
        in_specs=[smem(), pl.BlockSpec(attended.shape, lambda i: (0, 0))]
        + [pl.BlockSpec((half_rows, block), lambda i: (0, i))] * (2 * SEQ),
        out_specs=[pl.BlockSpec((block // piece // 2, piece, local_width), lambda i: (i, 0, 0))] * CORES,
        out_shape=[jax.ShapeDtypeStruct((owners, piece, local_width), jnp.bfloat16)] * CORES,
        compiler_params=params(),
        name="weight_grad",
    )(place, attended, *own, *other)


def device_of(core, seq):
    return core * SEQ + seq


def outward(round_):
    pairs = []
    for core in range(CORES):
        for token in range(SEQ):
            shard = token ^ round_
            pairs.append((device_of(core, token), device_of(shard % 2, 2 * core + shard // 2)))
    return pairs


def inward(round_):
    return [(target, source) for source, target in outward(round_)]


def send(value, pairs):
    return lax.ppermute(value, ("core", "seq"), pairs)


def swap_cores(value):
    return lax.ppermute(value, "core", [(0, 1), (1, 0)])


def shift(value, axis, by):
    count = lax.axis_size(axis)
    return lax.ppermute(value, axis, [(i, (i + by) % count) for i in range(count)])


def add(*terms):
    total = terms[0].astype(jnp.float32)
    for term in terms[1:]:
        total = total + term.astype(jnp.float32)
    return total.astype(jnp.bfloat16)


def take(value, index, axis=0):
    return lax.dynamic_index_in_dim(value, index, axis, keepdims=False)


def scatter(value, axis, dim=0):
    here = lax.axis_index(axis)
    count = lax.axis_size(axis)
    got = [shift(take(value, (here + by) % count, dim), axis, by) for by in (2, 1, 3)]
    return [take(value, here, dim)] + got


def to_shard_holders(w_out, core, seq):
    got = []
    for other in range(2):
        pairs = []
        for holder in range(CORES):
            for shard in range(SEQ):
                window = holder ^ other
                pairs.append((device_of(holder, shard), device_of(shard % 2, shard // 2 + 2 * window)))
        got.append(send(w_out, pairs))
    window = seq // 2
    return jnp.where(window == 0, jnp.concatenate(got), jnp.concatenate(got[::-1]))


def to_owners(totals, seq):
    window = seq // 2
    got = []
    for other in range(2):
        pairs = []
        for core in range(CORES):
            for at in range(SEQ):
                holder = (at // 2) ^ other
                pairs.append((device_of(core, at), device_of(holder, 2 * (at % 2) + core)))
        got.append(send(jnp.where((window ^ other) == 0, totals[0], totals[1]), pairs))
    return got[0].astype(jnp.float32) + got[1].astype(jnp.float32)


def after(values, *tokens):
    return lax.optimization_barrier((values, tokens))[0]


def per_device(queries, keys, values, gain_q, gain_k, tile_pairs, tile_lens, out_grad, w_out):
    core = lax.axis_index("core")
    seq = lax.axis_index("seq")
    count_z = lax.axis_size("z")
    count_x = lax.axis_size("x")
    rows, features = out_grad.shape
    shard = 2 * (seq % 2) + core
    tiles_per_block = tile_pairs.shape[0] // SEQ
    place = jnp.stack([seq, core, shard, shard * tiles_per_block]).astype(jnp.int32)
    lens = jnp.where(seq // 2 == core, tile_lens, swap_cores(tile_lens))

    def half_rows(rows_in, round_):
        half = seq % 2 if round_ % 2 == 0 else 1 - seq % 2
        return take(rows_in.reshape(2, rows // 2, features), half)

    own = [send(half_rows(out_grad, 0), outward(0))]
    packs = to_rounds(place, queries, keys, values, gain_q, gain_k)
    packs = [send(part, outward(r)) for r, part in enumerate(packs)]
    ready = (packs[0], packs[1], packs[2:])
    own += [send(half_rows(after(out_grad, ready[r - 1]), r), outward(r)) for r in range(1, SEQ)]
    other = [swap_cores(part) for part in own]
    w_all = lax.all_gather(to_shard_holders(w_out, core, seq), ("z", "x"), axis=0, tiled=True)

    def project(part):
        return jnp.dot(part, w_all, preferred_element_type=jnp.float32).astype(jnp.bfloat16)

    attended, probs = forward(place, tile_pairs, lens, packs)
    own_grads = [project(part) for part in own]
    other_grads = [project(part) for part in other]
    attended = after(attended, own_grads[:-1], other_grads[:-1])
    one, two = weight_grad(
        place, attended, own, other, 1.0 / (count_z * count_x * CORES), count_z * count_x
    )
    two = lax.psum_scatter(two, ("z", "x"), scatter_dimension=0, tiled=True)[0]
    one = scatter(one.reshape((count_z, count_x) + one.shape[1:]), "x", 1)
    parts = backward(place, tile_pairs, packs, own_grads, other_grads, after(probs, one[0]))
    token = parts[0]
    parts = [send(part, inward(r)) for r, part in enumerate(parts)]
    one = add(*after(one, token))
    one = add(*scatter(after(one, parts[0], parts[1]), "z"))
    grad_w = to_owners((one, two), seq)
    grad_q, grad_k, grad_v = finish(place, queries, keys, gain_q, gain_k, parts)
    return (grad_q, grad_k, grad_v, grad_w)


def solution(mesh):
    dp = mesh.shape["dp"]
    side = math.isqrt(dp // CORES)
    parts = Mesh(mesh.devices.reshape(side, side, CORES, SEQ), ("z", "x", "core", "seq"))
    dp_axes = ("z", "x", "core")
    tokens = P(dp_axes + ("seq",), None)
    return jax.shard_map(
        per_device,
        mesh=parts,
        in_specs=(tokens, tokens, tokens, P(), P(), P(), P(dp_axes, None), tokens, P(dp_axes, "seq")),
        out_specs=(tokens, tokens, tokens, P(dp_axes, "seq")),
        check_vma=False,
    )
```

```python
import functools
import math

import jax
import jax.numpy as jnp
from jax import lax
from jax.experimental import pallas as pl
from jax.experimental.pallas import tpu as pltpu
from jax.sharding import Mesh, PartitionSpec as P

HEAD_DIM = 128


EPS = 1e-06
LOG2E = 1.4426950408889634
MIN_LIVE = 40
SEQ = 4
CORES = 2
GROUP = 4


def smem():
    return pl.BlockSpec(memory_space=pltpu.SMEM)


def params():
    return pltpu.CompilerParams(vmem_limit_bytes=48 << 20)


def contract(left, right, left_dim, right_dim):
    return lax.dot_general(
        left, right, (((left_dim,), (right_dim,)), ((), ())), preferred_element_type=jnp.float32
    )


def row_scale_of(values_f):
    return lax.rsqrt(jnp.mean(values_f * values_f, axis=-1, keepdims=True) + EPS)


def shard_of(place_ref, round_, width):
    return pl.ds(pl.multiple_of(jnp.bitwise_xor(place_ref[0], round_) * width, 128), width)


def rounds_kernel(place_ref, q_ref, k_ref, v_ref, gain_q_ref, gain_k_ref, *refs):
    outs, normed = refs[:-1], refs[-1]
    for at, (x_ref, gain_ref) in enumerate(((q_ref, gain_q_ref), (k_ref, gain_k_ref))):
        values_f = x_ref[...].astype(jnp.float32)
        normed[at] = (values_f * row_scale_of(values_f) * gain_ref[...]).astype(jnp.bfloat16)
    for round_, out in enumerate(outs):
        columns = shard_of(place_ref, round_, out.shape[2])
        out[0] = normed[0, :, columns]
        out[1] = normed[1, :, columns]
        out[2] = v_ref[:, columns]


def to_rounds(place, queries, keys, values, gain_q, gain_k, block=64):
    rows, width = queries.shape
    row_spec = pl.BlockSpec((block, width), lambda i: (i, 0))
    gain_spec = pl.BlockSpec((1, width), lambda i: (0, 0))
    return pl.pallas_call(
        rounds_kernel,
        grid=(rows // block,),
        in_specs=[smem()] + [row_spec] * 3 + [gain_spec] * 2,
        out_specs=[pl.BlockSpec((3, block, width // SEQ), lambda i: (0, i, 0))] * SEQ,
        out_shape=[jax.ShapeDtypeStruct((3, rows, width // SEQ), jnp.bfloat16)] * SEQ,
        scratch_shapes=[pltpu.VMEM((2, block, width), jnp.bfloat16)],
        name="norm_rows",
    )(place, queries, keys, values, gain_q.reshape(1, width), gain_k.reshape(1, width))


def finish_kernel(place_ref, q_ref, k_ref, gain_q_ref, gain_k_ref, *refs):
    parts, outs, joined = refs[:SEQ], refs[SEQ:-1], refs[-1]
    width = q_ref.shape[1]
    for round_, part in enumerate(parts):
        columns = shard_of(place_ref, round_, part.shape[2])
        joined[0, :, columns] = part[0]
        joined[1, :, columns] = part[1]
        outs[2][:, columns] = part[2]
    for at, (x_ref, gain_ref) in enumerate(((q_ref, gain_q_ref), (k_ref, gain_k_ref))):
        values_f = x_ref[...].astype(jnp.float32)
        row_scale = row_scale_of(values_f)
        gated = gain_ref[...] * joined[at].astype(jnp.float32)
        inner = jnp.sum(gated * values_f, axis=-1, keepdims=True)
        back = values_f * (row_scale * row_scale * row_scale * inner * (1.0 / width))
        outs[at][...] = (row_scale * gated - back).astype(jnp.bfloat16)


def finish(place, queries, keys, gain_q, gain_k, parts, block=64):
    rows, width = queries.shape
    row_spec = pl.BlockSpec((block, width), lambda i: (i, 0))
    gain_spec = pl.BlockSpec((1, width), lambda i: (0, 0))
    return pl.pallas_call(
        finish_kernel,
        grid=(rows // block,),
        in_specs=[smem()]
        + [row_spec] * 2
        + [gain_spec] * 2
        + [pl.BlockSpec((3, block, width // SEQ), lambda i: (0, i, 0))] * SEQ,
        out_specs=[row_spec] * 3,
        out_shape=[jax.ShapeDtypeStruct((rows, width), jnp.bfloat16)] * 3,
        scratch_shapes=[pltpu.VMEM((2, block, width), jnp.bfloat16)],
        name="norm_back",
    )(place, queries, keys, gain_q.reshape(1, width), gain_k.reshape(1, width), *parts)


def tile_at(ref, index, rows):
    return ref[pl.ds(pl.multiple_of(index * rows, rows), rows), :]


def gather_pair(ref, near, rows):
    return jnp.concatenate(
        [
            jnp.concatenate([tile_at(ref, one, rows), tile_at(ref, two, rows)], axis=1)
            for one, two in zip(*near)
        ],
        axis=0,
    )


def spread(block, rows):
    twice = jnp.concatenate([block, block], axis=1)
    width = block.shape[1]
    own = (lax.broadcasted_iota(jnp.int32, twice.shape, 0) < rows) == (
        lax.broadcasted_iota(jnp.int32, twice.shape, 1) < width
    )
    return jnp.where(own, twice, jnp.zeros_like(twice))


def near_of(place_ref, pairs_ref, pair):
    flip = place_ref[3]
    return [
        [
            jnp.bitwise_xor(pairs_ref[jnp.bitwise_xor(2 * pair + half, flip), n], flip)
            for n in range(pairs_ref.shape[1])
        ]
        for half in range(2)
    ]


def load_parts(parts, whole):
    for at, part in enumerate(parts):
        whole[at * part.shape[0] : (at + 1) * part.shape[0], :] = part[...]


def diagonal(product, half, tile_rows, width):
    return product[half * tile_rows : (half + 1) * tile_rows, half * width : (half + 1) * width]


def forward_kernel(place_ref, pairs_ref, lens_ref, *refs):
    q_parts, k_parts, v_parts = refs[:SEQ], refs[SEQ : 2 * SEQ], refs[2 * SEQ : 3 * SEQ]
    att_ref, probs_ref, q_all, k_all, v_all = refs[3 * SEQ :]
    tile_count, neighbours = pairs_ref.shape
    clip_rows, width = q_all.shape
    tile_rows = clip_rows // tile_count
    rows = 2 * tile_rows
    depth = neighbours * tile_rows
    scale = LOG2E / math.sqrt(width)
    load_parts(q_parts, q_all)
    load_parts(k_parts, k_all)
    load_parts(v_parts, v_all)
    shape = (tile_rows - MIN_LIVE, rows)
    first = lax.broadcasted_iota(jnp.int32, shape, 1) < tile_rows
    slot = lax.broadcasted_iota(jnp.int32, shape, 0) + MIN_LIVE

    def length(tile):
        return lens_ref[0, jnp.bitwise_xor(tile, place_ref[3])]

    def score(pair, near):
        keys = gather_pair(k_all, near, tile_rows)
        queries = spread(q_all[pl.ds(pl.multiple_of(pair * rows, rows), rows), :], tile_rows)
        scores = contract(keys, queries, 1, 1)
        pieces = []
        for n in range(neighbours):
            start = n * tile_rows
            pieces.append(scores[start : start + MIN_LIVE])
            live = slot < jnp.where(first, length(near[0][n]), length(near[1][n]))
            pieces.append(jnp.where(live, scores[start + MIN_LIVE : start + tile_rows], -jnp.inf))
        return jnp.concatenate(pieces, axis=0)

    def soften(scores):
        weights = jnp.exp2((scores - jnp.max(scores, axis=0, keepdims=True)) * scale)
        return (weights * (1.0 / jnp.sum(weights, axis=0, keepdims=True))).astype(jnp.bfloat16)

    def body(group, carry):
        pairs = [group * GROUP + at for at in range(GROUP)]
        nears = [near_of(place_ref, pairs_ref, pair) for pair in pairs]
        probs = [soften(score(pair, near)) for pair, near in zip(pairs, nears)]
        attended = [
            contract(prob, gather_pair(v_all, near, tile_rows), 0, 0) for prob, near in zip(probs, nears)
        ]
        for pair, prob, product in zip(pairs, probs, attended):
            probs_ref[0, pl.ds(pl.multiple_of(pair * depth, depth), depth), :] = prob
            for half in range(2):
                place = pl.ds(pl.multiple_of((2 * pair + half) * tile_rows, tile_rows), tile_rows)
                att_ref[place, :] = diagonal(product, half, tile_rows, width).astype(jnp.bfloat16)
        return carry

    lax.fori_loop(0, tile_count // 2 // GROUP, body, 0)


def pack_specs(rows):
    return [pl.BlockSpec((None, rows, HEAD_DIM), lambda h, which=which: (which, 0, h)) for which in range(3)]


def forward(place, tile_pairs, lens, packs):
    _, rows, local_width = packs[0].shape
    heads = local_width // HEAD_DIM
    clip_rows = rows * SEQ
    pairs = tile_pairs.shape[0] // 2
    depth = tile_pairs.shape[1] * (clip_rows // tile_pairs.shape[0])
    return pl.pallas_call(
        forward_kernel,
        grid=(heads,),
        in_specs=[smem()] * 3 + [spec for spec in pack_specs(rows) for _ in packs],
        out_specs=[
            pl.BlockSpec((clip_rows, HEAD_DIM), lambda h: (0, h)),
            pl.BlockSpec((1, pairs * depth, HEAD_DIM), lambda h: (h, 0, 0)),
        ],
        out_shape=[
            jax.ShapeDtypeStruct((clip_rows, local_width), jnp.bfloat16),
            jax.ShapeDtypeStruct((heads, pairs * depth, HEAD_DIM), jnp.bfloat16),
        ],
        scratch_shapes=[pltpu.VMEM((clip_rows, HEAD_DIM), jnp.bfloat16)] * 3,
        compiler_params=params(),
        name="attention_forward",
    )(place, tile_pairs, lens, *packs, *packs, *packs)


def backward_kernel(place_ref, pairs_ref, *refs):
    q_parts, k_parts, v_parts = refs[:SEQ], refs[SEQ : 2 * SEQ], refs[2 * SEQ : 3 * SEQ]
    own_grads, other_grads = refs[3 * SEQ : 4 * SEQ], refs[4 * SEQ : 5 * SEQ]
    probs_ref = refs[5 * SEQ]
    outs = refs[5 * SEQ + 1 : 6 * SEQ + 1]
    q_all, k_all, v_all, g_all, gq_all, gk_acc, gv_acc = refs[6 * SEQ + 1 :]
    tile_count, neighbours = pairs_ref.shape
    clip_rows, width = q_all.shape
    tile_rows = clip_rows // tile_count
    rows = 2 * tile_rows
    depth = neighbours * tile_rows
    factor = 1.0 / math.sqrt(width)
    load_parts(q_parts, q_all)
    load_parts(k_parts, k_all)
    load_parts(v_parts, v_all)
    half_rows = own_grads[0].shape[0]
    core = place_ref[1]
    for at in range(SEQ):
        for grads, half in ((own_grads[at], core), (other_grads[at ^ 1], 1 - core)):
            g_all[pl.ds(pl.multiple_of((2 * at + half) * half_rows, half_rows), half_rows), :] = grads[...]
    gk_acc[...] = jnp.zeros_like(gk_acc)
    gv_acc[...] = jnp.zeros_like(gv_acc)

    def rows_of(pair):
        return pl.ds(pl.multiple_of(pair * rows, rows), rows)

    def body(group, carry):
        pairs = [group * GROUP + at for at in range(GROUP)]
        nears = [near_of(place_ref, pairs_ref, pair) for pair in pairs]
        probs = [
            probs_ref[0, pl.ds(pl.multiple_of(pair * depth, depth), depth), :] for pair in pairs
        ]
        grads = [spread(g_all[rows_of(pair), :], tile_rows) for pair in pairs]
        grad_scores = []
        for prob, grad, near in zip(probs, grads, nears):
            grad_prob = contract(gather_pair(v_all, near, tile_rows), grad, 1, 1)
            wide = prob.astype(jnp.float32)
            delta = jnp.sum(wide * grad_prob, axis=0, keepdims=True)
            grad_scores.append((wide * (grad_prob - delta)).astype(jnp.bfloat16))
        grad_queries = [
            contract(grad_score, gather_pair(k_all, near, tile_rows), 0, 0) * factor
            for grad_score, near in zip(grad_scores, nears)
        ]
        grad_keys = [
            contract(grad_score, spread(q_all[rows_of(pair), :], tile_rows), 1, 0)
            for grad_score, pair in zip(grad_scores, pairs)
        ]
        grad_vals = [contract(prob, grad, 1, 0) for prob, grad in zip(probs, grads)]
        for pair, near, grad_query, grad_key, grad_val in zip(
            pairs, nears, grad_queries, grad_keys, grad_vals
        ):
            for half in range(2):
                place = pl.ds(pl.multiple_of((2 * pair + half) * tile_rows, tile_rows), tile_rows)
                gq_all[place, :] = diagonal(grad_query, half, tile_rows, width).astype(jnp.bfloat16)
                for n in range(neighbours):
                    at = (slice(n * tile_rows, (n + 1) * tile_rows), slice(half * width, (half + 1) * width))
                    place = pl.ds(pl.multiple_of(near[half][n] * tile_rows, tile_rows), tile_rows)
                    gk_acc[place, :] += grad_key[at]
                    gv_acc[place, :] += grad_val[at]
        return carry

    lax.fori_loop(0, tile_count // 2 // GROUP, body, 0)
    for at, out in enumerate(outs):
        part = slice(at * out.shape[1], (at + 1) * out.shape[1])
        out[0] = gq_all[part, :]
        out[1] = (gk_acc[part, :] * factor).astype(jnp.bfloat16)
        out[2] = gv_acc[part, :].astype(jnp.bfloat16)


def backward(place, tile_pairs, packs, own_grads, other_grads, probs):
    _, rows, local_width = packs[0].shape
    heads = local_width // HEAD_DIM
    clip_rows = rows * SEQ
    grad_spec = pl.BlockSpec((own_grads[0].shape[0], HEAD_DIM), lambda h: (0, h))
    bf16_rows = pltpu.VMEM((clip_rows, HEAD_DIM), jnp.bfloat16)
    f32_rows = pltpu.VMEM((clip_rows, HEAD_DIM), jnp.float32)
    return pl.pallas_call(
        backward_kernel,
        grid=(heads,),
        in_specs=[smem()] * 2
        + [spec for spec in pack_specs(rows) for _ in packs]
        + [grad_spec] * (2 * SEQ)
        + [pl.BlockSpec((1,) + probs.shape[1:], lambda h: (h, 0, 0))],
        out_specs=[pl.BlockSpec((3, rows, HEAD_DIM), lambda h: (0, 0, h))] * SEQ,
        out_shape=[jax.ShapeDtypeStruct((3, rows, local_width), jnp.bfloat16)] * SEQ,
        scratch_shapes=[bf16_rows] * 5 + [f32_rows] * 2,
        compiler_params=params(),
        name="attention_backward",
    )(place, tile_pairs, *packs, *packs, *packs, *own_grads, *other_grads, probs)


def weight_grad_kernel(place_ref, mean, side, att_ref, *refs):
    own, other, outs = refs[:SEQ], refs[SEQ : 2 * SEQ], refs[2 * SEQ :]
    pieces, second = outs[:-1], outs[-1]
    half_rows = own[0].shape[0]
    core = place_ref[1]
    columns, attended = [], []
    for at in range(SEQ):
        for part, half in ((own[at], core), (other[at ^ 1], 1 - core)):
            columns.append(part[...])
            start = pl.multiple_of((2 * at + half) * half_rows, half_rows)
            attended.append(att_ref[pl.ds(start, half_rows), :])
    total = contract(jnp.concatenate(columns, axis=0), jnp.concatenate(attended, axis=0), 0, 0)
    total = (total * mean).astype(jnp.bfloat16)
    count, piece = second.shape[:2]
    step = pl.program_id(0)
    for at in range(count):
        start = 2 * at * piece
        second[at] = total[start + piece : start + 2 * piece]
        owner = step * count + at
        ahead = lax.rem(owner + side - place_ref[4], side)
        for by, out in enumerate(pieces):

            @pl.when(ahead == by)
            def _(out=out, start=start, owner=owner):
                out[owner // side] = total[start : start + piece]


def weight_grad(place, attended, own, other, mean, side, block=640):
    half_rows, features = own[0].shape
    local_width = attended.shape[1]
    piece = features // (side * side) // CORES
    return pl.pallas_call(
        lambda place_ref, *refs: weight_grad_kernel(place_ref, mean, side, *refs),
        grid=(features // block,),
        in_specs=[smem(), pl.BlockSpec(attended.shape, lambda i: (0, 0))]
        + [pl.BlockSpec((half_rows, block), lambda i: (0, i))] * (2 * SEQ),
        out_specs=[pl.BlockSpec((side, piece, local_width), lambda i: (0, 0, 0))] * side
        + [pl.BlockSpec((block // piece // 2, piece, local_width), lambda i: (i, 0, 0))],
        out_shape=[jax.ShapeDtypeStruct((side, piece, local_width), jnp.bfloat16)] * side
        + [jax.ShapeDtypeStruct((side * side, piece, local_width), jnp.bfloat16)],
        compiler_params=params(),
        name="weight_grad",
    )(place, attended, *own, *other)


def device_of(core, seq):
    return core * SEQ + seq


def outward(round_):
    pairs = []
    for core in range(CORES):
        for token in range(SEQ):
            shard = token ^ round_
            pairs.append((device_of(core, token), device_of(shard % 2, 2 * core + shard // 2)))
    return pairs


def inward(round_):
    return [(target, source) for source, target in outward(round_)]


def send(value, pairs):
    return lax.ppermute(value, ("core", "seq"), pairs)


def swap_cores(value):
    return lax.ppermute(value, "core", [(0, 1), (1, 0)])


def shift(value, axis, by):
    count = lax.axis_size(axis)
    return lax.ppermute(value, axis, [(i, (i + by) % count) for i in range(count)])


def add(*terms):
    total = terms[0].astype(jnp.float32)
    for term in terms[1:]:
        total = total + term.astype(jnp.float32)
    return total.astype(jnp.bfloat16)


def take(value, index, axis=0):
    return lax.dynamic_index_in_dim(value, index, axis, keepdims=False)


def scatter(value, axis, dim=0):
    here = lax.axis_index(axis)
    count = lax.axis_size(axis)
    got = [shift(take(value, (here + by) % count, dim), axis, by) for by in (2, 1, 3)]
    return [take(value, here, dim)] + got


def to_shard_holders(w_out, core, seq):
    got = []
    for other in range(2):
        pairs = []
        for holder in range(CORES):
            for shard in range(SEQ):
                window = holder ^ other
                pairs.append((device_of(holder, shard), device_of(shard % 2, shard // 2 + 2 * window)))
        got.append(send(w_out, pairs))
    window = seq // 2
    return jnp.where(window == 0, jnp.concatenate(got), jnp.concatenate(got[::-1]))


def to_owners(totals, seq):
    window = seq // 2
    got = []
    for other in range(2):
        pairs = []
        for core in range(CORES):
            for at in range(SEQ):
                holder = (at // 2) ^ other
                pairs.append((device_of(core, at), device_of(holder, 2 * (at % 2) + core)))
        got.append(send(jnp.where((window ^ other) == 0, totals[0], totals[1]), pairs))
    return got[0].astype(jnp.float32) + got[1].astype(jnp.float32)


def after(values, *tokens):
    return lax.optimization_barrier((values, tokens))[0]


def per_device(queries, keys, values, gain_q, gain_k, tile_pairs, tile_lens, out_grad, w_out):
    core = lax.axis_index("core")
    seq = lax.axis_index("seq")
    count_z = lax.axis_size("z")
    count_x = lax.axis_size("x")
    rows, features = out_grad.shape
    shard = 2 * (seq % 2) + core
    tiles_per_block = tile_pairs.shape[0] // SEQ
    place = jnp.stack([seq, core, shard, shard * tiles_per_block, lax.axis_index("x")]).astype(jnp.int32)
    lens = jnp.where(seq // 2 == core, tile_lens, swap_cores(tile_lens))

    def half_rows(rows_in, round_):
        half = seq % 2 if round_ % 2 == 0 else 1 - seq % 2
        return take(rows_in.reshape(2, rows // 2, features), half)

    own = [send(half_rows(out_grad, 0), outward(0))]
    packs = to_rounds(place, queries, keys, values, gain_q, gain_k)
    w_out = after(w_out, packs[0])
    packs = [send(after(part, own[0]) if r == 3 else part, outward(r)) for r, part in enumerate(packs)]
    ready = (packs[0], packs[1], packs[2:])
    own += [send(half_rows(after(out_grad, ready[r - 1]), r), outward(r)) for r in range(1, SEQ)]
    w_all = lax.all_gather(to_shard_holders(w_out, core, seq), ("z", "x"), axis=0, tiled=True)

    def project(part):
        return jnp.dot(part, w_all, preferred_element_type=jnp.float32).astype(jnp.bfloat16)

    attended, probs = forward(place, tile_pairs, lens, packs)
    other = [swap_cores(after(part, attended) if r == 2 else part) for r, part in enumerate(own[:-1])]
    own_grads = [project(part) for part in own[:-1]]
    other_grads = [project(part) for part in other]
    other.append(swap_cores(after(own[-1], own_grads, other_grads[:-1])))
    attended = after(attended, own_grads, other_grads)
    own_grads.append(project(own[-1]))
    other_grads.append(project(other[-1]))
    *one, two = weight_grad(place, attended, own, other, 1.0 / (count_z * count_x * CORES), count_x)
    two = lax.psum_scatter(two, "z", scatter_dimension=0, tiled=True)
    token = one[0]
    one = [one[0]] + [shift(one[by], "x", by) for by in (2, 1, 3)]
    parts = backward(place, tile_pairs, packs, own_grads, other_grads, after(probs, token))
    token = parts[0]
    parts = {r: send(parts[r], inward(r)) for r in (0, 2, 1, 3)}
    one = add(*after(one, token))
    one = add(*scatter(after(one, parts[0], parts[2]), "z"))
    two = add(*scatter(after(two, parts[0], parts[2]), "x"))
    grad_w = to_owners((one, two), seq)
    grad_q, grad_k, grad_v = finish(place, queries, keys, gain_q, gain_k, [parts[r] for r in range(SEQ)])
    return (grad_q, grad_k, grad_v, grad_w)


def solution(mesh):
    dp = mesh.shape["dp"]
    side = math.isqrt(dp // CORES)
    parts = Mesh(mesh.devices.reshape(side, side, CORES, SEQ), ("z", "x", "core", "seq"))
    dp_axes = ("z", "x", "core")
    tokens = P(dp_axes + ("seq",), None)
    return jax.shard_map(
        per_device,
        mesh=parts,
        in_specs=(tokens, tokens, tokens, P(), P(), P(), P(dp_axes, None), tokens, P(dp_axes, "seq")),
        out_specs=(tokens, tokens, tokens, P(dp_axes, "seq")),
        check_vma=False,
    )
```

```python
import functools
import math

import jax
import jax.numpy as jnp
from jax import lax
from jax.experimental import pallas as pl
from jax.experimental.pallas import tpu as pltpu
from jax.sharding import Mesh, PartitionSpec as P

HEAD_DIM = 128


EPS = 1e-06
LOG2E = 1.4426950408889634
MIN_LIVE = 40
SEQ = 4
CORES = 2
GROUP = 4
ORDER = (0, 3, 1, 2)


def smem():
    return pl.BlockSpec(memory_space=pltpu.SMEM)


def params():
    return pltpu.CompilerParams(vmem_limit_bytes=48 << 20)


def contract(left, right, left_dim, right_dim):
    return lax.dot_general(
        left, right, (((left_dim,), (right_dim,)), ((), ())), preferred_element_type=jnp.float32
    )


def row_scale_of(values_f):
    return lax.rsqrt(jnp.mean(values_f * values_f, axis=-1, keepdims=True) + EPS)


def shard_of(place_ref, round_, width):
    return pl.ds(pl.multiple_of(jnp.bitwise_xor(place_ref[0], round_) * width, 128), width)


def rounds_kernel(place_ref, q_ref, k_ref, v_ref, gain_q_ref, gain_k_ref, *refs):
    outs, normed = refs[:-1], refs[-1]
    for at, (x_ref, gain_ref) in enumerate(((q_ref, gain_q_ref), (k_ref, gain_k_ref))):
        values_f = x_ref[...].astype(jnp.float32)
        normed[at] = (values_f * row_scale_of(values_f) * gain_ref[...]).astype(jnp.bfloat16)
    for round_, out in enumerate(outs):
        columns = shard_of(place_ref, round_, out.shape[2])
        out[0] = normed[0, :, columns]
        out[1] = normed[1, :, columns]
        out[2] = v_ref[:, columns]


def to_rounds(place, queries, keys, values, gain_q, gain_k, block=64):
    rows, width = queries.shape
    row_spec = pl.BlockSpec((block, width), lambda i: (i, 0))
    gain_spec = pl.BlockSpec((1, width), lambda i: (0, 0))
    return pl.pallas_call(
        rounds_kernel,
        grid=(rows // block,),
        in_specs=[smem()] + [row_spec] * 3 + [gain_spec] * 2,
        out_specs=[pl.BlockSpec((3, block, width // SEQ), lambda i: (0, i, 0))] * SEQ,
        out_shape=[jax.ShapeDtypeStruct((3, rows, width // SEQ), jnp.bfloat16)] * SEQ,
        scratch_shapes=[pltpu.VMEM((2, block, width), jnp.bfloat16)],
        name="norm_rows",
    )(place, queries, keys, values, gain_q.reshape(1, width), gain_k.reshape(1, width))


def finish_kernel(place_ref, q_ref, k_ref, gain_q_ref, gain_k_ref, *refs):
    parts, outs, joined = refs[:SEQ], refs[SEQ:-1], refs[-1]
    width = q_ref.shape[1]
    for round_, part in enumerate(parts):
        columns = shard_of(place_ref, round_, part.shape[2])
        joined[0, :, columns] = part[0]
        joined[1, :, columns] = part[1]
        outs[2][:, columns] = part[2]
    for at, (x_ref, gain_ref) in enumerate(((q_ref, gain_q_ref), (k_ref, gain_k_ref))):
        values_f = x_ref[...].astype(jnp.float32)
        row_scale = row_scale_of(values_f)
        gated = gain_ref[...] * joined[at].astype(jnp.float32)
        inner = jnp.sum(gated * values_f, axis=-1, keepdims=True)
        back = values_f * (row_scale * row_scale * row_scale * inner * (1.0 / width))
        outs[at][...] = (row_scale * gated - back).astype(jnp.bfloat16)


def finish(place, queries, keys, gain_q, gain_k, parts, block=64):
    rows, width = queries.shape
    row_spec = pl.BlockSpec((block, width), lambda i: (i, 0))
    gain_spec = pl.BlockSpec((1, width), lambda i: (0, 0))
    return pl.pallas_call(
        finish_kernel,
        grid=(rows // block,),
        in_specs=[smem()]
        + [row_spec] * 2
        + [gain_spec] * 2
        + [pl.BlockSpec((3, block, width // SEQ), lambda i: (0, i, 0))] * SEQ,
        out_specs=[row_spec] * 3,
        out_shape=[jax.ShapeDtypeStruct((rows, width), jnp.bfloat16)] * 3,
        scratch_shapes=[pltpu.VMEM((2, block, width), jnp.bfloat16)],
        name="norm_back",
    )(place, queries, keys, gain_q.reshape(1, width), gain_k.reshape(1, width), *parts)


def tile_at(ref, index, rows):
    return ref[pl.ds(pl.multiple_of(index * rows, rows), rows), :]


def gather_pair(ref, near, rows):
    return jnp.concatenate(
        [
            jnp.concatenate([tile_at(ref, one, rows), tile_at(ref, two, rows)], axis=1)
            for one, two in zip(*near)
        ],
        axis=0,
    )


def spread(block, rows):
    twice = jnp.concatenate([block, block], axis=1)
    width = block.shape[1]
    own = (lax.broadcasted_iota(jnp.int32, twice.shape, 0) < rows) == (
        lax.broadcasted_iota(jnp.int32, twice.shape, 1) < width
    )
    return jnp.where(own, twice, jnp.zeros_like(twice))


def near_of(place_ref, pairs_ref, pair):
    flip = place_ref[3]
    return [
        [
            jnp.bitwise_xor(pairs_ref[jnp.bitwise_xor(2 * pair + half, flip), n], flip)
            for n in range(pairs_ref.shape[1])
        ]
        for half in range(2)
    ]


def load_parts(parts, whole):
    for at, part in enumerate(parts):
        whole[at * part.shape[0] : (at + 1) * part.shape[0], :] = part[...]


def diagonal(product, half, tile_rows, width):
    return product[half * tile_rows : (half + 1) * tile_rows, half * width : (half + 1) * width]


def forward_kernel(place_ref, pairs_ref, lens_ref, *refs):
    q_parts, k_parts, v_parts = refs[:SEQ], refs[SEQ : 2 * SEQ], refs[2 * SEQ : 3 * SEQ]
    att_ref, probs_ref, q_all, k_all, v_all = refs[3 * SEQ :]
    tile_count, neighbours = pairs_ref.shape
    clip_rows, width = q_all.shape
    tile_rows = clip_rows // tile_count
    rows = 2 * tile_rows
    depth = neighbours * tile_rows
    scale = LOG2E / math.sqrt(width)
    load_parts(q_parts, q_all)
    load_parts(k_parts, k_all)
    load_parts(v_parts, v_all)
    shape = (tile_rows - MIN_LIVE, rows)
    first = lax.broadcasted_iota(jnp.int32, shape, 1) < tile_rows
    slot = lax.broadcasted_iota(jnp.int32, shape, 0) + MIN_LIVE

    def length(tile):
        return lens_ref[0, jnp.bitwise_xor(tile, place_ref[3])]

    def score(pair, near):
        keys = gather_pair(k_all, near, tile_rows)
        queries = spread(q_all[pl.ds(pl.multiple_of(pair * rows, rows), rows), :], tile_rows)
        scores = contract(keys, queries, 1, 1)
        pieces = []
        for n in range(neighbours):
            start = n * tile_rows
            pieces.append(scores[start : start + MIN_LIVE])
            live = slot < jnp.where(first, length(near[0][n]), length(near[1][n]))
            pieces.append(jnp.where(live, scores[start + MIN_LIVE : start + tile_rows], -jnp.inf))
        return jnp.concatenate(pieces, axis=0)

    def soften(scores):
        weights = jnp.exp2((scores - jnp.max(scores, axis=0, keepdims=True)) * scale)
        return (weights * (1.0 / jnp.sum(weights, axis=0, keepdims=True))).astype(jnp.bfloat16)

    def body(group, carry):
        pairs = [group * GROUP + at for at in range(GROUP)]
        nears = [near_of(place_ref, pairs_ref, pair) for pair in pairs]
        probs = [soften(score(pair, near)) for pair, near in zip(pairs, nears)]
        attended = [
            contract(prob, gather_pair(v_all, near, tile_rows), 0, 0) for prob, near in zip(probs, nears)
        ]
        for pair, prob, product in zip(pairs, probs, attended):
            probs_ref[0, pl.ds(pl.multiple_of(pair * depth, depth), depth), :] = prob
            for half in range(2):
                place = pl.ds(pl.multiple_of((2 * pair + half) * tile_rows, tile_rows), tile_rows)
                att_ref[place, :] = diagonal(product, half, tile_rows, width).astype(jnp.bfloat16)
        return carry

    lax.fori_loop(0, tile_count // 2 // GROUP, body, 0)


def pack_specs(rows):
    return [pl.BlockSpec((None, rows, HEAD_DIM), lambda h, which=which: (which, 0, h)) for which in range(3)]


def forward(place, tile_pairs, lens, packs):
    _, rows, local_width = packs[0].shape
    heads = local_width // HEAD_DIM
    clip_rows = rows * SEQ
    pairs = tile_pairs.shape[0] // 2
    depth = tile_pairs.shape[1] * (clip_rows // tile_pairs.shape[0])
    return pl.pallas_call(
        forward_kernel,
        grid=(heads,),
        in_specs=[smem()] * 3 + [spec for spec in pack_specs(rows) for _ in packs],
        out_specs=[
            pl.BlockSpec((clip_rows, HEAD_DIM), lambda h: (0, h)),
            pl.BlockSpec((1, pairs * depth, HEAD_DIM), lambda h: (h, 0, 0)),
        ],
        out_shape=[
            jax.ShapeDtypeStruct((clip_rows, local_width), jnp.bfloat16),
            jax.ShapeDtypeStruct((heads, pairs * depth, HEAD_DIM), jnp.bfloat16),
        ],
        scratch_shapes=[pltpu.VMEM((clip_rows, HEAD_DIM), jnp.bfloat16)] * 3,
        compiler_params=params(),
        name="attention_forward",
    )(place, tile_pairs, lens, *packs, *packs, *packs)


def backward_kernel(place_ref, pairs_ref, *refs):
    q_parts, k_parts, v_parts = refs[:SEQ], refs[SEQ : 2 * SEQ], refs[2 * SEQ : 3 * SEQ]
    own_grads, other_grads = refs[3 * SEQ : 4 * SEQ], refs[4 * SEQ : 5 * SEQ]
    probs_ref = refs[5 * SEQ]
    outs = refs[5 * SEQ + 1 : 6 * SEQ + 1]
    q_all, k_all, v_all, g_all, gq_all, gk_acc, gv_acc = refs[6 * SEQ + 1 :]
    tile_count, neighbours = pairs_ref.shape
    clip_rows, width = q_all.shape
    tile_rows = clip_rows // tile_count
    rows = 2 * tile_rows
    depth = neighbours * tile_rows
    factor = 1.0 / math.sqrt(width)
    load_parts(q_parts, q_all)
    load_parts(k_parts, k_all)
    load_parts(v_parts, v_all)
    half_rows = own_grads[0].shape[0]
    core = place_ref[1]
    for at in range(SEQ):
        for grads, half in ((own_grads[at], core), (other_grads[at ^ 1], 1 - core)):
            g_all[pl.ds(pl.multiple_of((2 * at + half) * half_rows, half_rows), half_rows), :] = grads[...]
    gk_acc[...] = jnp.zeros_like(gk_acc)
    gv_acc[...] = jnp.zeros_like(gv_acc)

    def rows_of(pair):
        return pl.ds(pl.multiple_of(pair * rows, rows), rows)

    def body(group, carry):
        pairs = [group * GROUP + at for at in range(GROUP)]
        nears = [near_of(place_ref, pairs_ref, pair) for pair in pairs]
        probs = [
            probs_ref[0, pl.ds(pl.multiple_of(pair * depth, depth), depth), :] for pair in pairs
        ]
        grads = [spread(g_all[rows_of(pair), :], tile_rows) for pair in pairs]
        grad_scores = []
        for prob, grad, near in zip(probs, grads, nears):
            grad_prob = contract(gather_pair(v_all, near, tile_rows), grad, 1, 1)
            wide = prob.astype(jnp.float32)
            delta = jnp.sum(wide * grad_prob, axis=0, keepdims=True)
            grad_scores.append((wide * (grad_prob - delta)).astype(jnp.bfloat16))
        grad_queries = [
            contract(grad_score, gather_pair(k_all, near, tile_rows), 0, 0) * factor
            for grad_score, near in zip(grad_scores, nears)
        ]
        grad_keys = [
            contract(grad_score, spread(q_all[rows_of(pair), :], tile_rows), 1, 0)
            for grad_score, pair in zip(grad_scores, pairs)
        ]
        grad_vals = [contract(prob, grad, 1, 0) for prob, grad in zip(probs, grads)]
        for pair, near, grad_query, grad_key, grad_val in zip(
            pairs, nears, grad_queries, grad_keys, grad_vals
        ):
            for half in range(2):
                place = pl.ds(pl.multiple_of((2 * pair + half) * tile_rows, tile_rows), tile_rows)
                gq_all[place, :] = diagonal(grad_query, half, tile_rows, width).astype(jnp.bfloat16)
                for n in range(neighbours):
                    at = (slice(n * tile_rows, (n + 1) * tile_rows), slice(half * width, (half + 1) * width))
                    place = pl.ds(pl.multiple_of(near[half][n] * tile_rows, tile_rows), tile_rows)
                    gk_acc[place, :] += grad_key[at]
                    gv_acc[place, :] += grad_val[at]
        return carry

    lax.fori_loop(0, tile_count // 2 // GROUP, body, 0)
    for at, out in enumerate(outs):
        part = slice(at * out.shape[1], (at + 1) * out.shape[1])
        out[0] = gq_all[part, :]
        out[1] = (gk_acc[part, :] * factor).astype(jnp.bfloat16)
        out[2] = gv_acc[part, :].astype(jnp.bfloat16)


def backward(place, tile_pairs, packs, own_grads, other_grads, probs):
    _, rows, local_width = packs[0].shape
    heads = local_width // HEAD_DIM
    clip_rows = rows * SEQ
    grad_spec = pl.BlockSpec((own_grads[0].shape[0], HEAD_DIM), lambda h: (0, h))
    bf16_rows = pltpu.VMEM((clip_rows, HEAD_DIM), jnp.bfloat16)
    f32_rows = pltpu.VMEM((clip_rows, HEAD_DIM), jnp.float32)
    return pl.pallas_call(
        backward_kernel,
        grid=(heads,),
        in_specs=[smem()] * 2
        + [spec for spec in pack_specs(rows) for _ in packs]
        + [grad_spec] * (2 * SEQ)
        + [pl.BlockSpec((1,) + probs.shape[1:], lambda h: (h, 0, 0))],
        out_specs=[pl.BlockSpec((3, rows, HEAD_DIM), lambda h: (0, 0, h))] * SEQ,
        out_shape=[jax.ShapeDtypeStruct((3, rows, local_width), jnp.bfloat16)] * SEQ,
        scratch_shapes=[bf16_rows] * 5 + [f32_rows] * 2,
        compiler_params=params(),
        name="attention_backward",
    )(place, tile_pairs, *packs, *packs, *packs, *own_grads, *other_grads, probs)


def weight_grad_kernel(place_ref, mean, side, att_ref, *refs):
    own, other, outs = refs[:SEQ], refs[SEQ : 2 * SEQ], refs[2 * SEQ :]
    pieces, second = outs[:-1], outs[-1]
    half_rows = own[0].shape[0]
    core = place_ref[1]
    columns, attended = [], []
    for at in range(SEQ):
        for part, half in ((own[at], core), (other[at ^ 1], 1 - core)):
            columns.append(part[...])
            start = pl.multiple_of((2 * at + half) * half_rows, half_rows)
            attended.append(att_ref[pl.ds(start, half_rows), :])
    total = contract(jnp.concatenate(columns, axis=0), jnp.concatenate(attended, axis=0), 0, 0)
    total = (total * mean).astype(jnp.bfloat16)
    count, piece = second.shape[:2]
    step = pl.program_id(0)
    for at in range(count):
        start = 2 * at * piece
        second[at] = total[start + piece : start + 2 * piece]
        owner = step * count + at
        ahead = lax.rem(owner + side - place_ref[4], side)
        for by, out in enumerate(pieces):

            @pl.when(ahead == by)
            def _(out=out, start=start, owner=owner):
                out[owner // side] = total[start : start + piece]


def weight_grad(place, attended, own, other, mean, side, block=640):
    half_rows, features = own[0].shape
    local_width = attended.shape[1]
    piece = features // (side * side) // CORES
    return pl.pallas_call(
        lambda place_ref, *refs: weight_grad_kernel(place_ref, mean, side, *refs),
        grid=(features // block,),
        in_specs=[smem(), pl.BlockSpec(attended.shape, lambda i: (0, 0))]
        + [pl.BlockSpec((half_rows, block), lambda i: (0, i))] * (2 * SEQ),
        out_specs=[pl.BlockSpec((side, piece, local_width), lambda i: (0, 0, 0))] * side
        + [pl.BlockSpec((block // piece // 2, piece, local_width), lambda i: (i, 0, 0))],
        out_shape=[jax.ShapeDtypeStruct((side, piece, local_width), jnp.bfloat16)] * side
        + [jax.ShapeDtypeStruct((side * side, piece, local_width), jnp.bfloat16)],
        compiler_params=params(),
        name="weight_grad",
    )(place, attended, *own, *other)


def device_of(core, seq):
    return core * SEQ + seq


def outward(round_):
    pairs = []
    for core in range(CORES):
        for token in range(SEQ):
            shard = token ^ round_
            pairs.append((device_of(core, token), device_of(shard % 2, 2 * core + shard // 2)))
    return pairs


def inward(round_):
    return [(target, source) for source, target in outward(round_)]


def send(value, pairs):
    others = [pair for pair in pairs if pair[0] != pair[1]]
    got = lax.ppermute(value, ("core", "seq"), others)
    mine = [source for source, target in pairs if source == target]
    if not mine:
        return got
    here = device_of(lax.axis_index("core"), lax.axis_index("seq"))
    keep = functools.reduce(jnp.logical_or, [here == one for one in mine])
    return jnp.where(keep, value, got)


def swap_cores(value):
    return lax.ppermute(value, "core", [(0, 1), (1, 0)])


def shift(value, axis, by):
    count = lax.axis_size(axis)
    return lax.ppermute(value, axis, [(i, (i + by) % count) for i in range(count)])


def add(*terms):
    total = terms[0].astype(jnp.float32)
    for term in terms[1:]:
        total = total + term.astype(jnp.float32)
    return total.astype(jnp.bfloat16)


def take(value, index, axis=0):
    return lax.dynamic_index_in_dim(value, index, axis, keepdims=False)


def scatter(value, axis, dim=0):
    here = lax.axis_index(axis)
    count = lax.axis_size(axis)
    got = [shift(take(value, (here + by) % count, dim), axis, by) for by in (2, 1, 3)]
    return [take(value, here, dim)] + got


def to_shard_holders(w_out, seq, token):
    got = []
    for other in range(2):
        pairs = []
        for holder in range(CORES):
            for shard in range(SEQ):
                window = holder ^ other
                pairs.append((device_of(holder, shard), device_of(shard % 2, shard // 2 + 2 * window)))
        got.append(send(w_out, pairs))
    window = seq // 2
    got = after(got, token)
    return jnp.where(window == 0, jnp.concatenate(got), jnp.concatenate(got[::-1]))


def to_owners(totals, seq):
    window = seq // 2
    got = []
    for other in range(2):
        pairs = []
        for core in range(CORES):
            for at in range(SEQ):
                holder = (at // 2) ^ other
                pairs.append((device_of(core, at), device_of(holder, 2 * (at % 2) + core)))
        got.append(send(jnp.where((window ^ other) == 0, totals[0], totals[1]), pairs))
    return got[0].astype(jnp.float32) + got[1].astype(jnp.float32)


def after(values, *tokens):
    return lax.optimization_barrier((values, tokens))[0]


def per_device(queries, keys, values, gain_q, gain_k, tile_pairs, tile_lens, out_grad, w_out):
    core = lax.axis_index("core")
    seq = lax.axis_index("seq")
    count_z = lax.axis_size("z")
    count_x = lax.axis_size("x")
    rows, features = out_grad.shape
    shard = 2 * (seq % 2) + core
    tiles_per_block = tile_pairs.shape[0] // SEQ
    place = jnp.stack([seq, core, shard, shard * tiles_per_block, lax.axis_index("x")]).astype(jnp.int32)
    lens = jnp.where(seq // 2 == core, tile_lens, swap_cores(tile_lens))

    def half_rows(rows_in, round_):
        half = seq % 2 if round_ % 2 == 0 else 1 - seq % 2
        return take(rows_in.reshape(2, rows // 2, features), half)

    parts = to_rounds(place, queries, keys, values, gain_q, gain_k)
    w_rows = to_shard_holders(w_out, seq, parts[0])
    w_all = lax.all_gather(w_rows, ("z", "x"), axis=0, tiled=True)
    packs = {r: send(parts[r], outward(r)) for r in ORDER}
    came = [packs[r] for r in ORDER]
    own = {}
    for r, token in zip(ORDER, (None, came[0], came[1], came[2:])):
        own[r] = send(half_rows(out_grad if token is None else after(out_grad, token), r), outward(r))
    packs = [packs[r] for r in range(SEQ)]

    def project(part):
        return jnp.dot(part, w_all, preferred_element_type=jnp.float32).astype(jnp.bfloat16)

    attended, probs = forward(place, tile_pairs, lens, packs)
    one, two, three, last = ORDER
    other = {one: swap_cores(own[one]), two: swap_cores(own[two]), three: swap_cores(after(own[three], attended))}
    own_grads = {r: project(own[r]) for r in ORDER[:-1]}
    other_grads = {r: project(other[r]) for r in ORDER[:-1]}
    done = ([own_grads[r] for r in ORDER[:-1]], [other_grads[r] for r in ORDER[:-2]])
    other[last] = swap_cores(after(own[last], *done))
    attended = after(attended, *done, other_grads[three])
    own_grads[last] = project(own[last])
    other_grads[last] = project(other[last])
    own, other, own_grads, other_grads = [
        [table[r] for r in range(SEQ)] for table in (own, other, own_grads, other_grads)
    ]
    *one, two = weight_grad(place, attended, own, other, 1.0 / (count_z * count_x * CORES), count_x)
    two = lax.psum_scatter(two, "z", scatter_dimension=0, tiled=True)
    token = one[0]
    one = [one[0]] + [shift(one[by], "x", by) for by in (2, 1, 3)]
    parts = backward(place, tile_pairs, packs, own_grads, other_grads, after(probs, token))
    parts = {r: send(parts[r], inward(r)) for r in ORDER}
    one = add(*after(one, parts[ORDER[0]]))
    one = lax.psum_scatter(one, "z", scatter_dimension=0, tiled=True)[0]
    two = scatter(after(two, parts[ORDER[0]], parts[ORDER[1]]), "x")
    two = add(*after(two, parts[ORDER[2]], parts[ORDER[3]]))
    grad_w = to_owners((one, two), seq)
    grad_q, grad_k, grad_v = finish(
        place, queries, keys, gain_q, gain_k, [parts[r] for r in range(SEQ)]
    )
    return (grad_q, grad_k, grad_v, grad_w)


def solution(mesh):
    dp = mesh.shape["dp"]
    side = math.isqrt(dp // CORES)
    parts = Mesh(mesh.devices.reshape(side, side, CORES, SEQ), ("z", "x", "core", "seq"))
    dp_axes = ("z", "x", "core")
    tokens = P(dp_axes + ("seq",), None)
    return jax.shard_map(
        per_device,
        mesh=parts,
        in_specs=(tokens, tokens, tokens, P(), P(), P(), P(dp_axes, None), tokens, P(dp_axes, "seq")),
        out_specs=(tokens, tokens, tokens, P(dp_axes, "seq")),
        check_vma=False,
    )
```

```python
import functools
import math

import jax
import jax.numpy as jnp
from jax import lax
from jax.experimental import pallas as pl
from jax.experimental.pallas import tpu as pltpu
from jax.sharding import Mesh, PartitionSpec as P

HEAD_DIM = 128


EPS = 1e-06
LOG2E = 1.4426950408889634
MIN_LIVE = 40
SEQ = 4
CORES = 2
GROUP = 4
ORDER = (0, 3, 1, 2)


def smem():
    return pl.BlockSpec(memory_space=pltpu.SMEM)


def params():
    return pltpu.CompilerParams(vmem_limit_bytes=48 << 20)


def contract(left, right, left_dim, right_dim):
    return lax.dot_general(
        left, right, (((left_dim,), (right_dim,)), ((), ())), preferred_element_type=jnp.float32
    )


def row_scale_of(values_f):
    return lax.rsqrt(jnp.mean(values_f * values_f, axis=-1, keepdims=True) + EPS)


def shard_of(place_ref, round_, width):
    return pl.ds(pl.multiple_of(jnp.bitwise_xor(place_ref[0], round_) * width, 128), width)


def rounds_kernel(place_ref, q_ref, k_ref, v_ref, gain_q_ref, gain_k_ref, *refs):
    outs, normed = refs[:-1], refs[-1]
    for at, (x_ref, gain_ref) in enumerate(((q_ref, gain_q_ref), (k_ref, gain_k_ref))):
        values_f = x_ref[...].astype(jnp.float32)
        normed[at] = (values_f * row_scale_of(values_f) * gain_ref[...][None, :]).astype(jnp.bfloat16)
    for round_, out in enumerate(outs):
        columns = shard_of(place_ref, round_, out.shape[2])
        out[0] = normed[0, :, columns]
        out[1] = normed[1, :, columns]
        out[2] = v_ref[:, columns]


def to_rounds(place, queries, keys, values, gain_q, gain_k, block=64):
    rows, width = queries.shape
    row_spec = pl.BlockSpec((block, width), lambda i: (i, 0))
    gain_spec = pl.BlockSpec((width,), lambda i: (0,))
    return pl.pallas_call(
        rounds_kernel,
        grid=(rows // block,),
        in_specs=[smem()] + [row_spec] * 3 + [gain_spec] * 2,
        out_specs=[pl.BlockSpec((3, block, width // SEQ), lambda i: (0, i, 0))] * SEQ,
        out_shape=[jax.ShapeDtypeStruct((3, rows, width // SEQ), jnp.bfloat16)] * SEQ,
        scratch_shapes=[pltpu.VMEM((2, block, width), jnp.bfloat16)],
        name="norm_rows",
    )(place, queries, keys, values, gain_q, gain_k)


def finish_kernel(place_ref, q_ref, k_ref, gain_q_ref, gain_k_ref, *refs):
    parts, outs, joined = refs[:SEQ], refs[SEQ:-1], refs[-1]
    width = q_ref.shape[1]
    for round_, part in enumerate(parts):
        columns = shard_of(place_ref, round_, part.shape[2])
        joined[0, :, columns] = part[0]
        joined[1, :, columns] = part[1]
        outs[2][:, columns] = part[2]
    for at, (x_ref, gain_ref) in enumerate(((q_ref, gain_q_ref), (k_ref, gain_k_ref))):
        values_f = x_ref[...].astype(jnp.float32)
        row_scale = row_scale_of(values_f)
        gated = gain_ref[...][None, :] * joined[at].astype(jnp.float32)
        inner = jnp.sum(gated * values_f, axis=-1, keepdims=True)
        back = values_f * (row_scale * row_scale * row_scale * inner * (1.0 / width))
        outs[at][...] = (row_scale * gated - back).astype(jnp.bfloat16)


def finish(place, queries, keys, gain_q, gain_k, parts, block=64):
    rows, width = queries.shape
    row_spec = pl.BlockSpec((block, width), lambda i: (i, 0))
    gain_spec = pl.BlockSpec((width,), lambda i: (0,))
    return pl.pallas_call(
        finish_kernel,
        grid=(rows // block,),
        in_specs=[smem()]
        + [row_spec] * 2
        + [gain_spec] * 2
        + [pl.BlockSpec((3, block, width // SEQ), lambda i: (0, i, 0))] * SEQ,
        out_specs=[row_spec] * 3,
        out_shape=[jax.ShapeDtypeStruct((rows, width), jnp.bfloat16)] * 3,
        scratch_shapes=[pltpu.VMEM((2, block, width), jnp.bfloat16)],
        name="norm_back",
    )(place, queries, keys, gain_q, gain_k, *parts)


def tile_at(ref, index, rows):
    return ref[pl.ds(pl.multiple_of(index * rows, rows), rows), :]


def gather_pair(ref, near, rows):
    return jnp.concatenate(
        [
            jnp.concatenate([tile_at(ref, one, rows), tile_at(ref, two, rows)], axis=1)
            for one, two in zip(*near)
        ],
        axis=0,
    )


def spread(block, rows):
    twice = jnp.concatenate([block, block], axis=1)
    width = block.shape[1]
    own = (lax.broadcasted_iota(jnp.int32, twice.shape, 0) < rows) == (
        lax.broadcasted_iota(jnp.int32, twice.shape, 1) < width
    )
    return jnp.where(own, twice, jnp.zeros_like(twice))


def near_of(place_ref, pairs_ref, pair):
    flip = place_ref[3]
    return [
        [
            jnp.bitwise_xor(pairs_ref[jnp.bitwise_xor(2 * pair + half, flip), n], flip)
            for n in range(pairs_ref.shape[1])
        ]
        for half in range(2)
    ]


def load_parts(parts, whole):
    for at, part in enumerate(parts):
        whole[at * part.shape[0] : (at + 1) * part.shape[0], :] = part[...]


def diagonal(product, half, tile_rows, width):
    return product[half * tile_rows : (half + 1) * tile_rows, half * width : (half + 1) * width]


def forward_kernel(place_ref, pairs_ref, lens_ref, *refs):
    q_parts, k_parts, v_parts = refs[:SEQ], refs[SEQ : 2 * SEQ], refs[2 * SEQ : 3 * SEQ]
    att_ref, probs_ref, q_all, k_all, v_all = refs[3 * SEQ :]
    tile_count, neighbours = pairs_ref.shape
    clip_rows, width = q_all.shape
    tile_rows = clip_rows // tile_count
    rows = 2 * tile_rows
    depth = neighbours * tile_rows
    scale = LOG2E / math.sqrt(width)
    load_parts(q_parts, q_all)
    load_parts(k_parts, k_all)
    load_parts(v_parts, v_all)
    shape = (tile_rows - MIN_LIVE, rows)
    first = lax.broadcasted_iota(jnp.int32, shape, 1) < tile_rows
    slot = lax.broadcasted_iota(jnp.int32, shape, 0) + MIN_LIVE

    def length(tile):
        return lens_ref[0, jnp.bitwise_xor(tile, place_ref[3])]

    def score(pair, near):
        keys = gather_pair(k_all, near, tile_rows)
        queries = spread(q_all[pl.ds(pl.multiple_of(pair * rows, rows), rows), :], tile_rows)
        scores = contract(keys, queries, 1, 1)
        pieces = []
        for n in range(neighbours):
            start = n * tile_rows
            pieces.append(scores[start : start + MIN_LIVE])
            live = slot < jnp.where(first, length(near[0][n]), length(near[1][n]))
            pieces.append(jnp.where(live, scores[start + MIN_LIVE : start + tile_rows], -jnp.inf))
        return jnp.concatenate(pieces, axis=0)

    def soften(scores):
        weights = jnp.exp2((scores - jnp.max(scores, axis=0, keepdims=True)) * scale)
        return (weights * (1.0 / jnp.sum(weights, axis=0, keepdims=True))).astype(jnp.bfloat16)

    def body(group, carry):
        pairs = [group * GROUP + at for at in range(GROUP)]
        nears = [near_of(place_ref, pairs_ref, pair) for pair in pairs]
        probs = [soften(score(pair, near)) for pair, near in zip(pairs, nears)]
        attended = [
            contract(prob, gather_pair(v_all, near, tile_rows), 0, 0) for prob, near in zip(probs, nears)
        ]
        for pair, prob, product in zip(pairs, probs, attended):
            probs_ref[0, pl.ds(pl.multiple_of(pair * depth, depth), depth), :] = prob
            for half in range(2):
                place = pl.ds(pl.multiple_of((2 * pair + half) * tile_rows, tile_rows), tile_rows)
                att_ref[place, :] = diagonal(product, half, tile_rows, width).astype(jnp.bfloat16)
        return carry

    lax.fori_loop(0, tile_count // 2 // GROUP, body, 0)


def pack_specs(rows):
    return [pl.BlockSpec((None, rows, HEAD_DIM), lambda h, which=which: (which, 0, h)) for which in range(3)]


def forward(place, tile_pairs, lens, packs):
    _, rows, local_width = packs[0].shape
    heads = local_width // HEAD_DIM
    clip_rows = rows * SEQ
    pairs = tile_pairs.shape[0] // 2
    depth = tile_pairs.shape[1] * (clip_rows // tile_pairs.shape[0])
    return pl.pallas_call(
        forward_kernel,
        grid=(heads,),
        in_specs=[smem()] * 3 + [spec for spec in pack_specs(rows) for _ in packs],
        out_specs=[
            pl.BlockSpec((clip_rows, HEAD_DIM), lambda h: (0, h)),
            pl.BlockSpec((1, pairs * depth, HEAD_DIM), lambda h: (h, 0, 0)),
        ],
        out_shape=[
            jax.ShapeDtypeStruct((clip_rows, local_width), jnp.bfloat16),
            jax.ShapeDtypeStruct((heads, pairs * depth, HEAD_DIM), jnp.bfloat16),
        ],
        scratch_shapes=[pltpu.VMEM((clip_rows, HEAD_DIM), jnp.bfloat16)] * 3,
        compiler_params=params(),
        name="attention_forward",
    )(place, tile_pairs, lens, *packs, *packs, *packs)


def backward_kernel(place_ref, pairs_ref, *refs):
    q_parts, k_parts, v_parts = refs[:SEQ], refs[SEQ : 2 * SEQ], refs[2 * SEQ : 3 * SEQ]
    own_grads, other_grads = refs[3 * SEQ : 4 * SEQ], refs[4 * SEQ : 5 * SEQ]
    probs_ref = refs[5 * SEQ]
    outs = refs[5 * SEQ + 1 : 6 * SEQ + 1]
    q_all, k_all, v_all, g_all, gq_all, gk_acc, gv_acc = refs[6 * SEQ + 1 :]
    tile_count, neighbours = pairs_ref.shape
    clip_rows, width = q_all.shape
    tile_rows = clip_rows // tile_count
    rows = 2 * tile_rows
    depth = neighbours * tile_rows
    factor = 1.0 / math.sqrt(width)
    load_parts(q_parts, q_all)
    load_parts(k_parts, k_all)
    load_parts(v_parts, v_all)
    half_rows = own_grads[0].shape[0]
    core = place_ref[1]
    for at in range(SEQ):
        for grads, half in ((own_grads[at], core), (other_grads[at ^ 1], 1 - core)):
            g_all[pl.ds(pl.multiple_of((2 * at + half) * half_rows, half_rows), half_rows), :] = grads[...]
    gk_acc[...] = jnp.zeros_like(gk_acc)
    gv_acc[...] = jnp.zeros_like(gv_acc)

    def rows_of(pair):
        return pl.ds(pl.multiple_of(pair * rows, rows), rows)

    def body(group, carry):
        pairs = [group * GROUP + at for at in range(GROUP)]
        nears = [near_of(place_ref, pairs_ref, pair) for pair in pairs]
        probs = [
            probs_ref[0, pl.ds(pl.multiple_of(pair * depth, depth), depth), :] for pair in pairs
        ]
        grads = [spread(g_all[rows_of(pair), :], tile_rows) for pair in pairs]
        grad_scores = []
        for prob, grad, near in zip(probs, grads, nears):
            grad_prob = contract(gather_pair(v_all, near, tile_rows), grad, 1, 1)
            wide = prob.astype(jnp.float32)
            delta = jnp.sum(wide * grad_prob, axis=0, keepdims=True)
            grad_scores.append((wide * (grad_prob - delta)).astype(jnp.bfloat16))
        grad_queries = [
            contract(grad_score, gather_pair(k_all, near, tile_rows), 0, 0) * factor
            for grad_score, near in zip(grad_scores, nears)
        ]
        grad_keys = [
            contract(grad_score, spread(q_all[rows_of(pair), :], tile_rows), 1, 0)
            for grad_score, pair in zip(grad_scores, pairs)
        ]
        grad_vals = [contract(prob, grad, 1, 0) for prob, grad in zip(probs, grads)]
        for pair, near, grad_query, grad_key, grad_val in zip(
            pairs, nears, grad_queries, grad_keys, grad_vals
        ):
            for half in range(2):
                place = pl.ds(pl.multiple_of((2 * pair + half) * tile_rows, tile_rows), tile_rows)
                gq_all[place, :] = diagonal(grad_query, half, tile_rows, width).astype(jnp.bfloat16)
                for n in range(neighbours):
                    at = (slice(n * tile_rows, (n + 1) * tile_rows), slice(half * width, (half + 1) * width))
                    place = pl.ds(pl.multiple_of(near[half][n] * tile_rows, tile_rows), tile_rows)
                    gk_acc[place, :] += grad_key[at]
                    gv_acc[place, :] += grad_val[at]
        return carry

    lax.fori_loop(0, tile_count // 2 // GROUP, body, 0)
    for at, out in enumerate(outs):
        part = slice(at * out.shape[1], (at + 1) * out.shape[1])
        out[0] = gq_all[part, :]
        out[1] = (gk_acc[part, :] * factor).astype(jnp.bfloat16)
        out[2] = gv_acc[part, :].astype(jnp.bfloat16)


def backward(place, tile_pairs, packs, own_grads, other_grads, probs):
    _, rows, local_width = packs[0].shape
    heads = local_width // HEAD_DIM
    clip_rows = rows * SEQ
    grad_spec = pl.BlockSpec((own_grads[0].shape[0], HEAD_DIM), lambda h: (0, h))
    bf16_rows = pltpu.VMEM((clip_rows, HEAD_DIM), jnp.bfloat16)
    f32_rows = pltpu.VMEM((clip_rows, HEAD_DIM), jnp.float32)
    return pl.pallas_call(
        backward_kernel,
        grid=(heads,),
        in_specs=[smem()] * 2
        + [spec for spec in pack_specs(rows) for _ in packs]
        + [grad_spec] * (2 * SEQ)
        + [pl.BlockSpec((1,) + probs.shape[1:], lambda h: (h, 0, 0))],
        out_specs=[pl.BlockSpec((3, rows, HEAD_DIM), lambda h: (0, 0, h))] * SEQ,
        out_shape=[jax.ShapeDtypeStruct((3, rows, local_width), jnp.bfloat16)] * SEQ,
        scratch_shapes=[bf16_rows] * 5 + [f32_rows] * 2,
        compiler_params=params(),
        name="attention_backward",
    )(place, tile_pairs, *packs, *packs, *packs, *own_grads, *other_grads, probs)


def weight_grad_kernel(place_ref, mean, side, att_ref, *refs):
    own, other, outs = refs[:SEQ], refs[SEQ : 2 * SEQ], refs[2 * SEQ :]
    pieces, second = outs[:-1], outs[-1]
    half_rows = own[0].shape[0]
    core = place_ref[1]
    columns, attended = [], []
    for at in range(SEQ):
        for part, half in ((own[at], core), (other[at ^ 1], 1 - core)):
            columns.append(part[...])
            start = pl.multiple_of((2 * at + half) * half_rows, half_rows)
            attended.append(att_ref[pl.ds(start, half_rows), :])
    total = contract(jnp.concatenate(columns, axis=0), jnp.concatenate(attended, axis=0), 0, 0)
    total = (total * mean).astype(jnp.bfloat16)
    count, piece = second.shape[:2]
    step = pl.program_id(0)
    for at in range(count):
        start = 2 * at * piece
        second[at] = total[start + piece : start + 2 * piece]
        owner = step * count + at
        ahead = lax.rem(owner + side - place_ref[4], side)
        for by, out in enumerate(pieces):

            @pl.when(ahead == by)
            def _(out=out, start=start, owner=owner):
                out[owner // side] = total[start : start + piece]


def weight_grad(place, attended, own, other, mean, side, block=640):
    half_rows, features = own[0].shape
    local_width = attended.shape[1]
    piece = features // (side * side) // CORES
    return pl.pallas_call(
        lambda place_ref, *refs: weight_grad_kernel(place_ref, mean, side, *refs),
        grid=(features // block,),
        in_specs=[smem(), pl.BlockSpec(attended.shape, lambda i: (0, 0))]
        + [pl.BlockSpec((half_rows, block), lambda i: (0, i))] * (2 * SEQ),
        out_specs=[pl.BlockSpec((side, piece, local_width), lambda i: (0, 0, 0))] * side
        + [pl.BlockSpec((block // piece // 2, piece, local_width), lambda i: (i, 0, 0))],
        out_shape=[jax.ShapeDtypeStruct((side, piece, local_width), jnp.bfloat16)] * side
        + [jax.ShapeDtypeStruct((side * side, piece, local_width), jnp.bfloat16)],
        compiler_params=params(),
        name="weight_grad",
    )(place, attended, *own, *other)


def device_of(core, seq):
    return core * SEQ + seq


def outward(round_):
    pairs = []
    for core in range(CORES):
        for token in range(SEQ):
            shard = token ^ round_
            pairs.append((device_of(core, token), device_of(shard % 2, 2 * core + shard // 2)))
    return pairs


def inward(round_):
    return [(target, source) for source, target in outward(round_)]


def send(value, pairs):
    others = [pair for pair in pairs if pair[0] != pair[1]]
    got = lax.ppermute(value, ("core", "seq"), others)
    mine = [source for source, target in pairs if source == target]
    if not mine:
        return got
    here = device_of(lax.axis_index("core"), lax.axis_index("seq"))
    keep = functools.reduce(jnp.logical_or, [here == one for one in mine])
    return jnp.where(keep, value, got)


def swap_cores(value):
    return lax.ppermute(value, "core", [(0, 1), (1, 0)])


def shift(value, axis, by):
    count = lax.axis_size(axis)
    return lax.ppermute(value, axis, [(i, (i + by) % count) for i in range(count)])


def add(*terms):
    total = terms[0].astype(jnp.float32)
    for term in terms[1:]:
        total = total + term.astype(jnp.float32)
    return total.astype(jnp.bfloat16)


def take(value, index, axis=0):
    return lax.dynamic_index_in_dim(value, index, axis, keepdims=False)


def scatter(value, axis, dim=0):
    here = lax.axis_index(axis)
    count = lax.axis_size(axis)
    got = [shift(take(value, (here + by) % count, dim), axis, by) for by in (2, 1, 3)]
    return [take(value, here, dim)] + got


def to_shard_holders(w_out, seq, token):
    got = []
    for other in range(2):
        pairs = []
        for holder in range(CORES):
            for shard in range(SEQ):
                window = holder ^ other
                pairs.append((device_of(holder, shard), device_of(shard % 2, shard // 2 + 2 * window)))
        got.append(send(w_out, pairs))
    window = seq // 2
    got = after(got, token)
    return jnp.where(window == 0, jnp.concatenate(got), jnp.concatenate(got[::-1]))


def to_owners(totals, seq):
    window = seq // 2
    got = []
    for other in range(2):
        pairs = []
        for core in range(CORES):
            for at in range(SEQ):
                holder = (at // 2) ^ other
                pairs.append((device_of(core, at), device_of(holder, 2 * (at % 2) + core)))
        got.append(send(jnp.where((window ^ other) == 0, totals[0], totals[1]), pairs))
    return got[0].astype(jnp.float32) + got[1].astype(jnp.float32)


def after(values, *tokens):
    return lax.optimization_barrier((values, tokens))[0]


def per_device(queries, keys, values, gain_q, gain_k, tile_pairs, tile_lens, out_grad, w_out):
    core = lax.axis_index("core")
    seq = lax.axis_index("seq")
    count_z = lax.axis_size("z")
    count_x = lax.axis_size("x")
    rows, features = out_grad.shape
    shard = 2 * (seq % 2) + core
    tiles_per_block = tile_pairs.shape[0] // SEQ
    place = jnp.stack([seq, core, shard, shard * tiles_per_block, lax.axis_index("x")]).astype(jnp.int32)
    lens = jnp.where(seq // 2 == core, tile_lens, swap_cores(tile_lens))

    def half_rows(rows_in, round_):
        half = seq % 2 if round_ % 2 == 0 else 1 - seq % 2
        return take(rows_in.reshape(2, rows // 2, features), half)

    parts = to_rounds(place, queries, keys, values, gain_q, gain_k)
    w_rows = to_shard_holders(w_out, seq, parts[0])
    w_all = lax.all_gather(w_rows, ("z", "x"), axis=0, tiled=True)
    packs = {r: send(parts[r], outward(r)) for r in ORDER}
    came = [packs[r] for r in ORDER]
    own = {}
    for r, token in zip(ORDER, came):
        own[r] = send(half_rows(after(out_grad, token), r), outward(r))
    packs = [packs[r] for r in range(SEQ)]

    def project(part):
        return jnp.dot(part, w_all, preferred_element_type=jnp.float32).astype(jnp.bfloat16)

    attended, probs = forward(place, tile_pairs, lens, packs)
    one, two, three, last = ORDER
    other = {one: swap_cores(own[one]), two: swap_cores(after(own[two], attended))}
    own_grads = {one: project(own[one]), two: project(own[two])}
    other_grads = {one: project(other[one]), two: project(other[two])}
    other[three] = swap_cores(after(own[three], own_grads[one], other_grads[one]))
    own_grads[three], other_grads[three] = project(own[three]), project(other[three])
    done = ([own_grads[r] for r in ORDER[:-1]], [other_grads[r] for r in ORDER[:-2]])
    other[last] = swap_cores(after(own[last], *done))
    own_grads[last] = project(own[last])
    other_grads[last] = project(other[last])
    attended = after(attended, own_grads, other_grads)
    own, other, own_grads, other_grads = [
        [table[r] for r in range(SEQ)] for table in (own, other, own_grads, other_grads)
    ]
    *one, two = weight_grad(place, attended, own, other, 1.0 / (count_z * count_x * CORES), count_x)
    two = lax.psum_scatter(two, "z", scatter_dimension=0, tiled=True)
    token = one[0]
    one = [one[0]] + [shift(one[by], "x", by) for by in (2, 1, 3)]
    parts = backward(place, tile_pairs, packs, own_grads, other_grads, after(probs, token))
    one = add(*after(one, parts[0]))
    one = lax.psum_scatter(one, "z", scatter_dimension=0, tiled=True)[0]
    parts = {r: send(parts[r], inward(r)) for r in ORDER}
    two = scatter(after(two, parts[ORDER[0]], parts[ORDER[1]]), "x")
    two = add(*after(two, parts[ORDER[2]], parts[ORDER[3]]))
    grad_w = to_owners((one, two), seq)
    grad_q, grad_k, grad_v = finish(
        place, queries, keys, gain_q, gain_k, [parts[r] for r in range(SEQ)]
    )
    return (grad_q, grad_k, grad_v, grad_w)


def solution(mesh):
    dp = mesh.shape["dp"]
    side = math.isqrt(dp // CORES)
    parts = Mesh(mesh.devices.reshape(side, side, CORES, SEQ), ("z", "x", "core", "seq"))
    dp_axes = ("z", "x", "core")
    tokens = P(dp_axes + ("seq",), None)
    return jax.shard_map(
        per_device,
        mesh=parts,
        in_specs=(tokens, tokens, tokens, P(), P(), P(), P(dp_axes, None), tokens, P(dp_axes, "seq")),
        out_specs=(tokens, tokens, tokens, P(dp_axes, "seq")),
        check_vma=False,
    )
```

```python
import functools
import math

import jax
import jax.numpy as jnp
from jax import lax
from jax.experimental import pallas as pl
from jax.experimental.pallas import tpu as pltpu
from jax.sharding import Mesh, PartitionSpec as P

HEAD_DIM = 128


EPS = 1e-06
LOG2E = 1.4426950408889634
MIN_LIVE = 40
SEQ = 4
CORES = 2
GROUP = 4
ORDER = (0, 3, 1, 2)


def smem():
    return pl.BlockSpec(memory_space=pltpu.SMEM)


def params():
    return pltpu.CompilerParams(vmem_limit_bytes=48 << 20)


def contract(left, right, left_dim, right_dim):
    return lax.dot_general(
        left, right, (((left_dim,), (right_dim,)), ((), ())), preferred_element_type=jnp.float32
    )


def row_scale_of(values_f):
    return lax.rsqrt(jnp.mean(values_f * values_f, axis=-1, keepdims=True) + EPS)


def shard_of(place_ref, round_, width):
    return pl.ds(pl.multiple_of(jnp.bitwise_xor(place_ref[0], round_) * width, 128), width)


def rounds_kernel(place_ref, q_ref, k_ref, v_ref, gain_q_ref, gain_k_ref, *refs):
    outs, normed = refs[:-1], refs[-1]
    for at, (x_ref, gain_ref) in enumerate(((q_ref, gain_q_ref), (k_ref, gain_k_ref))):
        values_f = x_ref[...].astype(jnp.float32)
        normed[at] = (values_f * row_scale_of(values_f) * gain_ref[...][None, :]).astype(jnp.bfloat16)
    for round_, out in enumerate(outs):
        columns = shard_of(place_ref, round_, out.shape[2])
        out[0] = normed[0, :, columns]
        out[1] = normed[1, :, columns]
        out[2] = v_ref[:, columns]


def to_rounds(place, queries, keys, values, gain_q, gain_k, block=64):
    rows, width = queries.shape
    row_spec = pl.BlockSpec((block, width), lambda i: (i, 0))
    gain_spec = pl.BlockSpec((width,), lambda i: (0,))
    return pl.pallas_call(
        rounds_kernel,
        grid=(rows // block,),
        in_specs=[smem()] + [row_spec] * 3 + [gain_spec] * 2,
        out_specs=[pl.BlockSpec((3, block, width // SEQ), lambda i: (0, i, 0))] * SEQ,
        out_shape=[jax.ShapeDtypeStruct((3, rows, width // SEQ), jnp.bfloat16)] * SEQ,
        scratch_shapes=[pltpu.VMEM((2, block, width), jnp.bfloat16)],
        name="norm_rows",
    )(place, queries, keys, values, gain_q, gain_k)


def finish_kernel(place_ref, q_ref, k_ref, gain_q_ref, gain_k_ref, *refs):
    parts, outs, joined = refs[:SEQ], refs[SEQ:-1], refs[-1]
    width = q_ref.shape[1]
    for round_, part in enumerate(parts):
        columns = shard_of(place_ref, round_, part.shape[2])
        joined[0, :, columns] = part[0]
        joined[1, :, columns] = part[1]
        outs[2][:, columns] = part[2]
    for at, (x_ref, gain_ref) in enumerate(((q_ref, gain_q_ref), (k_ref, gain_k_ref))):
        values_f = x_ref[...].astype(jnp.float32)
        row_scale = row_scale_of(values_f)
        gated = gain_ref[...][None, :] * joined[at].astype(jnp.float32)
        inner = jnp.sum(gated * values_f, axis=-1, keepdims=True)
        back = values_f * (row_scale * row_scale * row_scale * inner * (1.0 / width))
        outs[at][...] = (row_scale * gated - back).astype(jnp.bfloat16)


def finish(place, queries, keys, gain_q, gain_k, parts, block=64):
    rows, width = queries.shape
    row_spec = pl.BlockSpec((block, width), lambda i: (i, 0))
    gain_spec = pl.BlockSpec((width,), lambda i: (0,))
    return pl.pallas_call(
        finish_kernel,
        grid=(rows // block,),
        in_specs=[smem()]
        + [row_spec] * 2
        + [gain_spec] * 2
        + [pl.BlockSpec((3, block, width // SEQ), lambda i: (0, i, 0))] * SEQ,
        out_specs=[row_spec] * 3,
        out_shape=[jax.ShapeDtypeStruct((rows, width), jnp.bfloat16)] * 3,
        scratch_shapes=[pltpu.VMEM((2, block, width), jnp.bfloat16)],
        name="norm_back",
    )(place, queries, keys, gain_q, gain_k, *parts)


def tile_at(ref, index, rows):
    return ref[pl.ds(pl.multiple_of(index * rows, rows), rows), :]


def gather_pair(ref, near, rows):
    return jnp.concatenate(
        [
            jnp.concatenate([tile_at(ref, one, rows), tile_at(ref, two, rows)], axis=1)
            for one, two in zip(*near)
        ],
        axis=0,
    )


def spread(block, rows):
    twice = jnp.concatenate([block, block], axis=1)
    width = block.shape[1]
    own = (lax.broadcasted_iota(jnp.int32, twice.shape, 0) < rows) == (
        lax.broadcasted_iota(jnp.int32, twice.shape, 1) < width
    )
    return jnp.where(own, twice, jnp.zeros_like(twice))


def near_of(place_ref, pairs_ref, pair):
    flip = place_ref[3]
    return [
        [
            jnp.bitwise_xor(pairs_ref[jnp.bitwise_xor(2 * pair + half, flip), n], flip)
            for n in range(pairs_ref.shape[1])
        ]
        for half in range(2)
    ]


def load_parts(parts, whole):
    for at, part in enumerate(parts):
        whole[at * part.shape[0] : (at + 1) * part.shape[0], :] = part[...]


def diagonal(product, half, tile_rows, width):
    return product[half * tile_rows : (half + 1) * tile_rows, half * width : (half + 1) * width]


def forward_kernel(place_ref, pairs_ref, lens_ref, *refs):
    q_parts, k_parts, v_parts = refs[:SEQ], refs[SEQ : 2 * SEQ], refs[2 * SEQ : 3 * SEQ]
    att_ref, probs_ref, q_all, k_all, v_all = refs[3 * SEQ :]
    tile_count, neighbours = pairs_ref.shape
    clip_rows, width = q_all.shape
    tile_rows = clip_rows // tile_count
    rows = 2 * tile_rows
    depth = neighbours * tile_rows
    scale = LOG2E / math.sqrt(width)
    load_parts(q_parts, q_all)
    load_parts(k_parts, k_all)
    load_parts(v_parts, v_all)
    shape = (tile_rows - MIN_LIVE, rows)
    first = lax.broadcasted_iota(jnp.int32, shape, 1) < tile_rows
    slot = lax.broadcasted_iota(jnp.int32, shape, 0) + MIN_LIVE

    def length(tile):
        return lens_ref[0, jnp.bitwise_xor(tile, place_ref[3])]

    def score(pair, near):
        keys = gather_pair(k_all, near, tile_rows)
        queries = spread(q_all[pl.ds(pl.multiple_of(pair * rows, rows), rows), :], tile_rows)
        scores = contract(keys, queries, 1, 1)
        pieces = []
        for n in range(neighbours):
            start = n * tile_rows
            pieces.append(scores[start : start + MIN_LIVE])
            live = slot < jnp.where(first, length(near[0][n]), length(near[1][n]))
            pieces.append(jnp.where(live, scores[start + MIN_LIVE : start + tile_rows], -jnp.inf))
        return jnp.concatenate(pieces, axis=0)

    def soften(scores):
        weights = jnp.exp2((scores - jnp.max(scores, axis=0, keepdims=True)) * scale)
        return (weights * (1.0 / jnp.sum(weights, axis=0, keepdims=True))).astype(jnp.bfloat16)

    def body(group, carry):
        pairs = [group * GROUP + at for at in range(GROUP)]
        nears = [near_of(place_ref, pairs_ref, pair) for pair in pairs]
        probs = [soften(score(pair, near)) for pair, near in zip(pairs, nears)]
        attended = [
            contract(prob, gather_pair(v_all, near, tile_rows), 0, 0) for prob, near in zip(probs, nears)
        ]
        for pair, prob, product in zip(pairs, probs, attended):
            probs_ref[0, pl.ds(pl.multiple_of(pair * depth, depth), depth), :] = prob
            for half in range(2):
                place = pl.ds(pl.multiple_of((2 * pair + half) * tile_rows, tile_rows), tile_rows)
                att_ref[place, :] = diagonal(product, half, tile_rows, width).astype(jnp.bfloat16)
        return carry

    lax.fori_loop(0, tile_count // 2 // GROUP, body, 0)


def pack_specs(rows):
    return [pl.BlockSpec((None, rows, HEAD_DIM), lambda h, which=which: (which, 0, h)) for which in range(3)]


def forward(place, tile_pairs, lens, packs):
    _, rows, local_width = packs[0].shape
    heads = local_width // HEAD_DIM
    clip_rows = rows * SEQ
    pairs = tile_pairs.shape[0] // 2
    depth = tile_pairs.shape[1] * (clip_rows // tile_pairs.shape[0])
    return pl.pallas_call(
        forward_kernel,
        grid=(heads,),
        in_specs=[smem()] * 3 + [spec for spec in pack_specs(rows) for _ in packs],
        out_specs=[
            pl.BlockSpec((clip_rows, HEAD_DIM), lambda h: (0, h)),
            pl.BlockSpec((1, pairs * depth, HEAD_DIM), lambda h: (h, 0, 0)),
        ],
        out_shape=[
            jax.ShapeDtypeStruct((clip_rows, local_width), jnp.bfloat16),
            jax.ShapeDtypeStruct((heads, pairs * depth, HEAD_DIM), jnp.bfloat16),
        ],
        scratch_shapes=[pltpu.VMEM((clip_rows, HEAD_DIM), jnp.bfloat16)] * 3,
        compiler_params=params(),
        name="attention_forward",
    )(place, tile_pairs, lens, *packs, *packs, *packs)


def backward_kernel(place_ref, pairs_ref, *refs):
    q_parts, k_parts, v_parts = refs[:SEQ], refs[SEQ : 2 * SEQ], refs[2 * SEQ : 3 * SEQ]
    own_grads, other_grads = refs[3 * SEQ : 4 * SEQ], refs[4 * SEQ : 5 * SEQ]
    probs_ref = refs[5 * SEQ]
    outs = refs[5 * SEQ + 1 : 6 * SEQ + 1]
    q_all, k_all, v_all, g_all, gq_all, gk_acc, gv_acc = refs[6 * SEQ + 1 :]
    tile_count, neighbours = pairs_ref.shape
    clip_rows, width = q_all.shape
    tile_rows = clip_rows // tile_count
    rows = 2 * tile_rows
    depth = neighbours * tile_rows
    factor = 1.0 / math.sqrt(width)
    load_parts(q_parts, q_all)
    load_parts(k_parts, k_all)
    load_parts(v_parts, v_all)
    half_rows = own_grads[0].shape[0]
    core = place_ref[1]
    for at in range(SEQ):
        for grads, half in ((own_grads[at], core), (other_grads[at ^ 1], 1 - core)):
            g_all[pl.ds(pl.multiple_of((2 * at + half) * half_rows, half_rows), half_rows), :] = grads[...]
    gk_acc[...] = jnp.zeros_like(gk_acc)
    gv_acc[...] = jnp.zeros_like(gv_acc)

    def rows_of(pair):
        return pl.ds(pl.multiple_of(pair * rows, rows), rows)

    def body(group, carry):
        pairs = [group * GROUP + at for at in range(GROUP)]
        nears = [near_of(place_ref, pairs_ref, pair) for pair in pairs]
        probs = [
            probs_ref[0, pl.ds(pl.multiple_of(pair * depth, depth), depth), :] for pair in pairs
        ]
        grads = [spread(g_all[rows_of(pair), :], tile_rows) for pair in pairs]
        grad_scores = []
        for prob, grad, near in zip(probs, grads, nears):
            grad_prob = contract(gather_pair(v_all, near, tile_rows), grad, 1, 1)
            wide = prob.astype(jnp.float32)
            delta = jnp.sum(wide * grad_prob, axis=0, keepdims=True)
            grad_scores.append((wide * (grad_prob - delta)).astype(jnp.bfloat16))
        grad_queries = [
            contract(grad_score, gather_pair(k_all, near, tile_rows), 0, 0) * factor
            for grad_score, near in zip(grad_scores, nears)
        ]
        grad_keys = [
            contract(grad_score, spread(q_all[rows_of(pair), :], tile_rows), 1, 0)
            for grad_score, pair in zip(grad_scores, pairs)
        ]
        grad_vals = [contract(prob, grad, 1, 0) for prob, grad in zip(probs, grads)]
        for pair, near, grad_query, grad_key, grad_val in zip(
            pairs, nears, grad_queries, grad_keys, grad_vals
        ):
            for half in range(2):
                place = pl.ds(pl.multiple_of((2 * pair + half) * tile_rows, tile_rows), tile_rows)
                gq_all[place, :] = diagonal(grad_query, half, tile_rows, width).astype(jnp.bfloat16)
                for n in range(neighbours):
                    at = (slice(n * tile_rows, (n + 1) * tile_rows), slice(half * width, (half + 1) * width))
                    place = pl.ds(pl.multiple_of(near[half][n] * tile_rows, tile_rows), tile_rows)
                    gk_acc[place, :] += grad_key[at]
                    gv_acc[place, :] += grad_val[at]
        return carry

    lax.fori_loop(0, tile_count // 2 // GROUP, body, 0)
    for at, out in enumerate(outs):
        part = slice(at * out.shape[1], (at + 1) * out.shape[1])
        out[0] = gq_all[part, :]
        out[1] = (gk_acc[part, :] * factor).astype(jnp.bfloat16)
        out[2] = gv_acc[part, :].astype(jnp.bfloat16)


def backward(place, tile_pairs, packs, own_grads, other_grads, probs):
    _, rows, local_width = packs[0].shape
    heads = local_width // HEAD_DIM
    clip_rows = rows * SEQ
    grad_spec = pl.BlockSpec((own_grads[0].shape[0], HEAD_DIM), lambda h: (0, h))
    bf16_rows = pltpu.VMEM((clip_rows, HEAD_DIM), jnp.bfloat16)
    f32_rows = pltpu.VMEM((clip_rows, HEAD_DIM), jnp.float32)
    return pl.pallas_call(
        backward_kernel,
        grid=(heads,),
        in_specs=[smem()] * 2
        + [spec for spec in pack_specs(rows) for _ in packs]
        + [grad_spec] * (2 * SEQ)
        + [pl.BlockSpec((1,) + probs.shape[1:], lambda h: (h, 0, 0))],
        out_specs=[pl.BlockSpec((3, rows, HEAD_DIM), lambda h: (0, 0, h))] * SEQ,
        out_shape=[jax.ShapeDtypeStruct((3, rows, local_width), jnp.bfloat16)] * SEQ,
        scratch_shapes=[bf16_rows] * 5 + [f32_rows] * 2,
        compiler_params=params(),
        name="attention_backward",
    )(place, tile_pairs, *packs, *packs, *packs, *own_grads, *other_grads, probs)


def weight_grad_kernel(place_ref, mean, side, att_ref, *refs):
    own, other, outs = refs[:SEQ], refs[SEQ : 2 * SEQ], refs[2 * SEQ :]
    pieces, second = outs[:-1], outs[-1]
    half_rows = own[0].shape[0]
    core = place_ref[1]
    columns, attended = [], []
    for at in range(SEQ):
        for part, half in ((own[at], core), (other[at ^ 1], 1 - core)):
            columns.append(part[...])
            start = pl.multiple_of((2 * at + half) * half_rows, half_rows)
            attended.append(att_ref[pl.ds(start, half_rows), :])
    total = contract(jnp.concatenate(columns, axis=0), jnp.concatenate(attended, axis=0), 0, 0)
    total = (total * mean).astype(jnp.bfloat16)
    count, piece = second.shape[:2]
    step = pl.program_id(0)
    for at in range(count):
        start = 2 * at * piece
        second[at] = total[start + piece : start + 2 * piece]
        owner = step * count + at
        ahead = lax.rem(owner + side - place_ref[4], side)
        for by, out in enumerate(pieces):

            @pl.when(ahead == by)
            def _(out=out, start=start, owner=owner):
                out[owner // side] = total[start : start + piece]


def weight_grad(place, attended, own, other, mean, side, block=640):
    half_rows, features = own[0].shape
    local_width = attended.shape[1]
    piece = features // (side * side) // CORES
    return pl.pallas_call(
        lambda place_ref, *refs: weight_grad_kernel(place_ref, mean, side, *refs),
        grid=(features // block,),
        in_specs=[smem(), pl.BlockSpec(attended.shape, lambda i: (0, 0))]
        + [pl.BlockSpec((half_rows, block), lambda i: (0, i))] * (2 * SEQ),
        out_specs=[pl.BlockSpec((side, piece, local_width), lambda i: (0, 0, 0))] * side
        + [pl.BlockSpec((block // piece // 2, piece, local_width), lambda i: (i, 0, 0))],
        out_shape=[jax.ShapeDtypeStruct((side, piece, local_width), jnp.bfloat16)] * side
        + [jax.ShapeDtypeStruct((side * side, piece, local_width), jnp.bfloat16)],
        compiler_params=params(),
        name="weight_grad",
    )(place, attended, *own, *other)


def device_of(core, seq):
    return core * SEQ + seq


def outward(round_):
    pairs = []
    for core in range(CORES):
        for token in range(SEQ):
            shard = token ^ round_
            pairs.append((device_of(core, token), device_of(shard % 2, 2 * core + shard // 2)))
    return pairs


def inward(round_):
    return [(target, source) for source, target in outward(round_)]


def send(value, pairs):
    others = [pair for pair in pairs if pair[0] != pair[1]]
    got = lax.ppermute(value, ("core", "seq"), others)
    mine = [source for source, target in pairs if source == target]
    if not mine:
        return got
    here = device_of(lax.axis_index("core"), lax.axis_index("seq"))
    keep = functools.reduce(jnp.logical_or, [here == one for one in mine])
    return jnp.where(keep, value, got)


def swap_cores(value):
    return lax.ppermute(value, "core", [(0, 1), (1, 0)])


def shift(value, axis, by):
    count = lax.axis_size(axis)
    return lax.ppermute(value, axis, [(i, (i + by) % count) for i in range(count)])


def add(*terms):
    total = terms[0].astype(jnp.float32)
    for term in terms[1:]:
        total = total + term.astype(jnp.float32)
    return total.astype(jnp.bfloat16)


def take(value, index, axis=0):
    return lax.dynamic_index_in_dim(value, index, axis, keepdims=False)


def scatter(value, axis, dim=0):
    here = lax.axis_index(axis)
    count = lax.axis_size(axis)
    got = [shift(take(value, (here + by) % count, dim), axis, by) for by in (2, 1, 3)]
    return [take(value, here, dim)] + got


def to_shard_holders(w_out, seq, token):
    got = []
    for other in range(2):
        pairs = []
        for holder in range(CORES):
            for shard in range(SEQ):
                window = holder ^ other
                pairs.append((device_of(holder, shard), device_of(shard % 2, shard // 2 + 2 * window)))
        got.append(send(w_out, pairs))
    window = seq // 2
    got = after(got, token)
    return jnp.where(window == 0, jnp.concatenate(got), jnp.concatenate(got[::-1]))


def to_owners(totals, seq):
    window = seq // 2
    got = []
    for other in range(2):
        pairs = []
        for core in range(CORES):
            for at in range(SEQ):
                holder = (at // 2) ^ other
                pairs.append((device_of(core, at), device_of(holder, 2 * (at % 2) + core)))
        got.append(send(jnp.where((window ^ other) == 0, totals[0], totals[1]), pairs))
    return got[0].astype(jnp.float32) + got[1].astype(jnp.float32)


def after(values, *tokens):
    return lax.optimization_barrier((values, tokens))[0]


def per_device(queries, keys, values, gain_q, gain_k, tile_pairs, tile_lens, out_grad, w_out):
    core = lax.axis_index("core")
    seq = lax.axis_index("seq")
    count_z = lax.axis_size("z")
    count_x = lax.axis_size("x")
    rows, features = out_grad.shape
    shard = 2 * (seq % 2) + core
    tiles_per_block = tile_pairs.shape[0] // SEQ
    place = jnp.stack([seq, core, shard, shard * tiles_per_block, lax.axis_index("x")]).astype(jnp.int32)
    lens = jnp.where(seq // 2 == core, tile_lens, swap_cores(tile_lens))

    def half_rows(rows_in, round_):
        half = seq % 2 if round_ % 2 == 0 else 1 - seq % 2
        return take(rows_in.reshape(2, rows // 2, features), half)

    parts = to_rounds(place, queries, keys, values, gain_q, gain_k)
    w_rows = to_shard_holders(w_out, seq, parts[0])
    w_all = lax.all_gather(w_rows, ("z", "x"), axis=0, tiled=True)
    packs = {r: send(parts[r], outward(r)) for r in ORDER}
    came = [packs[r] for r in ORDER]
    own = {}
    for r in ORDER:
        own[r] = send(half_rows(after(out_grad, came), r), outward(r))
    packs = [packs[r] for r in range(SEQ)]

    def project(part):
        return jnp.dot(part, w_all, preferred_element_type=jnp.float32).astype(jnp.bfloat16)

    attended, probs = forward(place, tile_pairs, lens, packs)
    one, two, three, last = ORDER
    other = {one: swap_cores(own[one]), two: swap_cores(after(own[two], attended))}
    own_grads = {one: project(own[one]), two: project(own[two])}
    other_grads = {one: project(other[one]), two: project(other[two])}
    other[three] = swap_cores(after(own[three], own_grads[one], other_grads[one]))
    own_grads[three], other_grads[three] = project(own[three]), project(other[three])
    done = ([own_grads[r] for r in ORDER[:-1]], [other_grads[r] for r in ORDER[:-2]])
    other[last] = swap_cores(after(own[last], *done))
    own_grads[last] = project(own[last])
    other_grads[last] = project(other[last])
    attended = after(attended, own_grads, other_grads)
    own, other, own_grads, other_grads = [
        [table[r] for r in range(SEQ)] for table in (own, other, own_grads, other_grads)
    ]
    *one, two = weight_grad(place, attended, own, other, 1.0 / (count_z * count_x * CORES), count_x)
    two = lax.psum_scatter(two, "z", scatter_dimension=0, tiled=True)
    token = one[0]
    one = [one[0]] + [shift(one[by], "x", by) for by in (2, 1, 3)]
    parts = backward(place, tile_pairs, packs, own_grads, other_grads, after(probs, token))
    one = add(*after(one, parts[0]))
    two = lax.optimization_barrier(add(*scatter(after(two, one), "x")))
    one = lax.optimization_barrier(add(*scatter(one, "z")))
    parts = {r: send(parts[r] if r in ORDER[:2] else after(parts[r], two), inward(r)) for r in ORDER}
    grad_w = to_owners((one, two), seq)
    grad_q, grad_k, grad_v = finish(
        place, queries, keys, gain_q, gain_k, [parts[r] for r in range(SEQ)]
    )
    return (grad_q, grad_k, grad_v, grad_w)


def solution(mesh):
    dp = mesh.shape["dp"]
    side = math.isqrt(dp // CORES)
    parts = Mesh(mesh.devices.reshape(side, side, CORES, SEQ), ("z", "x", "core", "seq"))
    dp_axes = ("z", "x", "core")
    tokens = P(dp_axes + ("seq",), None)
    return jax.shard_map(
        per_device,
        mesh=parts,
        in_specs=(tokens, tokens, tokens, P(), P(), P(), P(dp_axes, None), tokens, P(dp_axes, "seq")),
        out_specs=(tokens, tokens, tokens, P(dp_axes, "seq")),
        check_vma=False,
    )
```

```python
import functools
import math

import jax
import jax.numpy as jnp
from jax import lax
from jax.experimental import pallas as pl
from jax.experimental.pallas import tpu as pltpu
from jax.sharding import Mesh, PartitionSpec as P

HEAD_DIM = 128


EPS = 1e-06
LOG2E = 1.4426950408889634
MIN_LIVE = 40
SEQ = 4
CORES = 2
GROUP = 4
ORDER = (0, 3, 1, 2)


def smem():
    return pl.BlockSpec(memory_space=pltpu.SMEM)


def params():
    return pltpu.CompilerParams(vmem_limit_bytes=48 << 20)


def contract(left, right, left_dim, right_dim):
    return lax.dot_general(
        left, right, (((left_dim,), (right_dim,)), ((), ())), preferred_element_type=jnp.float32
    )


def row_scale_of(values_f):
    return lax.rsqrt(jnp.mean(values_f * values_f, axis=-1, keepdims=True) + EPS)


def shard_of(place_ref, round_, width):
    return pl.ds(pl.multiple_of(jnp.bitwise_xor(place_ref[0], round_) * width, 128), width)


def rounds_kernel(place_ref, q_ref, k_ref, v_ref, gain_q_ref, gain_k_ref, *refs):
    outs, normed = refs[:-1], refs[-1]
    for at, (x_ref, gain_ref) in enumerate(((q_ref, gain_q_ref), (k_ref, gain_k_ref))):
        values_f = x_ref[...].astype(jnp.float32)
        normed[at] = (values_f * row_scale_of(values_f) * gain_ref[...][None, :]).astype(jnp.bfloat16)
    for round_, out in enumerate(outs):
        columns = shard_of(place_ref, round_, out.shape[2])
        out[0] = normed[0, :, columns]
        out[1] = normed[1, :, columns]
        out[2] = v_ref[:, columns]


def to_rounds(place, queries, keys, values, gain_q, gain_k, block=64):
    rows, width = queries.shape
    row_spec = pl.BlockSpec((block, width), lambda i: (i, 0))
    gain_spec = pl.BlockSpec((width,), lambda i: (0,))
    return pl.pallas_call(
        rounds_kernel,
        grid=(rows // block,),
        in_specs=[smem()] + [row_spec] * 3 + [gain_spec] * 2,
        out_specs=[pl.BlockSpec((3, block, width // SEQ), lambda i: (0, i, 0))] * SEQ,
        out_shape=[jax.ShapeDtypeStruct((3, rows, width // SEQ), jnp.bfloat16)] * SEQ,
        scratch_shapes=[pltpu.VMEM((2, block, width), jnp.bfloat16)],
        name="norm_rows",
    )(place, queries, keys, values, gain_q, gain_k)


def finish_kernel(place_ref, q_ref, k_ref, gain_q_ref, gain_k_ref, *refs):
    parts, outs, joined = refs[:SEQ], refs[SEQ:-1], refs[-1]
    width = q_ref.shape[1]
    for round_, part in enumerate(parts):
        columns = shard_of(place_ref, round_, part.shape[2])
        joined[0, :, columns] = part[0]
        joined[1, :, columns] = part[1]
        outs[2][:, columns] = part[2]
    for at, (x_ref, gain_ref) in enumerate(((q_ref, gain_q_ref), (k_ref, gain_k_ref))):
        values_f = x_ref[...].astype(jnp.float32)
        row_scale = row_scale_of(values_f)
        gated = gain_ref[...][None, :] * joined[at].astype(jnp.float32)
        inner = jnp.sum(gated * values_f, axis=-1, keepdims=True)
        back = values_f * (row_scale * row_scale * row_scale * inner * (1.0 / width))
        outs[at][...] = (row_scale * gated - back).astype(jnp.bfloat16)


def finish(place, queries, keys, gain_q, gain_k, parts, block=64):
    rows, width = queries.shape
    row_spec = pl.BlockSpec((block, width), lambda i: (i, 0))
    gain_spec = pl.BlockSpec((width,), lambda i: (0,))
    return pl.pallas_call(
        finish_kernel,
        grid=(rows // block,),
        in_specs=[smem()]
        + [row_spec] * 2
        + [gain_spec] * 2
        + [pl.BlockSpec((3, block, width // SEQ), lambda i: (0, i, 0))] * SEQ,
        out_specs=[row_spec] * 3,
        out_shape=[jax.ShapeDtypeStruct((rows, width), jnp.bfloat16)] * 3,
        scratch_shapes=[pltpu.VMEM((2, block, width), jnp.bfloat16)],
        name="norm_back",
    )(place, queries, keys, gain_q, gain_k, *parts)


def tile_at(ref, index, rows):
    return ref[pl.ds(pl.multiple_of(index * rows, rows), rows), :]


def gather_pair(ref, near, rows):
    return jnp.concatenate(
        [
            jnp.concatenate([tile_at(ref, one, rows), tile_at(ref, two, rows)], axis=1)
            for one, two in zip(*near)
        ],
        axis=0,
    )


def spread(block, rows):
    twice = jnp.concatenate([block, block], axis=1)
    width = block.shape[1]
    own = (lax.broadcasted_iota(jnp.int32, twice.shape, 0) < rows) == (
        lax.broadcasted_iota(jnp.int32, twice.shape, 1) < width
    )
    return jnp.where(own, twice, jnp.zeros_like(twice))


def near_of(place_ref, pairs_ref, pair):
    flip = place_ref[3]
    return [
        [
            jnp.bitwise_xor(pairs_ref[jnp.bitwise_xor(2 * pair + half, flip), n], flip)
            for n in range(pairs_ref.shape[1])
        ]
        for half in range(2)
    ]


def load_parts(parts, whole):
    for at, part in enumerate(parts):
        whole[at * part.shape[0] : (at + 1) * part.shape[0], :] = part[...]


def diagonal(product, half, tile_rows, width):
    return product[half * tile_rows : (half + 1) * tile_rows, half * width : (half + 1) * width]


def forward_kernel(place_ref, pairs_ref, lens_ref, *refs):
    q_parts, k_parts, v_parts = refs[:SEQ], refs[SEQ : 2 * SEQ], refs[2 * SEQ : 3 * SEQ]
    att_ref, probs_ref, q_all, k_all, v_all = refs[3 * SEQ :]
    tile_count, neighbours = pairs_ref.shape
    clip_rows, width = q_all.shape
    tile_rows = clip_rows // tile_count
    rows = 2 * tile_rows
    depth = neighbours * tile_rows
    scale = LOG2E / math.sqrt(width)
    load_parts(q_parts, q_all)
    load_parts(k_parts, k_all)
    load_parts(v_parts, v_all)
    shape = (tile_rows - MIN_LIVE, rows)
    first = lax.broadcasted_iota(jnp.int32, shape, 1) < tile_rows
    slot = lax.broadcasted_iota(jnp.int32, shape, 0) + MIN_LIVE

    def length(tile):
        return lens_ref[0, jnp.bitwise_xor(tile, place_ref[3])]

    def score(pair, near):
        keys = gather_pair(k_all, near, tile_rows)
        queries = spread(q_all[pl.ds(pl.multiple_of(pair * rows, rows), rows), :], tile_rows)
        scores = contract(keys, queries, 1, 1)
        pieces = []
        for n in range(neighbours):
            start = n * tile_rows
            pieces.append(scores[start : start + MIN_LIVE])
            live = slot < jnp.where(first, length(near[0][n]), length(near[1][n]))
            pieces.append(jnp.where(live, scores[start + MIN_LIVE : start + tile_rows], -jnp.inf))
        return jnp.concatenate(pieces, axis=0)

    def soften(scores):
        weights = jnp.exp2((scores - jnp.max(scores, axis=0, keepdims=True)) * scale)
        return (weights * (1.0 / jnp.sum(weights, axis=0, keepdims=True))).astype(jnp.bfloat16)

    def body(group, carry):
        pairs = [group * GROUP + at for at in range(GROUP)]
        nears = [near_of(place_ref, pairs_ref, pair) for pair in pairs]
        probs = [soften(score(pair, near)) for pair, near in zip(pairs, nears)]
        attended = [
            contract(prob, gather_pair(v_all, near, tile_rows), 0, 0) for prob, near in zip(probs, nears)
        ]
        for pair, prob, product in zip(pairs, probs, attended):
            probs_ref[0, pl.ds(pl.multiple_of(pair * depth, depth), depth), :] = prob
            for half in range(2):
                place = pl.ds(pl.multiple_of((2 * pair + half) * tile_rows, tile_rows), tile_rows)
                att_ref[place, :] = diagonal(product, half, tile_rows, width).astype(jnp.bfloat16)
        return carry

    lax.fori_loop(0, tile_count // 2 // GROUP, body, 0)


def pack_specs(rows):
    return [pl.BlockSpec((None, rows, HEAD_DIM), lambda h, which=which: (which, 0, h)) for which in range(3)]


def forward(place, tile_pairs, lens, packs):
    _, rows, local_width = packs[0].shape
    heads = local_width // HEAD_DIM
    clip_rows = rows * SEQ
    pairs = tile_pairs.shape[0] // 2
    depth = tile_pairs.shape[1] * (clip_rows // tile_pairs.shape[0])
    return pl.pallas_call(
        forward_kernel,
        grid=(heads,),
        in_specs=[smem()] * 3 + [spec for spec in pack_specs(rows) for _ in packs],
        out_specs=[
            pl.BlockSpec((clip_rows, HEAD_DIM), lambda h: (0, h)),
            pl.BlockSpec((1, pairs * depth, HEAD_DIM), lambda h: (h, 0, 0)),
        ],
        out_shape=[
            jax.ShapeDtypeStruct((clip_rows, local_width), jnp.bfloat16),
            jax.ShapeDtypeStruct((heads, pairs * depth, HEAD_DIM), jnp.bfloat16),
        ],
        scratch_shapes=[pltpu.VMEM((clip_rows, HEAD_DIM), jnp.bfloat16)] * 3,
        compiler_params=params(),
        name="attention_forward",
    )(place, tile_pairs, lens, *packs, *packs, *packs)


def backward_kernel(place_ref, pairs_ref, *refs):
    q_parts, k_parts, v_parts = refs[:SEQ], refs[SEQ : 2 * SEQ], refs[2 * SEQ : 3 * SEQ]
    g_all, probs_ref = refs[3 * SEQ : 3 * SEQ + 2]
    outs = refs[3 * SEQ + 2 : 4 * SEQ + 2]
    q_all, k_all, v_all, gq_all, gk_acc, gv_acc = refs[4 * SEQ + 2 :]
    tile_count, neighbours = pairs_ref.shape
    clip_rows, width = q_all.shape
    tile_rows = clip_rows // tile_count
    rows = 2 * tile_rows
    depth = neighbours * tile_rows
    factor = 1.0 / math.sqrt(width)
    load_parts(q_parts, q_all)
    load_parts(k_parts, k_all)
    load_parts(v_parts, v_all)
    gk_acc[...] = jnp.zeros_like(gk_acc)
    gv_acc[...] = jnp.zeros_like(gv_acc)

    def rows_of(pair):
        return pl.ds(pl.multiple_of(pair * rows, rows), rows)

    def body(group, carry):
        pairs = [group * GROUP + at for at in range(GROUP)]
        nears = [near_of(place_ref, pairs_ref, pair) for pair in pairs]
        probs = [
            probs_ref[0, pl.ds(pl.multiple_of(pair * depth, depth), depth), :] for pair in pairs
        ]
        grads = [spread(g_all[rows_of(pair), :], tile_rows) for pair in pairs]
        grad_scores = []
        for prob, grad, near in zip(probs, grads, nears):
            grad_prob = contract(gather_pair(v_all, near, tile_rows), grad, 1, 1)
            wide = prob.astype(jnp.float32)
            delta = jnp.sum(wide * grad_prob, axis=0, keepdims=True)
            grad_scores.append((wide * (grad_prob - delta)).astype(jnp.bfloat16))
        grad_queries = [
            contract(grad_score, gather_pair(k_all, near, tile_rows), 0, 0) * factor
            for grad_score, near in zip(grad_scores, nears)
        ]
        grad_keys = [
            contract(grad_score, spread(q_all[rows_of(pair), :], tile_rows), 1, 0)
            for grad_score, pair in zip(grad_scores, pairs)
        ]
        grad_vals = [contract(prob, grad, 1, 0) for prob, grad in zip(probs, grads)]
        for pair, near, grad_query, grad_key, grad_val in zip(
            pairs, nears, grad_queries, grad_keys, grad_vals
        ):
            for half in range(2):
                place = pl.ds(pl.multiple_of((2 * pair + half) * tile_rows, tile_rows), tile_rows)
                gq_all[place, :] = diagonal(grad_query, half, tile_rows, width).astype(jnp.bfloat16)
                for n in range(neighbours):
                    at = (slice(n * tile_rows, (n + 1) * tile_rows), slice(half * width, (half + 1) * width))
                    place = pl.ds(pl.multiple_of(near[half][n] * tile_rows, tile_rows), tile_rows)
                    gk_acc[place, :] += grad_key[at]
                    gv_acc[place, :] += grad_val[at]
        return carry

    lax.fori_loop(0, tile_count // 2 // GROUP, body, 0)
    for at, out in enumerate(outs):
        part = slice(at * out.shape[1], (at + 1) * out.shape[1])
        out[0] = gq_all[part, :]
        out[1] = (gk_acc[part, :] * factor).astype(jnp.bfloat16)
        out[2] = gv_acc[part, :].astype(jnp.bfloat16)


def backward(place, tile_pairs, packs, grads, probs):
    _, rows, local_width = packs[0].shape
    heads = local_width // HEAD_DIM
    clip_rows = rows * SEQ
    bf16_rows = pltpu.VMEM((clip_rows, HEAD_DIM), jnp.bfloat16)
    f32_rows = pltpu.VMEM((clip_rows, HEAD_DIM), jnp.float32)
    return pl.pallas_call(
        backward_kernel,
        grid=(heads,),
        in_specs=[smem()] * 2
        + [spec for spec in pack_specs(rows) for _ in packs]
        + [pl.BlockSpec((clip_rows, HEAD_DIM), lambda h: (0, h))]
        + [pl.BlockSpec((1,) + probs.shape[1:], lambda h: (h, 0, 0))],
        out_specs=[pl.BlockSpec((3, rows, HEAD_DIM), lambda h: (0, 0, h))] * SEQ,
        out_shape=[jax.ShapeDtypeStruct((3, rows, local_width), jnp.bfloat16)] * SEQ,
        scratch_shapes=[bf16_rows] * 4 + [f32_rows] * 2,
        compiler_params=params(),
        name="attention_backward",
    )(place, tile_pairs, *packs, *packs, *packs, grads, probs)


def project_kernel(place_ref, mean, side, att_ref, w_ref, *refs):
    own, other = refs[:SEQ], refs[SEQ : 2 * SEQ]
    pieces, second, grad_ref, grad_acc = refs[2 * SEQ : -3], refs[-3], refs[-2], refs[-1]
    half_rows = own[0].shape[0]
    core = place_ref[1]
    columns, starts = [], []
    for at in range(SEQ):
        for part, half in ((own[at], core), (other[at ^ 1], 1 - core)):
            columns.append(part[...])
            starts.append(pl.multiple_of((2 * at + half) * half_rows, half_rows))
    columns = jnp.concatenate(columns, axis=0)
    attended = jnp.concatenate([att_ref[pl.ds(start, half_rows), :] for start in starts], axis=0)
    step = pl.program_id(0)
    product = contract(columns, w_ref[...], 1, 0)

    @pl.when(step == 0)
    def _():
        grad_acc[...] = product

    @pl.when(step > 0)
    def _():
        grad_acc[...] += product

    total = (contract(columns, attended, 0, 0) * mean).astype(jnp.bfloat16)
    count, piece = second.shape[:2]
    for at in range(count):
        start = 2 * at * piece
        second[at] = total[start + piece : start + 2 * piece]
        owner = step * count + at
        ahead = lax.rem(owner + side - place_ref[4], side)
        for by, out in enumerate(pieces):

            @pl.when(ahead == by)
            def _(out=out, start=start, owner=owner):
                out[owner // side] = total[start : start + piece]

    @pl.when(step == pl.num_programs(0) - 1)
    def _():
        for at, start in enumerate(starts):
            part = grad_acc[at * half_rows : (at + 1) * half_rows, :]
            grad_ref[pl.ds(start, half_rows), :] = part.astype(jnp.bfloat16)


def project(place, attended, w_all, own, other, mean, side, block=640):
    half_rows, features = own[0].shape
    clip_rows, local_width = attended.shape
    piece = features // (side * side) // CORES
    whole = pl.BlockSpec((clip_rows, local_width), lambda i: (0, 0))
    return pl.pallas_call(
        lambda place_ref, *refs: project_kernel(place_ref, mean, side, *refs),
        grid=(features // block,),
        in_specs=[smem(), whole, pl.BlockSpec((block, local_width), lambda i: (i, 0))]
        + [pl.BlockSpec((half_rows, block), lambda i: (0, i))] * (2 * SEQ),
        out_specs=[pl.BlockSpec((side, piece, local_width), lambda i: (0, 0, 0))] * side
        + [pl.BlockSpec((block // piece // 2, piece, local_width), lambda i: (i, 0, 0)), whole],
        out_shape=[jax.ShapeDtypeStruct((side, piece, local_width), jnp.bfloat16)] * side
        + [
            jax.ShapeDtypeStruct((side * side, piece, local_width), jnp.bfloat16),
            jax.ShapeDtypeStruct((clip_rows, local_width), jnp.bfloat16),
        ],
        scratch_shapes=[pltpu.VMEM((clip_rows, local_width), jnp.float32)],
        compiler_params=params(),
        name="project_and_weight_grad",
    )(place, attended, w_all, *own, *other)


def device_of(core, seq):
    return core * SEQ + seq


def outward(round_):
    pairs = []
    for core in range(CORES):
        for token in range(SEQ):
            shard = token ^ round_
            pairs.append((device_of(core, token), device_of(shard % 2, 2 * core + shard // 2)))
    return pairs


def inward(round_):
    return [(target, source) for source, target in outward(round_)]


def send(value, pairs):
    others = [pair for pair in pairs if pair[0] != pair[1]]
    got = lax.ppermute(value, ("core", "seq"), others)
    mine = [source for source, target in pairs if source == target]
    if not mine:
        return got
    here = device_of(lax.axis_index("core"), lax.axis_index("seq"))
    keep = functools.reduce(jnp.logical_or, [here == one for one in mine])
    return jnp.where(keep, value, got)


def swap_cores(value):
    return lax.ppermute(value, "core", [(0, 1), (1, 0)])


def shift(value, axis, by):
    count = lax.axis_size(axis)
    return lax.ppermute(value, axis, [(i, (i + by) % count) for i in range(count)])


def add(*terms):
    total = terms[0].astype(jnp.float32)
    for term in terms[1:]:
        total = total + term.astype(jnp.float32)
    return total.astype(jnp.bfloat16)


def take(value, index, axis=0):
    return lax.dynamic_index_in_dim(value, index, axis, keepdims=False)


def scatter(value, axis, dim=0):
    here = lax.axis_index(axis)
    count = lax.axis_size(axis)
    got = [shift(take(value, (here + by) % count, dim), axis, by) for by in (2, 1, 3)]
    return [take(value, here, dim)] + got


def to_shard_holders(w_out, seq, token):
    got = []
    for other in range(2):
        pairs = []
        for holder in range(CORES):
            for shard in range(SEQ):
                window = holder ^ other
                pairs.append((device_of(holder, shard), device_of(shard % 2, shard // 2 + 2 * window)))
        got.append(send(w_out, pairs))
    window = seq // 2
    got = after(got, token)
    return jnp.where(window == 0, jnp.concatenate(got), jnp.concatenate(got[::-1]))


def to_owners(totals, seq):
    window = seq // 2
    got = []
    for other in range(2):
        pairs = []
        for core in range(CORES):
            for at in range(SEQ):
                holder = (at // 2) ^ other
                pairs.append((device_of(core, at), device_of(holder, 2 * (at % 2) + core)))
        got.append(send(jnp.where((window ^ other) == 0, totals[0], totals[1]), pairs))
    return got[0].astype(jnp.float32) + got[1].astype(jnp.float32)


def after(values, *tokens):
    return lax.optimization_barrier((values, tokens))[0]


def per_device(queries, keys, values, gain_q, gain_k, tile_pairs, tile_lens, out_grad, w_out):
    core = lax.axis_index("core")
    seq = lax.axis_index("seq")
    count_z = lax.axis_size("z")
    count_x = lax.axis_size("x")
    rows, features = out_grad.shape
    shard = 2 * (seq % 2) + core
    tiles_per_block = tile_pairs.shape[0] // SEQ
    place = jnp.stack([seq, core, shard, shard * tiles_per_block, lax.axis_index("x")]).astype(jnp.int32)
    lens = jnp.where(seq // 2 == core, tile_lens, swap_cores(tile_lens))

    def half_rows(rows_in, round_):
        half = seq % 2 if round_ % 2 == 0 else 1 - seq % 2
        return take(rows_in.reshape(2, rows // 2, features), half)

    parts = to_rounds(place, queries, keys, values, gain_q, gain_k)
    w_rows = to_shard_holders(w_out, seq, parts[0])
    w_all = lax.all_gather(w_rows, ("z", "x"), axis=0, tiled=True)
    packs = {r: send(parts[r], outward(r)) for r in ORDER}
    came = [packs[r] for r in ORDER]
    own = {}
    for r in ORDER:
        own[r] = send(half_rows(after(out_grad, came), r), outward(r))
    packs = [packs[r] for r in range(SEQ)]

    attended, probs = forward(place, tile_pairs, lens, packs)
    other = {r: swap_cores(own[r] if r == ORDER[0] else after(own[r], attended)) for r in ORDER}
    own, other = [[table[r] for r in range(SEQ)] for table in (own, other)]
    *one, two, grads = project(
        place, attended, w_all, own, other, 1.0 / (count_z * count_x * CORES), count_x
    )
    two = lax.psum_scatter(two, "z", scatter_dimension=0, tiled=True)
    token = one[0]
    one = [one[0]] + [shift(one[by], "x", by) for by in (2, 1, 3)]
    parts = backward(place, tile_pairs, packs, grads, after(probs, token))
    one = add(*after(one, parts[0]))
    sent = {r: send(parts[r], inward(r)) for r in ORDER}
    two = lax.optimization_barrier(add(*scatter(after(two, [sent[r] for r in ORDER[:2]]), "x")))
    one = lax.optimization_barrier(add(*scatter(after(one, [sent[r] for r in ORDER[:2]]), "z")))
    parts = sent
    grad_w = to_owners((one, two), seq)
    grad_q, grad_k, grad_v = finish(
        place, queries, keys, gain_q, gain_k, [parts[r] for r in range(SEQ)]
    )
    return (grad_q, grad_k, grad_v, grad_w)


def solution(mesh):
    dp = mesh.shape["dp"]
    side = math.isqrt(dp // CORES)
    parts = Mesh(mesh.devices.reshape(side, side, CORES, SEQ), ("z", "x", "core", "seq"))
    dp_axes = ("z", "x", "core")
    tokens = P(dp_axes + ("seq",), None)
    return jax.shard_map(
        per_device,
        mesh=parts,
        in_specs=(tokens, tokens, tokens, P(), P(), P(), P(dp_axes, None), tokens, P(dp_axes, "seq")),
        out_specs=(tokens, tokens, tokens, P(dp_axes, "seq")),
        check_vma=False,
    )
```

```python
import functools
import math

import jax
import jax.numpy as jnp
from jax import lax
from jax.experimental import pallas as pl
from jax.experimental.pallas import tpu as pltpu
from jax.sharding import Mesh, PartitionSpec as P

HEAD_DIM = 128


EPS = 1e-06
LOG2E = 1.4426950408889634
MIN_LIVE = 40
SEQ = 4
CORES = 2
GROUP = 4
ORDER = (0, 3, 1, 2)


def smem():
    return pl.BlockSpec(memory_space=pltpu.SMEM)


def params():
    return pltpu.CompilerParams(vmem_limit_bytes=48 << 20)


def contract(left, right, left_dim, right_dim):
    return lax.dot_general(
        left, right, (((left_dim,), (right_dim,)), ((), ())), preferred_element_type=jnp.float32
    )


def row_scale_of(values_f):
    return lax.rsqrt(jnp.mean(values_f * values_f, axis=-1, keepdims=True) + EPS)


def shard_of(place_ref, round_, width):
    return pl.ds(pl.multiple_of(jnp.bitwise_xor(place_ref[0], round_) * width, 128), width)


def rounds_kernel(place_ref, q_ref, k_ref, v_ref, gain_q_ref, gain_k_ref, *refs):
    outs, normed = refs[:-1], refs[-1]
    for at, (x_ref, gain_ref) in enumerate(((q_ref, gain_q_ref), (k_ref, gain_k_ref))):
        values_f = x_ref[...].astype(jnp.float32)
        normed[at] = (values_f * row_scale_of(values_f) * gain_ref[...][None, :]).astype(jnp.bfloat16)
    for round_, out in enumerate(outs):
        columns = shard_of(place_ref, round_, out.shape[2])
        out[0] = normed[0, :, columns]
        out[1] = normed[1, :, columns]
        out[2] = v_ref[:, columns]


def to_rounds(place, queries, keys, values, gain_q, gain_k, block=64):
    rows, width = queries.shape
    row_spec = pl.BlockSpec((block, width), lambda i: (i, 0))
    gain_spec = pl.BlockSpec((width,), lambda i: (0,))
    return pl.pallas_call(
        rounds_kernel,
        grid=(rows // block,),
        in_specs=[smem()] + [row_spec] * 3 + [gain_spec] * 2,
        out_specs=[pl.BlockSpec((3, block, width // SEQ), lambda i: (0, i, 0))] * SEQ,
        out_shape=[jax.ShapeDtypeStruct((3, rows, width // SEQ), jnp.bfloat16)] * SEQ,
        scratch_shapes=[pltpu.VMEM((2, block, width), jnp.bfloat16)],
        name="norm_rows",
    )(place, queries, keys, values, gain_q, gain_k)


def finish_kernel(place_ref, q_ref, k_ref, gain_q_ref, gain_k_ref, *refs):
    parts, outs, joined = refs[:SEQ], refs[SEQ:-1], refs[-1]
    width = q_ref.shape[1]
    for round_, part in enumerate(parts):
        columns = shard_of(place_ref, round_, part.shape[2])
        joined[0, :, columns] = part[0]
        joined[1, :, columns] = part[1]
        outs[2][:, columns] = part[2]
    for at, (x_ref, gain_ref) in enumerate(((q_ref, gain_q_ref), (k_ref, gain_k_ref))):
        values_f = x_ref[...].astype(jnp.float32)
        row_scale = row_scale_of(values_f)
        gated = gain_ref[...][None, :] * joined[at].astype(jnp.float32)
        inner = jnp.sum(gated * values_f, axis=-1, keepdims=True)
        back = values_f * (row_scale * row_scale * row_scale * inner * (1.0 / width))
        outs[at][...] = (row_scale * gated - back).astype(jnp.bfloat16)


def finish(place, queries, keys, gain_q, gain_k, parts, block=64):
    rows, width = queries.shape
    row_spec = pl.BlockSpec((block, width), lambda i: (i, 0))
    gain_spec = pl.BlockSpec((width,), lambda i: (0,))
    return pl.pallas_call(
        finish_kernel,
        grid=(rows // block,),
        in_specs=[smem()]
        + [row_spec] * 2
        + [gain_spec] * 2
        + [pl.BlockSpec((3, block, width // SEQ), lambda i: (0, i, 0))] * SEQ,
        out_specs=[row_spec] * 3,
        out_shape=[jax.ShapeDtypeStruct((rows, width), jnp.bfloat16)] * 3,
        scratch_shapes=[pltpu.VMEM((2, block, width), jnp.bfloat16)],
        name="norm_back",
    )(place, queries, keys, gain_q, gain_k, *parts)


def tile_at(ref, index, rows):
    return ref[pl.ds(pl.multiple_of(index * rows, rows), rows), :]


def gather_pair(ref, near, rows):
    return jnp.concatenate(
        [
            jnp.concatenate([tile_at(ref, one, rows), tile_at(ref, two, rows)], axis=1)
            for one, two in zip(*near)
        ],
        axis=0,
    )


def spread(block, rows):
    twice = jnp.concatenate([block, block], axis=1)
    width = block.shape[1]
    own = (lax.broadcasted_iota(jnp.int32, twice.shape, 0) < rows) == (
        lax.broadcasted_iota(jnp.int32, twice.shape, 1) < width
    )
    return jnp.where(own, twice, jnp.zeros_like(twice))


def near_of(place_ref, pairs_ref, pair):
    flip = place_ref[3]
    return [
        [
            jnp.bitwise_xor(pairs_ref[jnp.bitwise_xor(2 * pair + half, flip), n], flip)
            for n in range(pairs_ref.shape[1])
        ]
        for half in range(2)
    ]


def load_parts(parts, whole):
    for at, part in enumerate(parts):
        whole[at * part.shape[0] : (at + 1) * part.shape[0], :] = part[...]


def diagonal(product, half, tile_rows, width):
    return product[half * tile_rows : (half + 1) * tile_rows, half * width : (half + 1) * width]


def forward_kernel(place_ref, pairs_ref, lens_ref, *refs):
    q_parts, k_parts, v_parts = refs[:SEQ], refs[SEQ : 2 * SEQ], refs[2 * SEQ : 3 * SEQ]
    att_ref, probs_ref, q_all, k_all, v_all = refs[3 * SEQ :]
    tile_count, neighbours = pairs_ref.shape
    clip_rows, width = q_all.shape
    tile_rows = clip_rows // tile_count
    rows = 2 * tile_rows
    depth = neighbours * tile_rows
    scale = LOG2E / math.sqrt(width)
    load_parts(q_parts, q_all)
    load_parts(k_parts, k_all)
    load_parts(v_parts, v_all)
    shape = (tile_rows - MIN_LIVE, rows)
    first = lax.broadcasted_iota(jnp.int32, shape, 1) < tile_rows
    slot = lax.broadcasted_iota(jnp.int32, shape, 0) + MIN_LIVE

    def length(tile):
        return lens_ref[0, jnp.bitwise_xor(tile, place_ref[3])]

    def score(pair, near):
        keys = gather_pair(k_all, near, tile_rows)
        queries = spread(q_all[pl.ds(pl.multiple_of(pair * rows, rows), rows), :], tile_rows)
        scores = contract(keys, queries, 1, 1)
        pieces = []
        for n in range(neighbours):
            start = n * tile_rows
            pieces.append(scores[start : start + MIN_LIVE])
            live = slot < jnp.where(first, length(near[0][n]), length(near[1][n]))
            pieces.append(jnp.where(live, scores[start + MIN_LIVE : start + tile_rows], -jnp.inf))
        return jnp.concatenate(pieces, axis=0)

    def soften(scores):
        weights = jnp.exp2((scores - jnp.max(scores, axis=0, keepdims=True)) * scale)
        return (weights * (1.0 / jnp.sum(weights, axis=0, keepdims=True))).astype(jnp.bfloat16)

    def body(group, carry):
        pairs = [group * GROUP + at for at in range(GROUP)]
        nears = [near_of(place_ref, pairs_ref, pair) for pair in pairs]
        probs = [soften(score(pair, near)) for pair, near in zip(pairs, nears)]
        attended = [
            contract(prob, gather_pair(v_all, near, tile_rows), 0, 0) for prob, near in zip(probs, nears)
        ]
        for pair, prob, product in zip(pairs, probs, attended):
            probs_ref[0, pl.ds(pl.multiple_of(pair * depth, depth), depth), :] = prob
            for half in range(2):
                place = pl.ds(pl.multiple_of((2 * pair + half) * tile_rows, tile_rows), tile_rows)
                att_ref[place, :] = diagonal(product, half, tile_rows, width).astype(jnp.bfloat16)
        return carry

    lax.fori_loop(0, tile_count // 2 // GROUP, body, 0)


def pack_specs(rows):
    return [pl.BlockSpec((None, rows, HEAD_DIM), lambda h, which=which: (which, 0, h)) for which in range(3)]


def forward(place, tile_pairs, lens, packs):
    _, rows, local_width = packs[0].shape
    heads = local_width // HEAD_DIM
    clip_rows = rows * SEQ
    pairs = tile_pairs.shape[0] // 2
    depth = tile_pairs.shape[1] * (clip_rows // tile_pairs.shape[0])
    return pl.pallas_call(
        forward_kernel,
        grid=(heads,),
        in_specs=[smem()] * 3 + [spec for spec in pack_specs(rows) for _ in packs],
        out_specs=[
            pl.BlockSpec((clip_rows, HEAD_DIM), lambda h: (0, h)),
            pl.BlockSpec((1, pairs * depth, HEAD_DIM), lambda h: (h, 0, 0)),
        ],
        out_shape=[
            jax.ShapeDtypeStruct((clip_rows, local_width), jnp.bfloat16),
            jax.ShapeDtypeStruct((heads, pairs * depth, HEAD_DIM), jnp.bfloat16),
        ],
        scratch_shapes=[pltpu.VMEM((clip_rows, HEAD_DIM), jnp.bfloat16)] * 3,
        compiler_params=params(),
        name="attention_forward",
    )(place, tile_pairs, lens, *packs, *packs, *packs)


def backward_kernel(place_ref, pairs_ref, *refs):
    q_parts, k_parts, v_parts = refs[:SEQ], refs[SEQ : 2 * SEQ], refs[2 * SEQ : 3 * SEQ]
    own_grads, other_grads = refs[3 * SEQ : 4 * SEQ], refs[4 * SEQ : 5 * SEQ]
    probs_ref = refs[5 * SEQ]
    outs = refs[5 * SEQ + 1 : 6 * SEQ + 1]
    q_all, k_all, v_all, g_all, gq_all, gk_acc, gv_acc = refs[6 * SEQ + 1 :]
    tile_count, neighbours = pairs_ref.shape
    clip_rows, width = q_all.shape
    tile_rows = clip_rows // tile_count
    rows = 2 * tile_rows
    depth = neighbours * tile_rows
    factor = 1.0 / math.sqrt(width)
    load_parts(q_parts, q_all)
    load_parts(k_parts, k_all)
    load_parts(v_parts, v_all)
    half_rows = own_grads[0].shape[0]
    core = place_ref[1]
    for at in range(SEQ):
        for grads, half in ((own_grads[at], core), (other_grads[at ^ 1], 1 - core)):
            g_all[pl.ds(pl.multiple_of((2 * at + half) * half_rows, half_rows), half_rows), :] = grads[...]
    gk_acc[...] = jnp.zeros_like(gk_acc)
    gv_acc[...] = jnp.zeros_like(gv_acc)

    def rows_of(pair):
        return pl.ds(pl.multiple_of(pair * rows, rows), rows)

    def body(group, carry):
        pairs = [group * GROUP + at for at in range(GROUP)]
        nears = [near_of(place_ref, pairs_ref, pair) for pair in pairs]
        probs = [
            probs_ref[0, pl.ds(pl.multiple_of(pair * depth, depth), depth), :] for pair in pairs
        ]
        grads = [spread(g_all[rows_of(pair), :], tile_rows) for pair in pairs]
        grad_scores = []
        for prob, grad, near in zip(probs, grads, nears):
            grad_prob = contract(gather_pair(v_all, near, tile_rows), grad, 1, 1)
            wide = prob.astype(jnp.float32)
            delta = jnp.sum(wide * grad_prob, axis=0, keepdims=True)
            grad_scores.append((wide * (grad_prob - delta)).astype(jnp.bfloat16))
        grad_queries = [
            contract(grad_score, gather_pair(k_all, near, tile_rows), 0, 0) * factor
            for grad_score, near in zip(grad_scores, nears)
        ]
        grad_keys = [
            contract(grad_score, spread(q_all[rows_of(pair), :], tile_rows), 1, 0)
            for grad_score, pair in zip(grad_scores, pairs)
        ]
        grad_vals = [contract(prob, grad, 1, 0) for prob, grad in zip(probs, grads)]
        for pair, near, grad_query, grad_key, grad_val in zip(
            pairs, nears, grad_queries, grad_keys, grad_vals
        ):
            for half in range(2):
                place = pl.ds(pl.multiple_of((2 * pair + half) * tile_rows, tile_rows), tile_rows)
                gq_all[place, :] = diagonal(grad_query, half, tile_rows, width).astype(jnp.bfloat16)
                for n in range(neighbours):
                    at = (slice(n * tile_rows, (n + 1) * tile_rows), slice(half * width, (half + 1) * width))
                    place = pl.ds(pl.multiple_of(near[half][n] * tile_rows, tile_rows), tile_rows)
                    gk_acc[place, :] += grad_key[at]
                    gv_acc[place, :] += grad_val[at]
        return carry

    lax.fori_loop(0, tile_count // 2 // GROUP, body, 0)
    for at, out in enumerate(outs):
        part = slice(at * out.shape[1], (at + 1) * out.shape[1])
        out[0] = gq_all[part, :]
        out[1] = (gk_acc[part, :] * factor).astype(jnp.bfloat16)
        out[2] = gv_acc[part, :].astype(jnp.bfloat16)


def backward(place, tile_pairs, packs, own_grads, other_grads, probs):
    _, rows, local_width = packs[0].shape
    heads = local_width // HEAD_DIM
    clip_rows = rows * SEQ
    grad_spec = pl.BlockSpec((own_grads[0].shape[0], HEAD_DIM), lambda h: (0, h))
    bf16_rows = pltpu.VMEM((clip_rows, HEAD_DIM), jnp.bfloat16)
    f32_rows = pltpu.VMEM((clip_rows, HEAD_DIM), jnp.float32)
    return pl.pallas_call(
        backward_kernel,
        grid=(heads,),
        in_specs=[smem()] * 2
        + [spec for spec in pack_specs(rows) for _ in packs]
        + [grad_spec] * (2 * SEQ)
        + [pl.BlockSpec((1,) + probs.shape[1:], lambda h: (h, 0, 0))],
        out_specs=[pl.BlockSpec((3, rows, HEAD_DIM), lambda h: (0, 0, h))] * SEQ,
        out_shape=[jax.ShapeDtypeStruct((3, rows, local_width), jnp.bfloat16)] * SEQ,
        scratch_shapes=[bf16_rows] * 5 + [f32_rows] * 2,
        compiler_params=params(),
        name="attention_backward",
    )(place, tile_pairs, *packs, *packs, *packs, *own_grads, *other_grads, probs)


def weight_grad_kernel(place_ref, mean, side, att_ref, *refs):
    own, other, outs = refs[:SEQ], refs[SEQ : 2 * SEQ], refs[2 * SEQ :]
    pieces, second = outs[:-1], outs[-1]
    half_rows = own[0].shape[0]
    core = place_ref[1]
    columns, attended = [], []
    for at in range(SEQ):
        for part, half in ((own[at], core), (other[at ^ 1], 1 - core)):
            columns.append(part[...])
            start = pl.multiple_of((2 * at + half) * half_rows, half_rows)
            attended.append(att_ref[pl.ds(start, half_rows), :])
    total = contract(jnp.concatenate(columns, axis=0), jnp.concatenate(attended, axis=0), 0, 0)
    total = (total * mean).astype(jnp.bfloat16)
    count, piece = second.shape[:2]
    step = pl.program_id(0)
    for at in range(count):
        start = 2 * at * piece
        second[at] = total[start + piece : start + 2 * piece]
        owner = step * count + at
        ahead = lax.rem(owner + side - place_ref[4], side)
        for by, out in enumerate(pieces):

            @pl.when(ahead == by)
            def _(out=out, start=start, owner=owner):
                out[owner // side] = total[start : start + piece]


def weight_grad(place, attended, own, other, mean, side, block=640):
    half_rows, features = own[0].shape
    local_width = attended.shape[1]
    piece = features // (side * side) // CORES
    return pl.pallas_call(
        lambda place_ref, *refs: weight_grad_kernel(place_ref, mean, side, *refs),
        grid=(features // block,),
        in_specs=[smem(), pl.BlockSpec(attended.shape, lambda i: (0, 0))]
        + [pl.BlockSpec((half_rows, block), lambda i: (0, i))] * (2 * SEQ),
        out_specs=[pl.BlockSpec((side, piece, local_width), lambda i: (0, 0, 0))] * side
        + [pl.BlockSpec((block // piece // 2, piece, local_width), lambda i: (i, 0, 0))],
        out_shape=[jax.ShapeDtypeStruct((side, piece, local_width), jnp.bfloat16)] * side
        + [jax.ShapeDtypeStruct((side * side, piece, local_width), jnp.bfloat16)],
        compiler_params=params(),
        name="weight_grad",
    )(place, attended, *own, *other)


def device_of(core, seq):
    return core * SEQ + seq


def outward(round_):
    pairs = []
    for core in range(CORES):
        for token in range(SEQ):
            shard = token ^ round_
            pairs.append((device_of(core, token), device_of(shard % 2, 2 * core + shard // 2)))
    return pairs


def inward(round_):
    return [(target, source) for source, target in outward(round_)]


def send(value, pairs):
    others = [pair for pair in pairs if pair[0] != pair[1]]
    got = lax.ppermute(value, ("core", "seq"), others)
    mine = [source for source, target in pairs if source == target]
    if not mine:
        return got
    here = device_of(lax.axis_index("core"), lax.axis_index("seq"))
    keep = functools.reduce(jnp.logical_or, [here == one for one in mine])
    return jnp.where(keep, value, got)


def swap_cores(value):
    return lax.ppermute(value, "core", [(0, 1), (1, 0)])


def shift(value, axis, by):
    count = lax.axis_size(axis)
    return lax.ppermute(value, axis, [(i, (i + by) % count) for i in range(count)])


def add(*terms):
    total = terms[0].astype(jnp.float32)
    for term in terms[1:]:
        total = total + term.astype(jnp.float32)
    return total.astype(jnp.bfloat16)


def take(value, index, axis=0):
    return lax.dynamic_index_in_dim(value, index, axis, keepdims=False)


def scatter(value, axis, dim=0):
    here = lax.axis_index(axis)
    count = lax.axis_size(axis)
    got = [shift(take(value, (here + by) % count, dim), axis, by) for by in (2, 1, 3)]
    return [take(value, here, dim)] + got


def to_shard_holders(w_out, seq, token):
    got = []
    for other in range(2):
        pairs = []
        for holder in range(CORES):
            for shard in range(SEQ):
                window = holder ^ other
                pairs.append((device_of(holder, shard), device_of(shard % 2, shard // 2 + 2 * window)))
        got.append(send(w_out, pairs))
    window = seq // 2
    got = after(got, token)
    return jnp.where(window == 0, jnp.concatenate(got), jnp.concatenate(got[::-1]))


def to_owners(totals, seq):
    window = seq // 2
    got = []
    for other in range(2):
        pairs = []
        for core in range(CORES):
            for at in range(SEQ):
                holder = (at // 2) ^ other
                pairs.append((device_of(core, at), device_of(holder, 2 * (at % 2) + core)))
        got.append(send(jnp.where((window ^ other) == 0, totals[0], totals[1]), pairs))
    return got[0].astype(jnp.float32) + got[1].astype(jnp.float32)


def after(values, *tokens):
    return lax.optimization_barrier((values, tokens))[0]


def per_device(queries, keys, values, gain_q, gain_k, tile_pairs, tile_lens, out_grad, w_out):
    core = lax.axis_index("core")
    seq = lax.axis_index("seq")
    count_z = lax.axis_size("z")
    count_x = lax.axis_size("x")
    rows, features = out_grad.shape
    shard = 2 * (seq % 2) + core
    tiles_per_block = tile_pairs.shape[0] // SEQ
    place = jnp.stack([seq, core, shard, shard * tiles_per_block, lax.axis_index("x")]).astype(jnp.int32)
    lens = jnp.where(seq // 2 == core, tile_lens, swap_cores(tile_lens))

    def half_rows(rows_in, round_):
        half = seq % 2 if round_ % 2 == 0 else 1 - seq % 2
        return take(rows_in.reshape(2, rows // 2, features), half)

    parts = to_rounds(place, queries, keys, values, gain_q, gain_k)
    w_rows = to_shard_holders(w_out, seq, parts[0])
    w_all = lax.all_gather(w_rows, ("z", "x"), axis=0, tiled=True)
    packs = {r: send(parts[r], outward(r)) for r in ORDER}
    came = [packs[r] for r in ORDER]
    own = {}
    for r in ORDER:
        own[r] = send(half_rows(after(out_grad, came), r), outward(r))
    packs = [packs[r] for r in range(SEQ)]

    def project(part):
        return jnp.dot(part, w_all, preferred_element_type=jnp.float32).astype(jnp.bfloat16)

    attended, probs = forward(place, tile_pairs, lens, packs)
    one, two, three, last = ORDER
    other = {one: swap_cores(own[one]), two: swap_cores(after(own[two], attended))}
    own_grads = {one: project(own[one]), two: project(own[two])}
    other_grads = {one: project(other[one]), two: project(other[two])}
    other[three] = swap_cores(after(own[three], list(own_grads.values()), list(other_grads.values())))
    own_grads[three], other_grads[three] = project(own[three]), project(other[three])
    done = ([own_grads[r] for r in ORDER[:-1]], [other_grads[r] for r in ORDER[:-2]])
    other[last] = swap_cores(after(own[last], *done))
    own_grads[last] = project(own[last])
    other_grads[last] = project(other[last])
    attended = after(attended, own_grads, other_grads)
    own, other, own_grads, other_grads = [
        [table[r] for r in range(SEQ)] for table in (own, other, own_grads, other_grads)
    ]
    *one, two = weight_grad(place, attended, own, other, 1.0 / (count_z * count_x * CORES), count_x)
    two = lax.psum_scatter(two, "z", scatter_dimension=0, tiled=True)
    token = one[0]
    one = [one[0]] + [shift(one[by], "x", by) for by in (2, 1, 3)]
    parts = backward(place, tile_pairs, packs, own_grads, other_grads, after(probs, token))
    one = add(*after(one, parts[0]))
    parts = {r: send(parts[r] if r in ORDER[:2] else after(parts[r], one), inward(r)) for r in ORDER}
    two = lax.optimization_barrier(add(*scatter(after(two, one), "x")))
    one = lax.optimization_barrier(add(*scatter(one, "z")))
    grad_w = to_owners((one, two), seq)
    grad_q, grad_k, grad_v = finish(
        place, queries, keys, gain_q, gain_k, [parts[r] for r in range(SEQ)]
    )
    return (grad_q, grad_k, grad_v, grad_w)


def solution(mesh):
    dp = mesh.shape["dp"]
    side = math.isqrt(dp // CORES)
    parts = Mesh(mesh.devices.reshape(side, side, CORES, SEQ), ("z", "x", "core", "seq"))
    dp_axes = ("z", "x", "core")
    tokens = P(dp_axes + ("seq",), None)
    return jax.shard_map(
        per_device,
        mesh=parts,
        in_specs=(tokens, tokens, tokens, P(), P(), P(), P(dp_axes, None), tokens, P(dp_axes, "seq")),
        out_specs=(tokens, tokens, tokens, P(dp_axes, "seq")),
        check_vma=False,
    )
```

```python
import functools
import math

import jax
import jax.numpy as jnp
from jax import lax
from jax.experimental import pallas as pl
from jax.experimental.pallas import tpu as pltpu
from jax.sharding import Mesh, PartitionSpec as P

HEAD_DIM = 128


EPS = 1e-06
LOG2E = 1.4426950408889634
MIN_LIVE = 40
SEQ = 4
CORES = 2
GROUP = 4
ORDER = (0, 3, 1, 2)


def smem():
    return pl.BlockSpec(memory_space=pltpu.SMEM)


def params():
    return pltpu.CompilerParams(vmem_limit_bytes=48 << 20)


def contract(left, right, left_dim, right_dim):
    return lax.dot_general(
        left, right, (((left_dim,), (right_dim,)), ((), ())), preferred_element_type=jnp.float32
    )


def row_scale_of(values_f):
    return lax.rsqrt(jnp.mean(values_f * values_f, axis=-1, keepdims=True) + EPS)


def shard_of(place_ref, round_, width):
    return pl.ds(pl.multiple_of(jnp.bitwise_xor(place_ref[0], round_) * width, 128), width)


def rounds_kernel(place_ref, q_ref, k_ref, v_ref, gain_q_ref, gain_k_ref, *refs):
    outs, normed = refs[:-1], refs[-1]
    for at, (x_ref, gain_ref) in enumerate(((q_ref, gain_q_ref), (k_ref, gain_k_ref))):
        values_f = x_ref[...].astype(jnp.float32)
        normed[at] = (values_f * row_scale_of(values_f) * gain_ref[...][None, :]).astype(jnp.bfloat16)
    for round_, out in enumerate(outs):
        columns = shard_of(place_ref, round_, out.shape[2])
        out[0] = normed[0, :, columns]
        out[1] = normed[1, :, columns]
        out[2] = v_ref[:, columns]


def to_rounds(place, queries, keys, values, gain_q, gain_k, block=64):
    rows, width = queries.shape
    row_spec = pl.BlockSpec((block, width), lambda i: (i, 0))
    gain_spec = pl.BlockSpec((width,), lambda i: (0,))
    return pl.pallas_call(
        rounds_kernel,
        grid=(rows // block,),
        in_specs=[smem()] + [row_spec] * 3 + [gain_spec] * 2,
        out_specs=[pl.BlockSpec((3, block, width // SEQ), lambda i: (0, i, 0))] * SEQ,
        out_shape=[jax.ShapeDtypeStruct((3, rows, width // SEQ), jnp.bfloat16)] * SEQ,
        scratch_shapes=[pltpu.VMEM((2, block, width), jnp.bfloat16)],
        name="norm_rows",
    )(place, queries, keys, values, gain_q, gain_k)


def finish_kernel(place_ref, q_ref, k_ref, gain_q_ref, gain_k_ref, *refs):
    parts, outs, joined = refs[:SEQ], refs[SEQ:-1], refs[-1]
    width = q_ref.shape[1]
    for round_, part in enumerate(parts):
        columns = shard_of(place_ref, round_, part.shape[2])
        joined[0, :, columns] = part[0]
        joined[1, :, columns] = part[1]
        outs[2][:, columns] = part[2]
    for at, (x_ref, gain_ref) in enumerate(((q_ref, gain_q_ref), (k_ref, gain_k_ref))):
        values_f = x_ref[...].astype(jnp.float32)
        row_scale = row_scale_of(values_f)
        gated = gain_ref[...][None, :] * joined[at].astype(jnp.float32)
        inner = jnp.sum(gated * values_f, axis=-1, keepdims=True)
        back = values_f * (row_scale * row_scale * row_scale * inner * (1.0 / width))
        outs[at][...] = (row_scale * gated - back).astype(jnp.bfloat16)


def finish(place, queries, keys, gain_q, gain_k, parts, block=64):
    rows, width = queries.shape
    row_spec = pl.BlockSpec((block, width), lambda i: (i, 0))
    gain_spec = pl.BlockSpec((width,), lambda i: (0,))
    return pl.pallas_call(
        finish_kernel,
        grid=(rows // block,),
        in_specs=[smem()]
        + [row_spec] * 2
        + [gain_spec] * 2
        + [pl.BlockSpec((3, block, width // SEQ), lambda i: (0, i, 0))] * SEQ,
        out_specs=[row_spec] * 3,
        out_shape=[jax.ShapeDtypeStruct((rows, width), jnp.bfloat16)] * 3,
        scratch_shapes=[pltpu.VMEM((2, block, width), jnp.bfloat16)],
        name="norm_back",
    )(place, queries, keys, gain_q, gain_k, *parts)


def tile_at(ref, index, rows):
    return ref[pl.ds(pl.multiple_of(index * rows, rows), rows), :]


def gather_pair(ref, near, rows):
    return jnp.concatenate(
        [
            jnp.concatenate([tile_at(ref, one, rows), tile_at(ref, two, rows)], axis=1)
            for one, two in zip(*near)
        ],
        axis=0,
    )


def spread(block, rows):
    twice = jnp.concatenate([block, block], axis=1)
    width = block.shape[1]
    own = (lax.broadcasted_iota(jnp.int32, twice.shape, 0) < rows) == (
        lax.broadcasted_iota(jnp.int32, twice.shape, 1) < width
    )
    return jnp.where(own, twice, jnp.zeros_like(twice))


def near_of(place_ref, pairs_ref, pair):
    flip = place_ref[3]
    return [
        [
            jnp.bitwise_xor(pairs_ref[jnp.bitwise_xor(2 * pair + half, flip), n], flip)
            for n in range(pairs_ref.shape[1])
        ]
        for half in range(2)
    ]


def load_parts(parts, whole):
    for at, part in enumerate(parts):
        whole[at * part.shape[0] : (at + 1) * part.shape[0], :] = part[...]


def diagonal(product, half, tile_rows, width):
    return product[half * tile_rows : (half + 1) * tile_rows, half * width : (half + 1) * width]


def forward_kernel(place_ref, pairs_ref, lens_ref, *refs):
    q_parts, k_parts, v_parts = refs[:SEQ], refs[SEQ : 2 * SEQ], refs[2 * SEQ : 3 * SEQ]
    att_ref, probs_ref, q_all, k_all, v_all = refs[3 * SEQ :]
    tile_count, neighbours = pairs_ref.shape
    clip_rows, width = q_all.shape
    tile_rows = clip_rows // tile_count
    rows = 2 * tile_rows
    depth = neighbours * tile_rows
    scale = LOG2E / math.sqrt(width)
    load_parts(q_parts, q_all)
    load_parts(k_parts, k_all)
    load_parts(v_parts, v_all)
    shape = (tile_rows - MIN_LIVE, rows)
    first = lax.broadcasted_iota(jnp.int32, shape, 1) < tile_rows
    slot = lax.broadcasted_iota(jnp.int32, shape, 0) + MIN_LIVE

    def length(tile):
        return lens_ref[0, jnp.bitwise_xor(tile, place_ref[3])]

    def score(pair, near):
        keys = gather_pair(k_all, near, tile_rows)
        queries = spread(q_all[pl.ds(pl.multiple_of(pair * rows, rows), rows), :], tile_rows)
        scores = contract(keys, queries, 1, 1)
        pieces = []
        for n in range(neighbours):
            start = n * tile_rows
            pieces.append(scores[start : start + MIN_LIVE])
            live = slot < jnp.where(first, length(near[0][n]), length(near[1][n]))
            pieces.append(jnp.where(live, scores[start + MIN_LIVE : start + tile_rows], -jnp.inf))
        return jnp.concatenate(pieces, axis=0)

    def soften(scores):
        weights = jnp.exp2((scores - jnp.max(scores, axis=0, keepdims=True)) * scale)
        return (weights * (1.0 / jnp.sum(weights, axis=0, keepdims=True))).astype(jnp.bfloat16)

    def body(group, carry):
        pairs = [group * GROUP + at for at in range(GROUP)]
        nears = [near_of(place_ref, pairs_ref, pair) for pair in pairs]
        probs = [soften(score(pair, near)) for pair, near in zip(pairs, nears)]
        attended = [
            contract(prob, gather_pair(v_all, near, tile_rows), 0, 0) for prob, near in zip(probs, nears)
        ]
        for pair, prob, product in zip(pairs, probs, attended):
            probs_ref[0, pl.ds(pl.multiple_of(pair * depth, depth), depth), :] = prob
            for half in range(2):
                place = pl.ds(pl.multiple_of((2 * pair + half) * tile_rows, tile_rows), tile_rows)
                att_ref[place, :] = diagonal(product, half, tile_rows, width).astype(jnp.bfloat16)
        return carry

    lax.fori_loop(0, tile_count // 2 // GROUP, body, 0)


def pack_specs(rows):
    return [pl.BlockSpec((None, rows, HEAD_DIM), lambda h, which=which: (which, 0, h)) for which in range(3)]


def forward(place, tile_pairs, lens, packs):
    _, rows, local_width = packs[0].shape
    heads = local_width // HEAD_DIM
    clip_rows = rows * SEQ
    pairs = tile_pairs.shape[0] // 2
    depth = tile_pairs.shape[1] * (clip_rows // tile_pairs.shape[0])
    return pl.pallas_call(
        forward_kernel,
        grid=(heads,),
        in_specs=[smem()] * 3 + [spec for spec in pack_specs(rows) for _ in packs],
        out_specs=[
            pl.BlockSpec((clip_rows, HEAD_DIM), lambda h: (0, h)),
            pl.BlockSpec((1, pairs * depth, HEAD_DIM), lambda h: (h, 0, 0)),
        ],
        out_shape=[
            jax.ShapeDtypeStruct((clip_rows, local_width), jnp.bfloat16),
            jax.ShapeDtypeStruct((heads, pairs * depth, HEAD_DIM), jnp.bfloat16),
        ],
        scratch_shapes=[pltpu.VMEM((clip_rows, HEAD_DIM), jnp.bfloat16)] * 3,
        compiler_params=params(),
        name="attention_forward",
    )(place, tile_pairs, lens, *packs, *packs, *packs)


def backward_kernel(place_ref, pairs_ref, *refs):
    q_parts, k_parts, v_parts = refs[:SEQ], refs[SEQ : 2 * SEQ], refs[2 * SEQ : 3 * SEQ]
    own_grads, other_grads = refs[3 * SEQ : 4 * SEQ], refs[4 * SEQ : 5 * SEQ]
    probs_ref = refs[5 * SEQ]
    outs = refs[5 * SEQ + 1 : 6 * SEQ + 1]
    q_all, k_all, v_all, g_all, gq_all, gk_acc, gv_acc = refs[6 * SEQ + 1 :]
    tile_count, neighbours = pairs_ref.shape
    clip_rows, width = q_all.shape
    tile_rows = clip_rows // tile_count
    rows = 2 * tile_rows
    depth = neighbours * tile_rows
    factor = 1.0 / math.sqrt(width)
    load_parts(q_parts, q_all)
    load_parts(k_parts, k_all)
    load_parts(v_parts, v_all)
    half_rows = own_grads[0].shape[0]
    core = place_ref[1]
    for at in range(SEQ):
        for grads, half in ((own_grads[at], core), (other_grads[at ^ 1], 1 - core)):
            g_all[pl.ds(pl.multiple_of((2 * at + half) * half_rows, half_rows), half_rows), :] = grads[...]
    gk_acc[...] = jnp.zeros_like(gk_acc)
    gv_acc[...] = jnp.zeros_like(gv_acc)

    def rows_of(pair):
        return pl.ds(pl.multiple_of(pair * rows, rows), rows)

    def body(group, carry):
        pairs = [group * GROUP + at for at in range(GROUP)]
        nears = [near_of(place_ref, pairs_ref, pair) for pair in pairs]
        probs = [
            probs_ref[0, pl.ds(pl.multiple_of(pair * depth, depth), depth), :] for pair in pairs
        ]
        grads = [spread(g_all[rows_of(pair), :], tile_rows) for pair in pairs]
        grad_scores = []
        for prob, grad, near in zip(probs, grads, nears):
            grad_prob = contract(gather_pair(v_all, near, tile_rows), grad, 1, 1)
            wide = prob.astype(jnp.float32)
            delta = jnp.sum(wide * grad_prob, axis=0, keepdims=True)
            grad_scores.append((wide * (grad_prob - delta)).astype(jnp.bfloat16))
        grad_queries = [
            contract(grad_score, gather_pair(k_all, near, tile_rows), 0, 0) * factor
            for grad_score, near in zip(grad_scores, nears)
        ]
        grad_keys = [
            contract(grad_score, spread(q_all[rows_of(pair), :], tile_rows), 1, 0)
            for grad_score, pair in zip(grad_scores, pairs)
        ]
        grad_vals = [contract(prob, grad, 1, 0) for prob, grad in zip(probs, grads)]
        for pair, near, grad_query, grad_key, grad_val in zip(
            pairs, nears, grad_queries, grad_keys, grad_vals
        ):
            for half in range(2):
                place = pl.ds(pl.multiple_of((2 * pair + half) * tile_rows, tile_rows), tile_rows)
                gq_all[place, :] = diagonal(grad_query, half, tile_rows, width).astype(jnp.bfloat16)
                for n in range(neighbours):
                    at = (slice(n * tile_rows, (n + 1) * tile_rows), slice(half * width, (half + 1) * width))
                    place = pl.ds(pl.multiple_of(near[half][n] * tile_rows, tile_rows), tile_rows)
                    gk_acc[place, :] += grad_key[at]
                    gv_acc[place, :] += grad_val[at]
        return carry

    lax.fori_loop(0, tile_count // 2 // GROUP, body, 0)
    for at, out in enumerate(outs):
        part = slice(at * out.shape[1], (at + 1) * out.shape[1])
        out[0] = gq_all[part, :]
        out[1] = (gk_acc[part, :] * factor).astype(jnp.bfloat16)
        out[2] = gv_acc[part, :].astype(jnp.bfloat16)


def backward(place, tile_pairs, packs, own_grads, other_grads, probs):
    _, rows, local_width = packs[0].shape
    heads = local_width // HEAD_DIM
    clip_rows = rows * SEQ
    grad_spec = pl.BlockSpec((own_grads[0].shape[0], HEAD_DIM), lambda h: (0, h))
    bf16_rows = pltpu.VMEM((clip_rows, HEAD_DIM), jnp.bfloat16)
    f32_rows = pltpu.VMEM((clip_rows, HEAD_DIM), jnp.float32)
    return pl.pallas_call(
        backward_kernel,
        grid=(heads,),
        in_specs=[smem()] * 2
        + [spec for spec in pack_specs(rows) for _ in packs]
        + [grad_spec] * (2 * SEQ)
        + [pl.BlockSpec((1,) + probs.shape[1:], lambda h: (h, 0, 0))],
        out_specs=[pl.BlockSpec((3, rows, HEAD_DIM), lambda h: (0, 0, h))] * SEQ,
        out_shape=[jax.ShapeDtypeStruct((3, rows, local_width), jnp.bfloat16)] * SEQ,
        scratch_shapes=[bf16_rows] * 5 + [f32_rows] * 2,
        compiler_params=params(),
        name="attention_backward",
    )(place, tile_pairs, *packs, *packs, *packs, *own_grads, *other_grads, probs)


def weight_grad_kernel(place_ref, mean, side, att_ref, *refs):
    own, other, outs = refs[:SEQ], refs[SEQ : 2 * SEQ], refs[2 * SEQ :]
    pieces, second = outs[:-1], outs[-1]
    half_rows = own[0].shape[0]
    core = place_ref[1]
    columns, attended = [], []
    for at in range(SEQ):
        for part, half in ((own[at], core), (other[at ^ 1], 1 - core)):
            columns.append(part[...])
            start = pl.multiple_of((2 * at + half) * half_rows, half_rows)
            attended.append(att_ref[pl.ds(start, half_rows), :])
    total = contract(jnp.concatenate(columns, axis=0), jnp.concatenate(attended, axis=0), 0, 0)
    total = (total * mean).astype(jnp.bfloat16)
    count, piece = second.shape[:2]
    step = pl.program_id(0)
    for at in range(count):
        start = 2 * at * piece
        second[at] = total[start + piece : start + 2 * piece]
        owner = step * count + at
        ahead = lax.rem(owner + side - place_ref[4], side)
        for by, out in enumerate(pieces):

            @pl.when(ahead == by)
            def _(out=out, start=start, owner=owner):
                out[owner // side] = total[start : start + piece]


def weight_grad(place, attended, own, other, mean, side, block=640):
    half_rows, features = own[0].shape
    local_width = attended.shape[1]
    piece = features // (side * side) // CORES
    return pl.pallas_call(
        lambda place_ref, *refs: weight_grad_kernel(place_ref, mean, side, *refs),
        grid=(features // block,),
        in_specs=[smem(), pl.BlockSpec(attended.shape, lambda i: (0, 0))]
        + [pl.BlockSpec((half_rows, block), lambda i: (0, i))] * (2 * SEQ),
        out_specs=[pl.BlockSpec((side, piece, local_width), lambda i: (0, 0, 0))] * side
        + [pl.BlockSpec((block // piece // 2, piece, local_width), lambda i: (i, 0, 0))],
        out_shape=[jax.ShapeDtypeStruct((side, piece, local_width), jnp.bfloat16)] * side
        + [jax.ShapeDtypeStruct((side * side, piece, local_width), jnp.bfloat16)],
        compiler_params=params(),
        name="weight_grad",
    )(place, attended, *own, *other)


def device_of(core, seq):
    return core * SEQ + seq


def outward(round_):
    pairs = []
    for core in range(CORES):
        for token in range(SEQ):
            shard = token ^ round_
            pairs.append((device_of(core, token), device_of(shard % 2, 2 * core + shard // 2)))
    return pairs


def inward(round_):
    return [(target, source) for source, target in outward(round_)]


def send(value, pairs):
    others = [pair for pair in pairs if pair[0] != pair[1]]
    got = lax.ppermute(value, ("core", "seq"), others)
    mine = [source for source, target in pairs if source == target]
    if not mine:
        return got
    here = device_of(lax.axis_index("core"), lax.axis_index("seq"))
    keep = functools.reduce(jnp.logical_or, [here == one for one in mine])
    return jnp.where(keep, value, got)


def swap_cores(value):
    return lax.ppermute(value, "core", [(0, 1), (1, 0)])


def shift(value, axis, by):
    count = lax.axis_size(axis)
    return lax.ppermute(value, axis, [(i, (i + by) % count) for i in range(count)])


def add(*terms):
    total = terms[0].astype(jnp.float32)
    for term in terms[1:]:
        total = total + term.astype(jnp.float32)
    return total.astype(jnp.bfloat16)


def take(value, index, axis=0):
    return lax.dynamic_index_in_dim(value, index, axis, keepdims=False)


def pair_sum(value, axis):
    here = lax.axis_index(axis)

    def swap(part, mask):
        return lax.ppermute(part, axis, [(i, i ^ mask) for i in range(lax.axis_size(axis))])

    got = swap(jnp.stack([take(value, here ^ 1), take(value, here ^ 2)]), 1)
    mine, theirs = add(take(value, here), got[0]), add(take(value, here ^ 3), got[1])
    return add(mine, swap(theirs, 3))


def to_shard_holders(w_out, seq, token):
    got = []
    for other in range(2):
        pairs = []
        for holder in range(CORES):
            for shard in range(SEQ):
                window = holder ^ other
                pairs.append((device_of(holder, shard), device_of(shard % 2, shard // 2 + 2 * window)))
        got.append(send(w_out, pairs))
    window = seq // 2
    got = after(got, token)
    return jnp.where(window == 0, jnp.concatenate(got), jnp.concatenate(got[::-1]))


def to_owners(totals, seq):
    window = seq // 2
    got = []
    for other in range(2):
        pairs = []
        for core in range(CORES):
            for at in range(SEQ):
                holder = (at // 2) ^ other
                pairs.append((device_of(core, at), device_of(holder, 2 * (at % 2) + core)))
        got.append(send(jnp.where((window ^ other) == 0, totals[0], totals[1]), pairs))
    return got[0].astype(jnp.float32) + got[1].astype(jnp.float32)


def after(values, *tokens):
    return lax.optimization_barrier((values, tokens))[0]


def per_device(queries, keys, values, gain_q, gain_k, tile_pairs, tile_lens, out_grad, w_out):
    core = lax.axis_index("core")
    seq = lax.axis_index("seq")
    count_z = lax.axis_size("z")
    count_x = lax.axis_size("x")
    rows, features = out_grad.shape
    shard = 2 * (seq % 2) + core
    tiles_per_block = tile_pairs.shape[0] // SEQ
    place = jnp.stack([seq, core, shard, shard * tiles_per_block, lax.axis_index("x")]).astype(jnp.int32)
    lens = jnp.where(seq // 2 == core, tile_lens, swap_cores(tile_lens))

    def half_rows(rows_in, round_):
        half = seq % 2 if round_ % 2 == 0 else 1 - seq % 2
        return take(rows_in.reshape(2, rows // 2, features), half)

    parts = to_rounds(place, queries, keys, values, gain_q, gain_k)
    w_rows = to_shard_holders(w_out, seq, parts[0])
    w_all = lax.all_gather(w_rows, ("z", "x"), axis=0, tiled=True)
    packs = {r: send(parts[r], outward(r)) for r in ORDER}
    came = [packs[r] for r in ORDER]
    own = {}
    for r in ORDER:
        own[r] = send(half_rows(after(out_grad, came), r), outward(r))
    packs = [packs[r] for r in range(SEQ)]

    def project(part):
        return jnp.dot(part, w_all, preferred_element_type=jnp.float32).astype(jnp.bfloat16)

    attended, probs = forward(place, tile_pairs, lens, packs)
    one, two, three, last = ORDER
    other = {one: swap_cores(own[one]), two: swap_cores(after(own[two], attended))}
    own_grads = {one: project(own[one]), two: project(own[two])}
    other_grads = {one: project(other[one]), two: project(other[two])}
    other[three] = swap_cores(after(own[three], list(own_grads.values()), list(other_grads.values())))
    own_grads[three], other_grads[three] = project(own[three]), project(other[three])
    done = ([own_grads[r] for r in ORDER[:-1]], [other_grads[r] for r in ORDER[:-2]])
    other[last] = swap_cores(after(own[last], *done))
    own_grads[last] = project(own[last])
    other_grads[last] = project(other[last])
    attended = after(attended, own_grads, other_grads)
    own, other, own_grads, other_grads = [
        [table[r] for r in range(SEQ)] for table in (own, other, own_grads, other_grads)
    ]
    *one, two = weight_grad(place, attended, own, other, 1.0 / (count_z * count_x * CORES), count_x)
    two = lax.psum_scatter(two, "z", scatter_dimension=0, tiled=True)
    token = one[0]
    one = [one[0]] + [shift(one[by], "x", by) for by in (2, 1, 3)]
    parts = backward(place, tile_pairs, packs, own_grads, other_grads, after(probs, token))
    one = add(*after(one, parts[0]))
    parts = {r: send(parts[r] if r in ORDER[:2] else after(parts[r], one), inward(r)) for r in ORDER}
    two = lax.optimization_barrier(pair_sum(after(two, one), "x"))
    one = lax.optimization_barrier(pair_sum(one, "z"))
    grad_w = to_owners((one, two), seq)
    grad_q, grad_k, grad_v = finish(
        place, queries, keys, gain_q, gain_k, [parts[r] for r in range(SEQ)]
    )
    return (grad_q, grad_k, grad_v, grad_w)


def solution(mesh):
    dp = mesh.shape["dp"]
    side = math.isqrt(dp // CORES)
    parts = Mesh(mesh.devices.reshape(side, side, CORES, SEQ), ("z", "x", "core", "seq"))
    dp_axes = ("z", "x", "core")
    tokens = P(dp_axes + ("seq",), None)
    return jax.shard_map(
        per_device,
        mesh=parts,
        in_specs=(tokens, tokens, tokens, P(), P(), P(), P(dp_axes, None), tokens, P(dp_axes, "seq")),
        out_specs=(tokens, tokens, tokens, P(dp_axes, "seq")),
        check_vma=False,
    )
```

```python
import functools
import math

import jax
import jax.numpy as jnp
from jax import lax
from jax.experimental import pallas as pl
from jax.experimental.pallas import tpu as pltpu
from jax.sharding import Mesh, PartitionSpec as P

HEAD_DIM = 128


EPS = 1e-06
LOG2E = 1.4426950408889634
MIN_LIVE = 40
SEQ = 4
CORES = 2
GROUP = 4
ORDER = (0, 3, 1, 2)


def smem():
    return pl.BlockSpec(memory_space=pltpu.SMEM)


def params():
    return pltpu.CompilerParams(vmem_limit_bytes=48 << 20)


def contract(left, right, left_dim, right_dim):
    return lax.dot_general(
        left, right, (((left_dim,), (right_dim,)), ((), ())), preferred_element_type=jnp.float32
    )


def row_scale_of(values_f):
    return lax.rsqrt(jnp.mean(values_f * values_f, axis=-1, keepdims=True) + EPS)


def shard_of(place_ref, round_, width):
    return pl.ds(pl.multiple_of(jnp.bitwise_xor(place_ref[0], round_) * width, 128), width)


def rounds_kernel(place_ref, q_ref, k_ref, v_ref, gain_q_ref, gain_k_ref, *refs):
    outs, normed = refs[:-1], refs[-1]
    for at, (x_ref, gain_ref) in enumerate(((q_ref, gain_q_ref), (k_ref, gain_k_ref))):
        values_f = x_ref[...].astype(jnp.float32)
        normed[at] = (values_f * row_scale_of(values_f) * gain_ref[...][None, :]).astype(jnp.bfloat16)
    for round_, out in enumerate(outs):
        columns = shard_of(place_ref, round_, out.shape[2])
        out[0] = normed[0, :, columns]
        out[1] = normed[1, :, columns]
        out[2] = v_ref[:, columns]


def to_rounds(place, queries, keys, values, gain_q, gain_k, block=64):
    rows, width = queries.shape
    row_spec = pl.BlockSpec((block, width), lambda i: (i, 0))
    gain_spec = pl.BlockSpec((width,), lambda i: (0,))
    return pl.pallas_call(
        rounds_kernel,
        grid=(rows // block,),
        in_specs=[smem()] + [row_spec] * 3 + [gain_spec] * 2,
        out_specs=[pl.BlockSpec((3, block, width // SEQ), lambda i: (0, i, 0))] * SEQ,
        out_shape=[jax.ShapeDtypeStruct((3, rows, width // SEQ), jnp.bfloat16)] * SEQ,
        scratch_shapes=[pltpu.VMEM((2, block, width), jnp.bfloat16)],
        name="norm_rows",
    )(place, queries, keys, values, gain_q, gain_k)


def finish_kernel(place_ref, q_ref, k_ref, gain_q_ref, gain_k_ref, *refs):
    parts, outs, joined = refs[:SEQ], refs[SEQ:-1], refs[-1]
    width = q_ref.shape[1]
    for round_, part in enumerate(parts):
        columns = shard_of(place_ref, round_, part.shape[2])
        joined[0, :, columns] = part[0]
        joined[1, :, columns] = part[1]
        outs[2][:, columns] = part[2]
    for at, (x_ref, gain_ref) in enumerate(((q_ref, gain_q_ref), (k_ref, gain_k_ref))):
        values_f = x_ref[...].astype(jnp.float32)
        row_scale = row_scale_of(values_f)
        gated = gain_ref[...][None, :] * joined[at].astype(jnp.float32)
        inner = jnp.sum(gated * values_f, axis=-1, keepdims=True)
        back = values_f * (row_scale * row_scale * row_scale * inner * (1.0 / width))
        outs[at][...] = (row_scale * gated - back).astype(jnp.bfloat16)


def finish(place, queries, keys, gain_q, gain_k, parts, block=64):
    rows, width = queries.shape
    row_spec = pl.BlockSpec((block, width), lambda i: (i, 0))
    gain_spec = pl.BlockSpec((width,), lambda i: (0,))
    return pl.pallas_call(
        finish_kernel,
        grid=(rows // block,),
        in_specs=[smem()]
        + [row_spec] * 2
        + [gain_spec] * 2
        + [pl.BlockSpec((3, block, width // SEQ), lambda i: (0, i, 0))] * SEQ,
        out_specs=[row_spec] * 3,
        out_shape=[jax.ShapeDtypeStruct((rows, width), jnp.bfloat16)] * 3,
        scratch_shapes=[pltpu.VMEM((2, block, width), jnp.bfloat16)],
        name="norm_back",
    )(place, queries, keys, gain_q, gain_k, *parts)


def tile_at(ref, index, rows):
    return ref[pl.ds(pl.multiple_of(index * rows, rows), rows), :]


def gather_pair(ref, near, rows):
    return jnp.concatenate(
        [
            jnp.concatenate([tile_at(ref, one, rows), tile_at(ref, two, rows)], axis=1)
            for one, two in zip(*near)
        ],
        axis=0,
    )


def spread(block, rows):
    twice = jnp.concatenate([block, block], axis=1)
    width = block.shape[1]
    own = (lax.broadcasted_iota(jnp.int32, twice.shape, 0) < rows) == (
        lax.broadcasted_iota(jnp.int32, twice.shape, 1) < width
    )
    return jnp.where(own, twice, jnp.zeros_like(twice))


def near_of(place_ref, pairs_ref, pair):
    flip = place_ref[3]
    return [
        [
            jnp.bitwise_xor(pairs_ref[jnp.bitwise_xor(2 * pair + half, flip), n], flip)
            for n in range(pairs_ref.shape[1])
        ]
        for half in range(2)
    ]


def load_parts(parts, whole):
    for at, part in enumerate(parts):
        whole[at * part.shape[0] : (at + 1) * part.shape[0], :] = part[...]


def diagonal(product, half, tile_rows, width):
    return product[half * tile_rows : (half + 1) * tile_rows, half * width : (half + 1) * width]


def forward_kernel(place_ref, pairs_ref, lens_ref, *refs):
    q_parts, k_parts, v_parts = refs[:SEQ], refs[SEQ : 2 * SEQ], refs[2 * SEQ : 3 * SEQ]
    att_ref, probs_ref, q_all, k_all, v_all = refs[3 * SEQ :]
    tile_count, neighbours = pairs_ref.shape
    clip_rows, width = q_all.shape
    tile_rows = clip_rows // tile_count
    rows = 2 * tile_rows
    depth = neighbours * tile_rows
    scale = LOG2E / math.sqrt(width)
    load_parts(q_parts, q_all)
    load_parts(k_parts, k_all)
    load_parts(v_parts, v_all)
    shape = (tile_rows - MIN_LIVE, rows)
    first = lax.broadcasted_iota(jnp.int32, shape, 1) < tile_rows
    slot = lax.broadcasted_iota(jnp.int32, shape, 0) + MIN_LIVE

    def length(tile):
        return lens_ref[0, jnp.bitwise_xor(tile, place_ref[3])]

    def score(pair, near):
        keys = gather_pair(k_all, near, tile_rows)
        queries = spread(q_all[pl.ds(pl.multiple_of(pair * rows, rows), rows), :], tile_rows)
        scores = contract(keys, queries, 1, 1)
        pieces = []
        for n in range(neighbours):
            start = n * tile_rows
            pieces.append(scores[start : start + MIN_LIVE])
            live = slot < jnp.where(first, length(near[0][n]), length(near[1][n]))
            pieces.append(jnp.where(live, scores[start + MIN_LIVE : start + tile_rows], -jnp.inf))
        return jnp.concatenate(pieces, axis=0)

    def soften(scores):
        weights = jnp.exp2((scores - jnp.max(scores, axis=0, keepdims=True)) * scale)
        return (weights * (1.0 / jnp.sum(weights, axis=0, keepdims=True))).astype(jnp.bfloat16)

    def body(group, carry):
        pairs = [group * GROUP + at for at in range(GROUP)]
        nears = [near_of(place_ref, pairs_ref, pair) for pair in pairs]
        probs = [soften(score(pair, near)) for pair, near in zip(pairs, nears)]
        attended = [
            contract(prob, gather_pair(v_all, near, tile_rows), 0, 0) for prob, near in zip(probs, nears)
        ]
        for pair, prob, product in zip(pairs, probs, attended):
            probs_ref[0, pl.ds(pl.multiple_of(pair * depth, depth), depth), :] = prob
            for half in range(2):
                place = pl.ds(pl.multiple_of((2 * pair + half) * tile_rows, tile_rows), tile_rows)
                att_ref[place, :] = diagonal(product, half, tile_rows, width).astype(jnp.bfloat16)
        return carry

    lax.fori_loop(0, tile_count // 2 // GROUP, body, 0)


def pack_specs(rows):
    return [pl.BlockSpec((None, rows, HEAD_DIM), lambda h, which=which: (which, 0, h)) for which in range(3)]


def forward(place, tile_pairs, lens, packs):
    _, rows, local_width = packs[0].shape
    heads = local_width // HEAD_DIM
    clip_rows = rows * SEQ
    pairs = tile_pairs.shape[0] // 2
    depth = tile_pairs.shape[1] * (clip_rows // tile_pairs.shape[0])
    return pl.pallas_call(
        forward_kernel,
        grid=(heads,),
        in_specs=[smem()] * 3 + [spec for spec in pack_specs(rows) for _ in packs],
        out_specs=[
            pl.BlockSpec((clip_rows, HEAD_DIM), lambda h: (0, h)),
            pl.BlockSpec((1, pairs * depth, HEAD_DIM), lambda h: (h, 0, 0)),
        ],
        out_shape=[
            jax.ShapeDtypeStruct((clip_rows, local_width), jnp.bfloat16),
            jax.ShapeDtypeStruct((heads, pairs * depth, HEAD_DIM), jnp.bfloat16),
        ],
        scratch_shapes=[pltpu.VMEM((clip_rows, HEAD_DIM), jnp.bfloat16)] * 3,
        compiler_params=params(),
        name="attention_forward",
    )(place, tile_pairs, lens, *packs, *packs, *packs)


def backward_kernel(place_ref, pairs_ref, *refs):
    q_parts, k_parts, v_parts = refs[:SEQ], refs[SEQ : 2 * SEQ], refs[2 * SEQ : 3 * SEQ]
    own_grads, other_grads = refs[3 * SEQ : 4 * SEQ], refs[4 * SEQ : 5 * SEQ]
    probs_ref = refs[5 * SEQ]
    outs = refs[5 * SEQ + 1 : 6 * SEQ + 1]
    q_all, k_all, v_all, g_all, gq_all, gk_acc, gv_acc = refs[6 * SEQ + 1 :]
    tile_count, neighbours = pairs_ref.shape
    clip_rows, width = q_all.shape
    tile_rows = clip_rows // tile_count
    rows = 2 * tile_rows
    depth = neighbours * tile_rows
    factor = 1.0 / math.sqrt(width)
    load_parts(q_parts, q_all)
    load_parts(k_parts, k_all)
    load_parts(v_parts, v_all)
    half_rows = own_grads[0].shape[0]
    core = place_ref[1]
    for at in range(SEQ):
        for grads, half in ((own_grads[at], core), (other_grads[at ^ 1], 1 - core)):
            g_all[pl.ds(pl.multiple_of((2 * at + half) * half_rows, half_rows), half_rows), :] = grads[...]
    gk_acc[...] = jnp.zeros_like(gk_acc)
    gv_acc[...] = jnp.zeros_like(gv_acc)

    def rows_of(pair):
        return pl.ds(pl.multiple_of(pair * rows, rows), rows)

    def body(group, carry):
        pairs = [group * GROUP + at for at in range(GROUP)]
        nears = [near_of(place_ref, pairs_ref, pair) for pair in pairs]
        probs = [
            probs_ref[0, pl.ds(pl.multiple_of(pair * depth, depth), depth), :] for pair in pairs
        ]
        grads = [spread(g_all[rows_of(pair), :], tile_rows) for pair in pairs]
        grad_scores = []
        for prob, grad, near in zip(probs, grads, nears):
            grad_prob = contract(gather_pair(v_all, near, tile_rows), grad, 1, 1)
            wide = prob.astype(jnp.float32)
            delta = jnp.sum(wide * grad_prob, axis=0, keepdims=True)
            grad_scores.append((wide * (grad_prob - delta)).astype(jnp.bfloat16))
        grad_queries = [
            contract(grad_score, gather_pair(k_all, near, tile_rows), 0, 0) * factor
            for grad_score, near in zip(grad_scores, nears)
        ]
        grad_keys = [
            contract(grad_score, spread(q_all[rows_of(pair), :], tile_rows), 1, 0)
            for grad_score, pair in zip(grad_scores, pairs)
        ]
        grad_vals = [contract(prob, grad, 1, 0) for prob, grad in zip(probs, grads)]
        for pair, near, grad_query, grad_key, grad_val in zip(
            pairs, nears, grad_queries, grad_keys, grad_vals
        ):
            for half in range(2):
                place = pl.ds(pl.multiple_of((2 * pair + half) * tile_rows, tile_rows), tile_rows)
                gq_all[place, :] = diagonal(grad_query, half, tile_rows, width).astype(jnp.bfloat16)
                for n in range(neighbours):
                    at = (slice(n * tile_rows, (n + 1) * tile_rows), slice(half * width, (half + 1) * width))
                    place = pl.ds(pl.multiple_of(near[half][n] * tile_rows, tile_rows), tile_rows)
                    gk_acc[place, :] += grad_key[at]
                    gv_acc[place, :] += grad_val[at]
        return carry

    lax.fori_loop(0, tile_count // 2 // GROUP, body, 0)
    for at, out in enumerate(outs):
        part = slice(at * out.shape[1], (at + 1) * out.shape[1])
        out[0] = gq_all[part, :]
        out[1] = (gk_acc[part, :] * factor).astype(jnp.bfloat16)
        out[2] = gv_acc[part, :].astype(jnp.bfloat16)


def backward(place, tile_pairs, packs, own_grads, other_grads, probs):
    _, rows, local_width = packs[0].shape
    heads = local_width // HEAD_DIM
    clip_rows = rows * SEQ
    grad_spec = pl.BlockSpec((own_grads[0].shape[0], HEAD_DIM), lambda h: (0, h))
    bf16_rows = pltpu.VMEM((clip_rows, HEAD_DIM), jnp.bfloat16)
    f32_rows = pltpu.VMEM((clip_rows, HEAD_DIM), jnp.float32)
    return pl.pallas_call(
        backward_kernel,
        grid=(heads,),
        in_specs=[smem()] * 2
        + [spec for spec in pack_specs(rows) for _ in packs]
        + [grad_spec] * (2 * SEQ)
        + [pl.BlockSpec((1,) + probs.shape[1:], lambda h: (h, 0, 0))],
        out_specs=[pl.BlockSpec((3, rows, HEAD_DIM), lambda h: (0, 0, h))] * SEQ,
        out_shape=[jax.ShapeDtypeStruct((3, rows, local_width), jnp.bfloat16)] * SEQ,
        scratch_shapes=[bf16_rows] * 5 + [f32_rows] * 2,
        compiler_params=params(),
        name="attention_backward",
    )(place, tile_pairs, *packs, *packs, *packs, *own_grads, *other_grads, probs)


def weight_grad_kernel(place_ref, mean, side, att_ref, *refs):
    own, other, outs = refs[:SEQ], refs[SEQ : 2 * SEQ], refs[2 * SEQ :]
    pieces, second = outs[:-1], outs[-1]
    half_rows = own[0].shape[0]
    core = place_ref[1]
    columns, attended = [], []
    for at in range(SEQ):
        for part, half in ((own[at], core), (other[at ^ 1], 1 - core)):
            columns.append(part[...])
            start = pl.multiple_of((2 * at + half) * half_rows, half_rows)
            attended.append(att_ref[pl.ds(start, half_rows), :])
    total = contract(jnp.concatenate(columns, axis=0), jnp.concatenate(attended, axis=0), 0, 0)
    total = (total * mean).astype(jnp.bfloat16)
    count, piece = second.shape[:2]
    step = pl.program_id(0)
    for at in range(count):
        start = 2 * at * piece
        second[at] = total[start + piece : start + 2 * piece]
        owner = step * count + at
        ahead = lax.rem(owner + side - place_ref[4], side)
        for by, out in enumerate(pieces):

            @pl.when(ahead == by)
            def _(out=out, start=start, owner=owner):
                out[owner // side] = total[start : start + piece]


def weight_grad(place, attended, own, other, mean, side, block=640):
    half_rows, features = own[0].shape
    local_width = attended.shape[1]
    piece = features // (side * side) // CORES
    return pl.pallas_call(
        lambda place_ref, *refs: weight_grad_kernel(place_ref, mean, side, *refs),
        grid=(features // block,),
        in_specs=[smem(), pl.BlockSpec(attended.shape, lambda i: (0, 0))]
        + [pl.BlockSpec((half_rows, block), lambda i: (0, i))] * (2 * SEQ),
        out_specs=[pl.BlockSpec((side, piece, local_width), lambda i: (0, 0, 0))] * side
        + [pl.BlockSpec((block // piece // 2, piece, local_width), lambda i: (i, 0, 0))],
        out_shape=[jax.ShapeDtypeStruct((side, piece, local_width), jnp.bfloat16)] * side
        + [jax.ShapeDtypeStruct((side * side, piece, local_width), jnp.bfloat16)],
        compiler_params=params(),
        name="weight_grad",
    )(place, attended, *own, *other)


def device_of(core, seq):
    return core * SEQ + seq


def outward(round_):
    pairs = []
    for core in range(CORES):
        for token in range(SEQ):
            shard = token ^ round_
            pairs.append((device_of(core, token), device_of(shard % 2, 2 * core + shard // 2)))
    return pairs


def inward(round_):
    return [(target, source) for source, target in outward(round_)]


def send(value, pairs):
    others = [pair for pair in pairs if pair[0] != pair[1]]
    got = lax.ppermute(value, ("core", "seq"), others)
    mine = [source for source, target in pairs if source == target]
    if not mine:
        return got
    here = device_of(lax.axis_index("core"), lax.axis_index("seq"))
    keep = functools.reduce(jnp.logical_or, [here == one for one in mine])
    return jnp.where(keep, value, got)


def swap_cores(value):
    return lax.ppermute(value, "core", [(0, 1), (1, 0)])


def shift(value, axis, by):
    count = lax.axis_size(axis)
    return lax.ppermute(value, axis, [(i, (i + by) % count) for i in range(count)])


def add(*terms):
    total = terms[0].astype(jnp.float32)
    for term in terms[1:]:
        total = total + term.astype(jnp.float32)
    return total.astype(jnp.bfloat16)


def take(value, index, axis=0):
    return lax.dynamic_index_in_dim(value, index, axis, keepdims=False)


def pair_sum(value, axis):
    here = lax.axis_index(axis)

    def swap(part, mask):
        return lax.ppermute(part, axis, [(i, i ^ mask) for i in range(lax.axis_size(axis))])

    got = swap(jnp.stack([take(value, here ^ 1), take(value, here ^ 2)]), 1)
    mine, theirs = add(take(value, here), got[0]), add(take(value, here ^ 3), got[1])
    return add(mine, swap(theirs, 3))


def to_shard_holders(w_out, seq, token):
    got = []
    for other in range(2):
        pairs = []
        for holder in range(CORES):
            for shard in range(SEQ):
                window = holder ^ other
                pairs.append((device_of(holder, shard), device_of(shard % 2, shard // 2 + 2 * window)))
        got.append(send(w_out, pairs))
    window = seq // 2
    got = after(got, token)
    return jnp.where(window == 0, jnp.concatenate(got), jnp.concatenate(got[::-1]))


def to_owners(totals, seq):
    window = seq // 2
    got = []
    for other in range(2):
        pairs = []
        for core in range(CORES):
            for at in range(SEQ):
                holder = (at // 2) ^ other
                pairs.append((device_of(core, at), device_of(holder, 2 * (at % 2) + core)))
        got.append(send(jnp.where((window ^ other) == 0, totals[0], totals[1]), pairs))
    return got[0].astype(jnp.float32) + got[1].astype(jnp.float32)


def after(values, *tokens):
    return lax.optimization_barrier((values, tokens))[0]


def per_device(queries, keys, values, gain_q, gain_k, tile_pairs, tile_lens, out_grad, w_out):
    core = lax.axis_index("core")
    seq = lax.axis_index("seq")
    count_z = lax.axis_size("z")
    count_x = lax.axis_size("x")
    rows, features = out_grad.shape
    shard = 2 * (seq % 2) + core
    tiles_per_block = tile_pairs.shape[0] // SEQ
    place = jnp.stack([seq, core, shard, shard * tiles_per_block, lax.axis_index("x")]).astype(jnp.int32)
    lens = jnp.where(seq // 2 == core, tile_lens, swap_cores(tile_lens))

    def half_rows(rows_in, round_):
        half = seq % 2 if round_ % 2 == 0 else 1 - seq % 2
        return take(rows_in.reshape(2, rows // 2, features), half)

    parts = to_rounds(place, queries, keys, values, gain_q, gain_k)
    w_rows = to_shard_holders(w_out, seq, parts[0])
    w_all = lax.all_gather(w_rows, ("z", "x"), axis=0, tiled=True)
    packs = {r: send(parts[r], outward(r)) for r in ORDER}
    came = [packs[r] for r in ORDER]
    own = {}
    for r in ORDER:
        own[r] = send(half_rows(after(out_grad, came), r), outward(r))
    packs = [packs[r] for r in range(SEQ)]

    def project(part):
        return jnp.dot(part, w_all, preferred_element_type=jnp.float32).astype(jnp.bfloat16)

    attended, probs = forward(place, tile_pairs, lens, packs)
    one, two, three, last = ORDER
    other = {one: swap_cores(own[one]), two: swap_cores(after(own[two], attended))}
    own_grads = {one: project(own[one]), two: project(own[two])}
    other_grads = {one: project(other[one]), two: project(other[two])}
    other[three] = swap_cores(after(own[three], list(own_grads.values()), list(other_grads.values())))
    own_grads[three], other_grads[three] = project(own[three]), project(other[three])
    done = ([own_grads[r] for r in ORDER[:-1]], [other_grads[r] for r in ORDER[:-2]])
    other[last] = swap_cores(after(own[last], *done))
    own_grads[last] = project(own[last])
    other_grads[last] = project(other[last])
    attended = after(attended, own_grads, other_grads)
    own, other, own_grads, other_grads = [
        [table[r] for r in range(SEQ)] for table in (own, other, own_grads, other_grads)
    ]
    *one, two = weight_grad(place, attended, own, other, 1.0 / (count_z * count_x * CORES), count_x)
    two = lax.psum_scatter(two, "z", scatter_dimension=0, tiled=True)
    token = one[0]
    one = [one[0]] + [shift(one[by], "x", by) for by in (2, 1, 3)]
    parts = backward(place, tile_pairs, packs, own_grads, other_grads, after(probs, token))
    one = add(*after(one, parts[0]))
    parts = {r: send(parts[r] if r in ORDER[:3] else after(parts[r], one), inward(r)) for r in ORDER}
    two = lax.optimization_barrier(pair_sum(after(two, one), "x"))
    one = lax.optimization_barrier(pair_sum(one, "z"))
    grad_w = to_owners((one, two), seq)
    grad_q, grad_k, grad_v = finish(
        place, queries, keys, gain_q, gain_k, [parts[r] for r in range(SEQ)]
    )
    return (grad_q, grad_k, grad_v, grad_w)


def solution(mesh):
    dp = mesh.shape["dp"]
    side = math.isqrt(dp // CORES)
    parts = Mesh(mesh.devices.reshape(side, side, CORES, SEQ), ("z", "x", "core", "seq"))
    dp_axes = ("z", "x", "core")
    tokens = P(dp_axes + ("seq",), None)
    return jax.shard_map(
        per_device,
        mesh=parts,
        in_specs=(tokens, tokens, tokens, P(), P(), P(), P(dp_axes, None), tokens, P(dp_axes, "seq")),
        out_specs=(tokens, tokens, tokens, P(dp_axes, "seq")),
        check_vma=False,
    )
```
